32 devices in a mesh: dp: 4 (over y, x), fsdp: 8 (over z, core).
Axes of the slice: x: 2, y: 2, z: 4, core: 2. Of those that a mesh axis runs over, the one named last changes fastest.
Arguments:
- tokens: bfloat16 [12544, 768], P(('dp', 'fsdp')), may hold values from -6 to 6
- cotangent: bfloat16 [12544, 768], P(('dp', 'fsdp')), may hold values from -6 to 6
- keep_index: int32 [256, 49], P(('dp', 'fsdp')), may hold values from 0 to 195
- clip_ids: int32 [32, 8], P(('dp', 'fsdp')), may hold values from 0 to 1, never falling along the last dimension, each value on 1 to 7 neighbouring positions
- flat_params: float32 [7087104], P('fsdp'), as said below
- first_moment: float32 [7087104], P('fsdp'), may hold values from -0.0022538076 to 0.0022538076
- second_moment: float32 [7087104], P('fsdp'), may hold values from 1.1758447e-11 to 1.1288108e-09
Outputs:
- layer_out: bfloat16 [12544, 768], P(('dp', 'fsdp'))
- grad_tokens: float32 [12544, 768], P(('dp', 'fsdp'))
- grad_params: float32 [7087104], P('fsdp')
- param_change: float32 [7087104], P('fsdp')
- new_first: float32 [7087104], P('fsdp')
- new_second: float32 [7087104], P('fsdp')
The draws below stay inside these ranges and needn't reach their ends.
Inputs may be any that keep to these rules, and one draw needn't show every extreme that they name: `clip_ids`: clip numbers never fall along a device's images; each clip has 1 to 7 images. `flat_params`: the layer's parameters in the layout of the steps.
All inputs are finite; a program needn't handle non-finite values.
Results may differ from the reference program's by a relative error of at most 0.015.
Values may be sent and summed in bfloat16 or wider, within the bound.
A program may use at most 256 MiB of HBM per device.

```python
import math
import jax
import jax.numpy as jnp
import numpy as np
from jax import lax

D = 768
FF = 3072
HEADS = 12
HEAD_DIM = 64
PATCHES = 196
GRID = 14
KEEP = 49
IMG_DEV = 8
IMAGES = 256
TOKENS = 12544
CLIPS = 2
CLIP_MOST = 7
PARAMS = 7087104
DEVICES = 32


def draw_flat_params(key, part):
    noise = jax.random.normal(key, (PARAMS,), jnp.float32)
    position = jnp.arange(PARAMS)
    mats = 4 * D * D + 2 * D * FF
    inv_model = 1.0 / D ** 0.5
    inv_hidden = 1.0 / FF ** 0.5
    scale_vec = jnp.where(position < 3 * D * D, inv_model, jnp.where(position < 4 * D * D, 6.0 * inv_model, jnp.where(position < 4 * D * D + D * FF, inv_model, jnp.where(position < mats, inv_hidden, 0.1))))
    is_gain = (position >= mats) & (position < mats + D) | (position >= mats + 5 * D) & (position < mats + 6 * D)
    return jnp.where(is_gain, 1.0, 0.0) + noise * scale_vec


def touch_ends(array, key, low, high):
    shape = array.shape
    place = [jax.random.randint(jax.random.fold_in(key, axis), (), 0, shape[axis]) for axis in range(len(shape))]
    array = array.at[tuple(place)].set(low)
    longest = shape.index(max(shape))
    place[longest] = (place[longest] + 1) % shape[longest]
    return array.at[tuple(place)].set(high)


def level_of(stream_key, shape, split, smallest, top_value):
    gain, own = 1.0, jax.random.fold_in(stream_key, 6)
    for dim, shards_of in split:
        steps = jnp.exp(jax.random.uniform(jax.random.fold_in(own, dim), (shards_of,), jnp.float32, smallest / len(split), top_value / len(split)))
        gain = gain * jnp.repeat(steps, shape[dim] // shards_of).reshape([-1 if axis == dim else 1 for axis in range(len(shape))])
    return gain


def profile(amount, total, reach, slope):
    weights = [(1 << 20) // math.isqrt(standing ** slope) + 1 for standing in range(2, amount + 1)]
    rest, holding = total - reach - (amount - 1), [1] * (amount - 1)
    while rest > 0:
        movable = [i for i in range(amount - 1) if holding[i] < reach]
        mass, budget = sum([weights[i] for i in movable]), rest
        for i in movable:
            addition = min(reach - holding[i], max(1, budget * weights[i] // mass), rest)
            holding[i] = holding[i] + addition
            rest = rest - addition
    return np.array([reach] + holding)


def uneven(own_key, number_of, total, bound, skew):
    if number_of == 2:
        one = jax.random.randint(own_key, (), max(1, total - bound), min(bound, total - 1) + 1)
        return jnp.stack([one, total - one])
    sizes = jnp.asarray(profile(number_of, total, bound, skew), jnp.int32)
    twos = (number_of - 1) // 2
    source_of, sink = sizes[1:1 + 2 * twos:2], sizes[2:2 + 2 * twos:2]
    margin = jnp.minimum(source_of - 1, bound - sink)
    moved = jax.random.randint(jax.random.fold_in(own_key, 1), (twos,), 0, 1 << 20) % (margin + 1)
    sizes = sizes.at[1:1 + 2 * twos:2].set(source_of - moved).at[2:2 + 2 * twos:2].set(sink + moved)
    return sizes[jax.random.permutation(jax.random.fold_in(own_key, 2), number_of)]


def scatter_about(stream_key, dims, width, reach, cuts=(), held_as=jnp.bfloat16):
    drawn = jax.random.normal(stream_key, dims, jnp.float32) * width
    if len(cuts) > 0:
        drawn = level_of(stream_key, dims, cuts, -0.22, 0.18) * drawn
    return jnp.clip(drawn, min=-reach, max=reach).astype(held_as)


def setup_inputs(seed: int = 0) -> dict:
    key_of = jax.random.split(jax.random.key(seed), 8)
    tokens = scatter_about(key_of[0], (TOKENS, D), 1.0, 6.0, ((0, 32),))
    cotangent = scatter_about(key_of[1], (TOKENS, D), 1.0, 6.0, ((0, 32),))
    keep_index = touch_ends(jax.random.randint(key_of[2], (IMAGES, KEEP), 0, PATCHES), jax.random.fold_in(key_of[2], 1), 0, PATCHES - 1).astype(jnp.int32)
    clip_ids = jax.vmap(lambda own: jnp.searchsorted(jnp.cumsum(uneven(own, CLIPS, IMG_DEV, CLIP_MOST, 2)), jnp.arange(IMG_DEV), side="right"))(jax.random.split(key_of[3], DEVICES)).reshape((DEVICES, IMG_DEV)).astype(jnp.int32)
    flat_params = draw_flat_params(jax.random.fold_in(key_of[7], 71), 0)
    first_moment = scatter_about(key_of[5], (PARAMS,), (1.0 / (PARAMS ** 0.5)), 0.0022538076, ((0, 8),), jnp.float32)
    second_moment = jnp.clip(jnp.exp(math.log(1.1288108225926408e-09) - 4.564348 * jax.random.uniform(key_of[6], (PARAMS,), jnp.float32) ** level_of(key_of[6], (PARAMS,), ((0, 8),), -0.2, 0.2)), 1.17584466469145e-11, 1.1288108225926408e-09)
    return dict(tokens=tokens, cotangent=cotangent, keep_index=keep_index, clip_ids=clip_ids, flat_params=flat_params, first_moment=first_moment, second_moment=second_moment)


first_correct = 0.9999734386011124
second_correct = 0.09520785288629106

@jax.custom_vjp
def low(v):
    return lax.optimization_barrier(v.astype(jnp.bfloat16)).astype(jnp.float32)

@jax.custom_vjp
def low_back(v):
    return v

def low_keep(v):
    return (low(v), None)

def low_pass(kept, grad):
    return (grad,)

def back_keep(v):
    return (v, None)

def back_low(kept, grad):
    return (low(grad),)
low.defvjp(low_keep, low_pass)
low_back.defvjp(back_keep, back_low)

def both_ways(values):
    return low(low_back(values))

def precise(left, right):
    return jnp.dot(left, right, precision=lax.Precision.HIGHEST)

def layer_norm(values, gain_vec, shift_vec):
    row_mean = lax.optimization_barrier(jnp.mean(values, axis=-1, keepdims=True))
    centered = values - row_mean
    variance = lax.optimization_barrier(jnp.mean(centered * centered, axis=-1, keepdims=True))
    return centered * lax.rsqrt(variance + 1e-06) * gain_vec + shift_vec

def positions(keep_flat):
    quarter = D // 4
    frequency = 1.0 / 10000.0 ** (jnp.arange(quarter).astype(jnp.float32) / quarter)
    row_angle = (keep_flat // GRID).astype(jnp.float32)[:, None] * frequency
    col_angle = (keep_flat % GRID).astype(jnp.float32)[:, None] * frequency
    return jnp.concatenate([jnp.sin(row_angle), jnp.cos(row_angle), jnp.sin(col_angle), jnp.cos(col_angle)], axis=1)

def unpack_flat(flat):
    mats = 4 * D * D + 2 * D * FF
    w_qkv = flat[:3 * D * D].reshape(D, 3 * D)
    w_out = flat[3 * D * D:4 * D * D].reshape(D, D)
    w_up = flat[4 * D * D:4 * D * D + D * FF].reshape(D, FF)
    w_down = flat[4 * D * D + D * FF:mats].reshape(FF, D)
    vectors = flat[mats:mats + 8 * D].reshape(8, D)
    bias_up = flat[mats + 8 * D:]
    return (w_qkv, w_out, w_up, w_down, vectors, bias_up)

def group_forward(weights, group_tokens, group_keep, group_clip):
    w_qkv, w_out, w_up, w_down, vectors, bias_up = weights
    tok_count = group_tokens.shape[0]
    embedded = group_tokens + positions(group_keep)
    normed = low(layer_norm(embedded, vectors[0], vectors[1]))
    mixed_qkv = precise(normed, w_qkv)
    query_part = both_ways(mixed_qkv[:, :D] + vectors[2])
    key_part = both_ways(mixed_qkv[:, D:2 * D])
    value_part = both_ways(mixed_qkv[:, 2 * D:] + vectors[3])
    query_heads = query_part.reshape(tok_count, HEADS, HEAD_DIM)
    key_heads = key_part.reshape(tok_count, HEADS, HEAD_DIM)
    value_heads = value_part.reshape(tok_count, HEADS, HEAD_DIM)
    raw_scores = jnp.einsum('qhd,khd->hqk', query_heads, key_heads, precision=lax.Precision.HIGHEST)
    scores = low_back(raw_scores) * HEAD_DIM ** (-0.5)
    clip_tok = jnp.repeat(group_clip, KEEP)
    same_clip = clip_tok[:, None] == clip_tok[None, :]
    scores = jnp.where(same_clip[None], scores, -1e+30)
    row_top = lax.optimization_barrier(jnp.max(scores, axis=-1, keepdims=True))
    weight_exp = jnp.exp(scores - row_top)
    soft = low(weight_exp / lax.optimization_barrier(jnp.sum(weight_exp, axis=-1, keepdims=True)))
    attended = jnp.einsum('hqk,khd->qhd', soft, value_heads, precision=lax.Precision.HIGHEST)
    attended = both_ways(attended.reshape(tok_count, D))
    branch_one = low_back(precise(attended, w_out) + vectors[4])
    resid = embedded + branch_one
    normed_two = low(layer_norm(resid, vectors[5], vectors[6]))
    pre_act = low_back(precise(normed_two, w_up) + bias_up)
    activated = low(jax.nn.gelu(pre_act, approximate=False))
    branch_two = low_back(precise(activated, w_down) + vectors[7])
    return resid + branch_two

def reference(tokens, cotangent, keep_index, clip_ids, flat_params, first_moment, second_moment):
    all_tokens = tokens.astype(jnp.float32)
    groups = clip_ids.shape[0]

    def forward(token_values, params):
        weights = unpack_flat(low(params))

        def one_group(group_item):
            return group_forward(weights, group_item[0], group_item[1], group_item[2])
        outputs = lax.map(jax.checkpoint(one_group), (token_values.reshape(groups, -1, D), keep_index.reshape(groups, -1), clip_ids))
        return outputs.reshape(-1, D)
    result, pullback = jax.vjp(forward, all_tokens, flat_params)
    grad_tokens, grad_params = pullback(cotangent.astype(jnp.float32))
    grad_norm = jnp.sqrt(jnp.sum(grad_params * grad_params))
    clip_factor = jnp.minimum(1.0, 1.0 / (grad_norm + 1e-06))
    clipped = grad_params * clip_factor
    new_first = 0.9 * first_moment + 0.1 * clipped
    new_second = 0.999 * second_moment + 0.001 * clipped * clipped
    first_hat = new_first / first_correct
    second_hat = new_second / second_correct
    mats = 4 * D * D + 2 * D * FF
    decay_mask = (jnp.arange(PARAMS) < mats).astype(jnp.float32)
    step_rate = 0.001 * 0.75 ** 6
    param_change = step_rate * (first_hat / (jnp.sqrt(second_hat) + 1e-08) + 0.05 * decay_mask * flat_params)
    return (result.astype(jnp.bfloat16), grad_tokens, grad_params, param_change, new_first, new_second)
```

```python
import functools

import jax
import jax.numpy as jnp
import numpy as np
from jax import lax
from jax.experimental import pallas as pl
from jax.experimental.pallas import tpu as pltpu
from jax.sharding import PartitionSpec as P

D = 768
FF = 3072
HEADS = 12
HEAD_DIM = 64
GRID = 14
KEEP = 49
MATS = 4 * D * D + 2 * D * FF

first_correct = 0.9999734386011124
second_correct = 0.09520785288629106

F32 = jnp.float32
BF16 = jnp.bfloat16
MESH = pl.DeviceIdType.MESH
LIMIT = 66_000_000

ROWS = 400
CHUNK = 80
PIECE = 96
PIECES = 12
LANES = 128
TAIL = 72


def ge(s, k):
    return (s + 8 - k) // 8


def piece_of(s, i):
    g5 = (i + 4) // 8
    forms = (
        8 * (i // 4) + i % 4,
        8 * (i // 4) + 4 + i % 4,
        24 + i + (i // 8) * (7 * i - 56),
        33 + 8 * (i // 3) + i % 3,
        36 + 8 * (i // 3) + i % 3,
        (1 - g5) * (39 + 8 * i) + g5 * (60 + i),
        72 + i,
        84 + i,
    )
    out = 0
    for k, form in enumerate(forms):
        out = out + (ge(s, k) - ge(s, k + 1)) * form
    return out


def dot(a, b):
    return lax.dot_general(a, b, (((1,), (0,)), ((), ())), preferred_element_type=F32)


def dot_nt(a, b):
    return lax.dot_general(a, b, (((1,), (1,)), ((), ())), preferred_element_type=F32)


def dot_tn(a, b):
    return lax.dot_general(a, b, (((0,), (0,)), ((), ())), preferred_element_type=F32)


def loop(start, stop, body):
    def step(i, carry):
        body(i)
        return carry

    lax.fori_loop(start, stop, step, 0)


def chunks(body):
    loop(0, ROWS // CHUNK, lambda n: body(pl.ds(pl.multiple_of(n * CHUNK, CHUNK), CHUNK)))


class Place:
    def __init__(self):
        self.dp = lax.axis_index("dp")
        self.s = lax.axis_index("fsdp")
        self.x, self.y = self.dp % 2, self.dp // 2
        self.z, self.c = self.s // 2, self.s % 2
        self.sib = self.at(self.dp, self.s + 1 - 2 * self.c)
        self.xn = self.at(self.dp + 1 - 2 * self.x, self.s)
        self.yn = self.at(self.dp + 2 - 4 * self.y, self.s)
        self.up = self.at(self.dp, self.s + 2)
        self.down = self.at(self.dp, self.s - 2)

    def at(self, dp, s):
        return (dp, s)

    def barrier(self):
        sem = pltpu.get_barrier_semaphore()
        for n in range(1, 8):
            pl.semaphore_signal(sem, inc=1, device_id=self.at(self.dp, (self.s + n) % 8), device_id_type=MESH)
        for peer in (self.xn, self.yn):
            pl.semaphore_signal(sem, inc=1, device_id=peer, device_id_type=MESH)
        pl.semaphore_wait(sem, 9)


def remote(src, dst, send, recv, to):
    return pltpu.make_async_remote_copy(
        src_ref=src, dst_ref=dst, send_sem=send, recv_sem=recv, device_id=to, device_id_type=MESH
    )


def weave(s, body):
    @pl.when(s <= 1)
    def _():
        loop(0, 12, lambda i: body(i, 18, (i % 4) * (96 * 18) + (i // 4) * 6))

    @pl.when(s == 2)
    def _():
        loop(0, 8, lambda i: body(i, 6, i * (96 * 6)))
        loop(8, 12, lambda i: body(i, 24, 4608 + (i - 8) * 6))

    @pl.when((s == 3) | (s == 4))
    def _():
        loop(0, 12, lambda i: body(i, 24, (i % 3) * (96 * 24) + (i // 3) * 6))

    @pl.when(s == 5)
    def _():
        loop(0, 4, lambda i: body(i, 24, i * 6))
        loop(4, 12, lambda i: body(i, 6, 2304 + (i - 4) * (96 * 6)))

    @pl.when(s >= 6)
    def _():
        loop(0, 12, lambda i: body(i, 6, i * (96 * 6)))


def gather_kernel(own_ref, g_ref, v_ref, buf, tail, vbuf, edge_sem, v_send, v_recv, z_send, z_recv, p_send, p_recv, c_send, c_recv):
    me = Place()
    s, z, c = me.s, me.z, me.c
    q = me.dp
    rows = own_ref.shape[0]
    tail[...] = own_ref[rows - TAIL : rows, :]
    me.barrier()

    edge = remote(tail, buf.at[pl.ds(0, TAIL)], edge_sem.at[0], edge_sem.at[1], me.at(me.dp, (s + 1) % 8))

    @pl.when(s < 7)
    def _():
        edge.start()

    @pl.when(s == 7)
    def _():
        for n in range(7):
            remote(tail, vbuf, v_send.at[n], v_recv, me.at(me.dp, n)).start()
        vbuf[...] = tail[...]

    full = rows // 8
    loop(0, full // 5, lambda n: buf.__setitem__((pl.ds(pl.multiple_of(TAIL + n * 40, 8), 40), slice(None)), own_ref[pl.ds(pl.multiple_of(n * 40, 8), 40), :]))
    buf[TAIL + full * 8 : TAIL + rows, :] = own_ref[full * 8 : rows, :]

    @pl.when(s > 0)
    def _():
        edge.wait_recv()

    def to_sib(p, i):
        piece = piece_of(2 * p + c, i)
        remote(g_ref.at[piece], g_ref.at[piece], c_send.at[p, i], c_recv.at[p, i], me.sib).start()

    def z_copy(p, k, way, to):
        piece = piece_of(2 * p + c, 3 * q + k)
        return remote(g_ref.at[piece], g_ref.at[piece], z_send.at[way, p, k], z_recv.at[p, k], to)

    def plane_copy(kind, p, quarter, k, to):
        piece = piece_of(2 * p + c, 3 * quarter + k)
        ref = g_ref.at[piece]
        if kind >= 2:
            ref = g_ref.at[piece, pl.ds(48 * (kind - 2), 48)]
        return remote(ref, ref, p_send.at[kind, p, k], p_recv.at[kind, p, k], to)

    def place_piece(i, stride, first):
        piece = piece_of(s, i)
        for j in range(6):
            g_ref[piece, :, LANES * j : LANES * (j + 1)] = buf[pl.ds(TAIL - 9 * s + first + j, PIECE, stride=stride), :].astype(BF16)

    weave(s, place_piece)

    def own_sends(k):
        @pl.when(z < 3)
        def _():
            z_copy(z, k, 0, me.up).start()

        @pl.when(z > 0)
        def _():
            z_copy(z, k, 1, me.down).start()

    loop(0, 3, own_sends)
    loop(0, 12, lambda i: to_sib(z, i))

    qx = me.dp + 1 - 2 * me.x
    qy = me.dp + 2 - 4 * me.y
    qd = 3 - me.dp

    def both(d, body):
        @pl.when(z >= d)
        def _():
            loop(0, 3, lambda k: body(z - d, k, 0))

        @pl.when(z + d <= 3)
        def _():
            loop(0, 3, lambda k: body(z + d, k, 1))

    def z_arrive(p, k, way):
        z_copy(p, k, way, me.up).wait_recv()
        if way == 0:

            @pl.when(z < 3)
            def _():
                z_copy(p, k, 0, me.up).start()
        else:

            @pl.when(z > 0)
            def _():
                z_copy(p, k, 1, me.down).start()

        plane_copy(0, p, q, k, me.xn).start()
        plane_copy(1, p, q, k, me.yn).start()
        to_sib(p, 3 * q + k)

    def xy_arrive(p, k, way):
        plane_copy(0, p, qx, k, me.xn).wait_recv()
        plane_copy(3, p, qx, k, me.yn).start()
        to_sib(p, 3 * qx + k)
        plane_copy(1, p, qy, k, me.yn).wait_recv()
        plane_copy(2, p, qy, k, me.xn).start()
        to_sib(p, 3 * qy + k)

    def d_arrive(p, k, way):
        plane_copy(2, p, qd, k, me.xn).wait_recv()
        plane_copy(3, p, qd, k, me.yn).wait_recv()
        to_sib(p, 3 * qd + k)

    both(1, z_arrive)
    both(2, z_arrive)
    both(1, xy_arrive)
    both(3, z_arrive)
    both(2, xy_arrive)
    both(1, d_arrive)
    both(3, xy_arrive)
    both(2, d_arrive)
    both(3, d_arrive)

    @pl.when(s < 7)
    def _():
        remote(tail, vbuf, v_send.at[0], v_recv, me.sib).wait_recv()
        edge.wait_send()

    @pl.when(s == 7)
    def _():
        for n in range(7):
            remote(tail, vbuf, v_send.at[n], v_recv, me.sib).wait_send()

    for j in range(6):
        v_ref[0:12, LANES * j : LANES * (j + 1)] = vbuf[pl.ds(j, 12, stride=6), :].astype(BF16).astype(F32)

    def own_done(k):
        @pl.when(z < 3)
        def _():
            z_copy(z, k, 0, me.up).wait_send()

        @pl.when(z > 0)
        def _():
            z_copy(z, k, 1, me.down).wait_send()

    loop(0, 3, own_done)

    def far_done(p, k, way):
        if way == 0:

            @pl.when(z < 3)
            def _():
                z_copy(p, k, 0, me.up).wait_send()
        else:

            @pl.when(z > 0)
            def _():
                z_copy(p, k, 1, me.down).wait_send()

        plane_copy(0, p, q, k, me.xn).wait_send()
        plane_copy(1, p, q, k, me.yn).wait_send()
        plane_copy(2, p, qy, k, me.xn).wait_send()
        plane_copy(3, p, qx, k, me.yn).wait_send()

    for d in (1, 2, 3):
        both(d, far_done)

    def sib_done(n):
        p, i = n // 12, n % 12
        piece = piece_of(2 * p + c, i)
        copy = remote(g_ref.at[piece], g_ref.at[piece], c_send.at[p, i], c_recv.at[p, i], me.sib)
        copy.wait_send()
        copy.wait_recv()

    loop(0, 48, sib_done)


def gather(own):
    dma = pltpu.SemaphoreType.DMA
    return pl.pallas_call(
        gather_kernel,
        name="gather",
        out_shape=(jax.ShapeDtypeStruct((96, PIECE, D), BF16), jax.ShapeDtypeStruct((16, D), F32)),
        in_specs=[pl.BlockSpec(memory_space=pltpu.VMEM)],
        out_specs=(pl.BlockSpec(memory_space=pltpu.VMEM), pl.BlockSpec(memory_space=pltpu.VMEM)),
        scratch_shapes=[
            pltpu.VMEM((7000, LANES), F32),
            pltpu.VMEM((TAIL, LANES), F32),
            pltpu.VMEM((TAIL, LANES), F32),
            dma((2,)),
            dma((7,)),
            dma,
            dma((2, 4, 3)),
            dma((4, 3)),
            dma((4, 4, 3)),
            dma((4, 4, 3)),
            dma((4, 12)),
            dma((4, 12)),
        ],
        compiler_params=pltpu.CompilerParams(collective_id=0, has_side_effects=True, vmem_limit_bytes=LIMIT),
    )(own)


def position_table():
    quarter = D // 4
    exponent = np.arange(quarter, dtype=np.float32) / np.float32(quarter)
    frequency = np.float32(1.0) / np.power(np.float32(10000.0), exponent).astype(np.float32)
    angle = (np.arange(GRID, dtype=np.float32)[:, None] * frequency).astype(np.float64)
    waves = np.concatenate([np.sin(angle), np.cos(angle)], axis=1).astype(np.float32)
    table = np.zeros((32, D), np.float32)
    table[:GRID, : D // 2] = waves
    table[16 : 16 + GRID, D // 2 :] = waves
    parts = []
    for _ in range(3):
        part = table.astype(jnp.bfloat16)
        parts.append(part)
        table = table - part.astype(np.float32)
    return np.stack(parts)


def norm_stats(v):
    mean = jnp.mean(v, axis=-1, keepdims=True)
    centered = v - mean
    rstd = lax.rsqrt(jnp.mean(centered * centered, axis=-1, keepdims=True) + 1e-06)
    return centered * rstd, rstd


def block(g_ref, b):
    return g_ref[pl.ds(8 * b, 8)].reshape(D, D)


def slabs(ref, first):
    return jnp.concatenate([ref[first + j] for j in range(6)], axis=1)


def embed(tok_ref, keep_ref, table_ref, v_ref, emb, n1):
    real = tok_ref.shape[0]
    emb[0:real, :] = tok_ref[...].astype(F32)
    emb[real:, :] = jnp.zeros((ROWS - real, D), F32)
    gain, shift = v_ref[0:1, :], v_ref[1:2, :]

    def body(at):
        keep = keep_ref[at, :]
        row = (keep * 4682) >> 16
        col = keep - GRID * row + 16
        lane = lax.broadcasted_iota(jnp.int32, (CHUNK, 32), 1)
        hot = jnp.where((lane == row) | (lane == col), 1.0, 0.0).astype(BF16)
        spot = dot(hot, table_ref[0]) + (dot(hot, table_ref[1]) + dot(hot, table_ref[2]))
        value = emb[at, :] + spot
        emb[at, :] = value
        n1[at, :] = (norm_stats(value)[0] * gain + shift).astype(BF16)

    chunks(body)


def project(n1, g_ref, v_ref, qkv):
    for b in range(3):
        mixed = dot(n1[...], block(g_ref, b))
        if b != 1:
            mixed = mixed + v_ref[2 + b // 2 : 3 + b // 2, :]
        for j in range(6):
            qkv[6 * b + j] = mixed[:, LANES * j : LANES * (j + 1)].astype(BF16)


def attend(j, same_of, qkv, att, lse):
    query, key, value = qkv[j], qkv[6 + j], qkv[12 + j]
    first = lax.broadcasted_iota(jnp.int32, (ROWS, LANES), 1) < HEAD_DIM
    turned = value.T
    parts = []
    for h in range(2):
        own = jnp.where(first if h == 0 else ~first, query, jnp.zeros_like(query))
        scores = jnp.where(same_of(), dot_nt(key, own) * 0.125, -1e30)
        top = jnp.max(scores, axis=0, keepdims=True)
        weight = jnp.exp(scores - top)
        total = jnp.sum(weight, axis=0, keepdims=True)
        soft = (weight * (1.0 / total)).astype(BF16)
        lse[2 * j + h] = top + jnp.log(total)
        parts.append(dot(turned[HEAD_DIM * h : HEAD_DIM * (h + 1), :], soft))
    att[j] = jnp.concatenate(parts, axis=0).T.astype(BF16)


def out_project(att, g_ref, v_ref, emb, resid, n2):
    resid[...] = dot(slabs(att, 0), block(g_ref, 3))
    bias, gain, shift = v_ref[4:5, :], v_ref[5:6, :], v_ref[6:7, :]

    def body(at):
        value = emb[at, :] + resid[at, :] + bias
        resid[at, :] = value
        n2[at, :] = (norm_stats(value)[0] * gain + shift).astype(BF16)

    chunks(body)


def expand(j, n2, g_ref, v_ref, work, act, slope):
    work[...] = dot(n2[...], block(g_ref, 4 + j))

    def body(at):
        pre = work[at, :] + v_ref[pl.ds(8 + j, 1), :]
        phi = 0.5 * (1.0 + lax.erf(pre * 0.7071067811865476))
        act[j, at, :] = (pre * phi).astype(BF16)
        slope[j, at, :] = phi + pre * (0.3989422804014327 * jnp.exp(-0.5 * pre * pre))

    chunks(body)


def contract(j, act, g_ref, work):
    part = dot(act[j], block(g_ref, 8 + j))

    @pl.when(j == 0)
    def _():
        work[...] = part

    @pl.when(j > 0)
    def _():
        work[...] += part


def forward_kernel(tok_ref, keep_ref, clip_col, clip_row, table_ref, g_ref, v_ref, out_ref, emb, n1, qkv, att, lse, resid, n2, act, slope, work):
    same_of = lambda: clip_col[...] == clip_row[...]
    embed(tok_ref, keep_ref, table_ref, v_ref, emb, n1)
    project(n1, g_ref, v_ref, qkv)
    loop(0, 6, lambda j: attend(j, same_of, qkv, att, lse))
    out_project(att, g_ref, v_ref, emb, resid, n2)
    loop(0, 4, lambda j: expand(j, n2, g_ref, v_ref, work, act, slope))
    loop(0, 4, lambda j: contract(j, act, g_ref, work))
    real = out_ref.shape[0]
    out_ref[...] = (resid[0:real, :] + work[0:real, :] + v_ref[7:8, :]).astype(BF16)


def kept_shapes():
    return [
        ((ROWS, D), F32),
        ((ROWS, D), BF16),
        ((18, ROWS, LANES), BF16),
        ((6, ROWS, LANES), BF16),
        ((HEADS, 1, ROWS), F32),
        ((ROWS, D), F32),
        ((ROWS, D), BF16),
        ((4, ROWS, D), BF16),
        ((4, ROWS, D), F32),
    ]


VM = pl.BlockSpec(memory_space=pltpu.VMEM)


def forward(tokens, keep, clip_col, clip_row, weights, vectors):
    table = jnp.asarray(position_table())
    return pl.pallas_call(
        forward_kernel,
        name="forward",
        out_shape=[jax.ShapeDtypeStruct(tokens.shape, BF16)] + [jax.ShapeDtypeStruct(*k) for k in kept_shapes()],
        in_specs=[VM] * 7,
        out_specs=[VM] * 10,
        scratch_shapes=[pltpu.VMEM((ROWS, D), F32)],
        compiler_params=pltpu.CompilerParams(vmem_limit_bytes=LIMIT),
    )(tokens, keep, clip_col, clip_row, table, weights, vectors)


def col_sums(dest, row, source):
    dest[row : row + 1, :] = jnp.sum(source, axis=0, keepdims=True)


def put_block(gw, b, value):
    gw[pl.ds(8 * b, 8)] = value.astype(BF16).reshape(8, PIECE, D)


def down_grad(j, cot, act, gw):
    put_block(gw, 8 + j, dot_tn(act[j], cot[...]))


def act_grad(j, cot, n2, g_ref, slope, gw, gv, work, pre_low, gn):
    work[...] = dot_nt(cot[...], block(g_ref, 8 + j))
    total = jnp.zeros((8, D), F32)

    def body(n, total):
        at = pl.ds(pl.multiple_of(n * CHUNK, CHUNK), CHUNK)
        low = (slope[j, at, :] * work[at, :]).astype(BF16)
        pre_low[at, :] = low
        return total + jnp.sum(low.astype(F32).reshape(CHUNK // 8, 8, D), axis=0)

    total = lax.fori_loop(0, ROWS // CHUNK, body, total)
    gv[pl.ds(8 + j, 1), :] = jnp.sum(total, axis=0, keepdims=True)
    put_block(gw, 4 + j, dot_tn(n2[...], pre_low[...]))
    part = dot_nt(pre_low[...], block(g_ref, 4 + j))

    @pl.when(j == 0)
    def _():
        gn[...] = part

    @pl.when(j > 0)
    def _():
        gn[...] += part


def norm_back(value_ref, gn, gain, extra, store, gv, row):
    def body(n, sums):
        at = pl.ds(pl.multiple_of(n * CHUNK, CHUNK), CHUNK)
        hat, rstd = norm_stats(value_ref[at, :])
        grad = gn[at, :]
        fold = lambda v: jnp.sum(v.reshape(CHUNK // 8, 8, D), axis=0)
        sums = (sums[0] + fold(grad * hat), sums[1] + fold(grad))
        grad = grad * gain
        inner = jnp.mean(grad * hat, axis=-1, keepdims=True)
        store(at, extra(at) + rstd * (grad - jnp.mean(grad, axis=-1, keepdims=True) - hat * inner))
        return sums

    zero = jnp.zeros((8, D), F32)
    one, two = lax.fori_loop(0, ROWS // CHUNK, body, (zero, zero))
    gv[row : row + 1, :] = jnp.sum(one, axis=0, keepdims=True)
    gv[row + 1 : row + 2, :] = jnp.sum(two, axis=0, keepdims=True)


def attend_back(j, same_of, qkv, lse, ga, gm):
    query, key, value, grad = qkv[j], qkv[6 + j], qkv[12 + j], ga[j]
    first = lax.broadcasted_iota(jnp.int32, (ROWS, LANES), 1) < HEAD_DIM
    turned = key.T
    parts, grad_key, grad_value = [], None, None
    for h in range(2):
        mine = first if h == 0 else ~first
        own = jnp.where(mine, query, jnp.zeros_like(query))
        own_grad = jnp.where(mine, grad, jnp.zeros_like(grad))
        soft = jnp.where(same_of(), jnp.exp(dot_nt(key, own) * 0.125 - lse[2 * j + h]), 0.0)
        grad_soft = dot_nt(value, own_grad)
        inner = jnp.sum(soft * grad_soft, axis=0, keepdims=True)
        raw = (0.125 * soft * (grad_soft - inner)).astype(BF16)
        one = dot(soft.astype(BF16), own_grad)
        two = dot(raw, own)
        grad_value = one if h == 0 else grad_value + one
        grad_key = two if h == 0 else grad_key + two
        parts.append(dot(turned[HEAD_DIM * h : HEAD_DIM * (h + 1), :], raw))
    gm[j] = jnp.concatenate(parts, axis=0).T.astype(BF16)
    gm[6 + j] = grad_key.astype(BF16)
    gm[12 + j] = grad_value.astype(BF16)


def backward_kernel(cot_ref, clip_col, clip_row, g_ref, v_ref, emb, n1, qkv, att, lse, resid, n2, act, slope, gtok_ref, gw, gv, cot, work, low, gn, ga, gm):
    same_of = lambda: clip_col[...] == clip_row[...]
    real = cot_ref.shape[0]
    gv[...] = jnp.zeros_like(gv)
    cot[...] = jnp.concatenate([cot_ref[...].astype(F32), jnp.zeros((ROWS - real, D), F32)], axis=0).astype(BF16)
    col_sums(gv, 7, cot[...].astype(F32))
    loop(0, 4, lambda j: down_grad(j, cot, act, gw))
    loop(0, 4, lambda j: act_grad(j, cot, n2, g_ref, slope, gw, gv, work, low, gn))

    def keep_resid(at, value):
        work[at, :] = value
        low[at, :] = value.astype(BF16)

    norm_back(resid, gn, v_ref[5:6, :], lambda at: cot[at, :].astype(F32), keep_resid, gv, 5)
    col_sums(gv, 4, low[...].astype(F32))
    put_block(gw, 3, dot_tn(slabs(att, 0), low[...]))
    grad = dot_nt(low[...], block(g_ref, 3))
    for j in range(6):
        ga[j] = grad[:, LANES * j : LANES * (j + 1)].astype(BF16)
    loop(0, 6, lambda j: attend_back(j, same_of, qkv, lse, ga, gm))
    for b in range(3):
        mixed = slabs(gm, 6 * b)
        if b != 1:
            col_sums(gv, 2 + b // 2, mixed.astype(F32))
        put_block(gw, b, dot_tn(n1[...], mixed))
        part = dot_nt(mixed, block(g_ref, b))
        gn[...] = part if b == 0 else gn[...] + part

    def keep_tokens(at, value):
        work[at, :] = value

    norm_back(emb, gn, v_ref[0:1, :], lambda at: work[at, :], keep_tokens, gv, 0)
    gtok_ref[...] = work[0:real, :]


def backward(cotangent, clip_col, clip_row, weights, vectors, kept):
    return pl.pallas_call(
        backward_kernel,
        name="backward",
        out_shape=[
            jax.ShapeDtypeStruct(cotangent.shape, F32),
            jax.ShapeDtypeStruct((96, PIECE, D), BF16),
            jax.ShapeDtypeStruct((16, D), F32),
        ],
        in_specs=[VM] * 14,
        out_specs=[VM] * 3,
        scratch_shapes=[
            pltpu.VMEM((ROWS, D), BF16),
            pltpu.VMEM((ROWS, D), F32),
            pltpu.VMEM((ROWS, D), BF16),
            pltpu.VMEM((ROWS, D), F32),
            pltpu.VMEM((6, ROWS, LANES), BF16),
            pltpu.VMEM((18, ROWS, LANES), BF16),
        ],
        compiler_params=pltpu.CompilerParams(vmem_limit_bytes=LIMIT),
    )(cotangent, clip_col, clip_row, weights, vectors, *kept)


FLAT = 7240
HALF = PIECE // 2


def reduce_kernel(
    gw_in, gv_ref, flat_ref, norm_ref,
    gw, sib, xa, ya, yb, xb, zu, zd, shard, vsum, vpart, norms,
    load_sem, sib_send, sib_recv, h_send, h_recv, t_send, t_recv, z_send, z_recv, g_send, g_recv, v_send, v_recv, e_sem, n_send, n_recv,
):
    me = Place()
    s, z, c, x, y = me.s, me.z, me.c, me.x, me.y
    q = me.dp
    load = pltpu.make_async_copy(gw_in, gw, load_sem)
    load.start()
    flat_ref[6912:, :] = jnp.zeros((FLAT - 6912, LANES), F32)
    me.barrier()
    load.wait()

    def add_into(piece, rows, got):
        gw[piece, rows, :] = (gw[piece, rows, :].astype(F32) + got.astype(F32)).astype(BF16)

    low, high, whole = pl.ds(0, HALF), pl.ds(HALF, HALF), pl.ds(0, PIECE)

    def sib_copy(p, i):
        piece = piece_of(2 * p + 1 - c, i)
        return remote(gw.at[piece], sib.at[p, i], sib_send.at[p, i], sib_recv.at[p, i], me.sib)

    loop(0, 48, lambda n: sib_copy(3 - n // 12, n % 12).start())

    vsum[0] = gv_ref[...]
    partners = (me.sib, me.xn, me.yn, me.at(me.dp, (s + 2 - 4 * (z % 2)) % 8), me.at(me.dp, (s + 4) % 8))

    def v_step(n):
        copy = remote(vsum.at[n], vpart.at[n], v_send.at[n], v_recv.at[n], partners[n])
        return copy

    def xa_copy(p, yy, k):
        piece = piece_of(2 * p + c, 3 * (2 * yy + 1 - x) + k)
        return remote(gw.at[piece, low], xa.at[p, yy, k], h_send.at[0, p, yy, k], h_recv.at[0, p, yy, k], me.xn)

    def yb_copy(p, xx, k):
        piece = piece_of(2 * p + c, 3 * (2 * (1 - y) + xx) + k)
        return remote(gw.at[piece, high], yb.at[p, xx, k], h_send.at[1, p, xx, k], h_recv.at[1, p, xx, k], me.yn)

    def ya_copy(p, k):
        piece = piece_of(2 * p + c, 3 * (2 * (1 - y) + x) + k)
        return remote(gw.at[piece, low], ya.at[p, k], t_send.at[0, p, k], t_recv.at[0, p, k], me.yn)

    def xb_copy(p, k):
        piece = piece_of(2 * p + c, 3 * (2 * y + 1 - x) + k)
        return remote(gw.at[piece, high], xb.at[p, k], t_send.at[1, p, k], t_recv.at[1, p, k], me.xn)

    def from_sib(p):
        def body(i):
            sib_copy(p, i).wait_recv()
            piece = piece_of(2 * p + c, i)
            add_into(piece, whole, sib[p, i])

        loop(0, 12, body)

        def send(k):
            for n in range(2):
                xa_copy(p, n, k).start()
                yb_copy(p, n, k).start()

        loop(0, 3, send)

    def first_half(p):
        def body(k):
            xa_copy(p, 1 - y, k).wait_recv()
            add_into(piece_of(2 * p + c, 3 * (2 * (1 - y) + x) + k), low, xa[p, 1 - y, k])
            ya_copy(p, k).start()
            yb_copy(p, 1 - x, k).wait_recv()
            add_into(piece_of(2 * p + c, 3 * (2 * y + 1 - x) + k), high, yb[p, 1 - x, k])
            xb_copy(p, k).start()
            own = piece_of(2 * p + c, 3 * q + k)
            xa_copy(p, y, k).wait_recv()
            add_into(own, low, xa[p, y, k])
            yb_copy(p, x, k).wait_recv()
            add_into(own, high, yb[p, x, k])

        loop(0, 3, body)

    def z_copy(p, k, way):
        piece = piece_of(2 * p + c, 3 * q + k)
        return remote(gw.at[piece], (zu, zd)[way].at[p, k], z_send.at[way, p, k], z_recv.at[way, p, k], (me.up, me.down)[way])

    def second_half(p):
        def body(k):
            own = piece_of(2 * p + c, 3 * q + k)
            ya_copy(p, k).wait_recv()
            add_into(own, low, ya[p, k])
            xb_copy(p, k).wait_recv()
            add_into(own, high, xb[p, k])

            @pl.when((z == 0) & (p > 0))
            def _():
                z_copy(p, k, 0).start()

            @pl.when((z == 3) & (p < 3))
            def _():
                z_copy(p, k, 1).start()

        loop(0, 3, body)

    def along_z(p):
        def body(k):
            own = piece_of(2 * p + c, 3 * q + k)

            @pl.when((z > 0) & (z < p))
            def _():
                z_copy(p, k, 0).wait_recv()
                add_into(own, whole, zu[p, k])
                z_copy(p, k, 0).start()

            @pl.when((z < 3) & (z > p))
            def _():
                z_copy(p, k, 1).wait_recv()
                add_into(own, whole, zd[p, k])
                z_copy(p, k, 1).start()

        loop(0, 3, body)

    def share(kind, quarter, k):
        at = 3 * quarter + k
        ref = shard.at[at] if kind < 2 else shard.at[at, (low, high)[kind - 2]]
        to = (me.xn, me.yn, me.xn, me.yn)[kind]
        return remote(ref, ref, g_send.at[kind, k], g_recv.at[kind, k], to)

    def finish(k):
        own = piece_of(2 * z + c, 3 * q + k)

        @pl.when(z > 0)
        def _():
            z_copy(z, k, 0).wait_recv()
            add_into(own, whole, zu[z, k])

        @pl.when(z < 3)
        def _():
            z_copy(z, k, 1).wait_recv()
            add_into(own, whole, zd[z, k])

        shard[3 * q + k] = gw[own]
        share(0, q, k).start()
        share(1, q, k).start()

    def v_turn(n):
        copy = v_step(n)
        copy.wait_recv()
        vsum[n + 1] = vsum[n] + vpart[n]
        if n < 4:
            v_step(n + 1).start()

    v_step(0).start()
    from_sib(3)
    v_turn(0)
    from_sib(2)
    first_half(3)
    v_turn(1)
    from_sib(1)
    first_half(2)
    second_half(3)
    v_turn(2)
    from_sib(0)
    first_half(1)
    second_half(2)
    along_z(3)
    v_turn(3)
    first_half(0)
    second_half(1)
    along_z(2)
    v_turn(4)
    second_half(0)
    along_z(1)
    along_z(0)
    loop(0, 3, finish)

    qx, qy, qd = q + 1 - 2 * x, q + 2 - 4 * y, 3 - q

    def pass_on(k):
        share(0, qx, k).wait_recv()
        share(3, qx, k).start()
        share(1, qy, k).wait_recv()
        share(2, qy, k).start()

    loop(0, 3, pass_on)

    def last(k):
        share(2, qd, k).wait_recv()
        share(3, qd, k).wait_recv()

    loop(0, 3, last)

    norms[0] = jnp.zeros((8, LANES), F32)

    def lay(i, stride, first):
        total = norms[0]
        for j in range(6):
            part = shard[i, :, LANES * j : LANES * (j + 1)].astype(F32)
            flat_ref[pl.ds(first + j, PIECE, stride=stride), :] = part
            total = total + jnp.sum((part * part).reshape(PIECE // 8, 8, LANES), axis=0)
        norms[0] = total

    weave(s, lay)

    @pl.when(s == 7)
    def _():
        total = norms[0]
        for j in range(6):
            part = vsum[5, 0:12, LANES * j : LANES * (j + 1)]
            flat_ref[pl.ds(6912 + j, 12, stride=6), :] = part
            total = total + jnp.concatenate([part[0:8] * part[0:8], jnp.zeros((8, LANES), F32)], axis=0)[0:8]
            total = total + jnp.concatenate([part[8:12] * part[8:12], jnp.zeros((4, LANES), F32)], axis=0)
        norms[0] = total

    edge = remote(flat_ref.at[pl.ds(0, TAIL)], flat_ref.at[pl.ds(6912, TAIL)], e_sem.at[0], e_sem.at[1], me.at(me.dp, (s + 7) % 8))

    @pl.when(s > 0)
    def _():
        edge.start()

    def norm_copy(n):
        return remote(norms.at[0], norms.at[n], n_send.at[n], n_recv.at[n], me.at(me.dp, (s + n) % 8))

    for n in range(1, 8):
        norm_copy(n).start()

    def sent_sib(n):
        sib_copy(n // 12, n % 12).wait_send()

    loop(0, 48, sent_sib)

    def sent_plane(n):
        p, k = n // 3, n % 3
        for m in range(2):
            xa_copy(p, m, k).wait_send()
            yb_copy(p, m, k).wait_send()
        ya_copy(p, k).wait_send()
        xb_copy(p, k).wait_send()

        @pl.when(z < p)
        def _():
            z_copy(p, k, 0).wait_send()

        @pl.when(z > p)
        def _():
            z_copy(p, k, 1).wait_send()

    loop(0, 12, sent_plane)

    def sent_share(k):
        share(0, q, k).wait_send()
        share(1, q, k).wait_send()
        share(2, qy, k).wait_send()
        share(3, qx, k).wait_send()

    loop(0, 3, sent_share)
    for n in range(5):
        v_step(n).wait_send()

    total = norms[0]
    for n in range(1, 8):
        norm_copy(n).wait()
        total = total + norms[n]
    norm_ref[...] = total

    @pl.when(s > 0)
    def _():
        edge.wait_send()

    @pl.when(s < 7)
    def _():
        edge.wait_recv()


def reduce(gw, gv):
    dma = pltpu.SemaphoreType.DMA
    return pl.pallas_call(
        reduce_kernel,
        name="reduce",
        out_shape=(jax.ShapeDtypeStruct((FLAT, LANES), F32), jax.ShapeDtypeStruct((8, LANES), F32)),
        in_specs=[pl.BlockSpec(memory_space=pl.ANY), VM],
        out_specs=(VM, VM),
        scratch_shapes=[
            pltpu.VMEM((96, PIECE, D), BF16),
            pltpu.VMEM((4, 12, PIECE, D), BF16),
            pltpu.VMEM((4, 2, 3, HALF, D), BF16),
            pltpu.VMEM((4, 3, HALF, D), BF16),
            pltpu.VMEM((4, 2, 3, HALF, D), BF16),
            pltpu.VMEM((4, 3, HALF, D), BF16),
            pltpu.VMEM((4, 3, PIECE, D), BF16),
            pltpu.VMEM((4, 3, PIECE, D), BF16),
            pltpu.VMEM((12, PIECE, D), BF16),
            pltpu.VMEM((6, 16, D), F32),
            pltpu.VMEM((5, 16, D), F32),
            pltpu.VMEM((8, 8, LANES), F32),
            dma,
            dma((4, 12)),
            dma((4, 12)),
            dma((2, 4, 2, 3)),
            dma((2, 4, 2, 3)),
            dma((2, 4, 3)),
            dma((2, 4, 3)),
            dma((2, 4, 3)),
            dma((2, 4, 3)),
            dma((4, 3)),
            dma((4, 3)),
            dma((5,)),
            dma((5,)),
            dma((2,)),
            dma((8,)),
            dma((8,)),
        ],
        compiler_params=pltpu.CompilerParams(collective_id=1, has_side_effects=True, vmem_limit_bytes=LIMIT),
    )(gw, gv)


STEP_ROWS = 1024


def update_kernel(flat_ref, norm_ref, param_ref, first_ref, second_ref, grad_out, change_out, first_out, second_out):
    s = lax.axis_index("fsdp")
    n = pl.program_id(0)
    rows = param_ref.shape[0]
    grad = flat_ref[pl.ds(n * rows + 9 * s, rows), :]
    squares = jnp.sum(jnp.sum(norm_ref[...], axis=0, keepdims=True), axis=1, keepdims=True)
    factor = jnp.minimum(1.0, 1.0 / (jnp.sqrt(squares) + 1e-06))
    clipped = grad * factor
    new_first = 0.9 * first_ref[...] + 0.1 * clipped
    new_second = 0.999 * second_ref[...] + 0.001 * clipped * clipped
    first_hat = new_first * (1.0 / first_correct)
    second_hat = new_second * (1.0 / second_correct)
    row = s * 6921 + n * rows + lax.broadcasted_iota(jnp.int32, (rows, LANES), 0)
    decay = jnp.where(row < MATS // LANES, 0.05, 0.0)
    step_rate = 0.001 * 0.75**6
    grad_out[...] = grad
    first_out[...] = new_first
    second_out[...] = new_second
    change_out[...] = step_rate * (first_hat / (jnp.sqrt(second_hat) + 1e-08) + decay * param_ref[...])


def update(flat, norm, params, first, second):
    rows = params.shape[0]
    spec = pl.BlockSpec((STEP_ROWS, LANES), lambda n: (n, 0))
    return pl.pallas_call(
        update_kernel,
        name="update",
        grid=(pl.cdiv(rows, STEP_ROWS),),
        out_shape=[jax.ShapeDtypeStruct((rows, LANES), F32)] * 4,
        in_specs=[VM, VM, spec, spec, spec],
        out_specs=[spec] * 4,
        compiler_params=pltpu.CompilerParams(vmem_limit_bytes=LIMIT),
    )(flat, norm, params, first, second)


def shards(tokens, cotangent, keep_index, clip_ids, flat_params, first_moment, second_moment):
    flat = flat_params.reshape(-1, LANES)
    weights, vectors = gather(flat)
    pad = ROWS - tokens.shape[0]
    keep = jnp.pad(keep_index.reshape(-1, 1), ((0, pad), (0, 0)))
    clip = jnp.pad(jnp.repeat(clip_ids.reshape(-1), KEEP), (0, pad), constant_values=-1)
    clip_col, clip_row = clip[:, None], clip[None, :]
    layer_out, *kept = forward(tokens, keep, clip_col, clip_row, weights, vectors)
    grad_tokens, gw, gv = backward(cotangent, clip_col, clip_row, weights, vectors, kept)
    summed, norm = reduce(gw, gv)
    outs = update(summed, norm, flat, first_moment.reshape(-1, LANES), second_moment.reshape(-1, LANES))
    grad, change, first, second = (o.reshape(-1) for o in outs)
    return (layer_out, grad_tokens, grad, change, first, second)


def layer_norm(values, gain_vec, shift_vec):
    row_mean = jnp.mean(values, axis=-1, keepdims=True)
    centered = values - row_mean
    variance = jnp.mean(centered * centered, axis=-1, keepdims=True)
    return centered * lax.rsqrt(variance + 1e-06) * gain_vec + shift_vec


def gelu_exact(values):
    return jax.nn.gelu(values, approximate=False)


def positions(keep_flat):
    quarter = D // 4
    frequency = 1.0 / 10000.0 ** (jnp.arange(quarter).astype(jnp.float32) / quarter)
    row_angle = (keep_flat // GRID).astype(jnp.float32)[:, None] * frequency
    col_angle = (keep_flat % GRID).astype(jnp.float32)[:, None] * frequency
    return jnp.concatenate(
        [jnp.sin(row_angle), jnp.cos(row_angle), jnp.sin(col_angle), jnp.cos(col_angle)], axis=1
    )


def unpack_flat(flat):
    mats = 4 * D * D + 2 * D * FF
    w_qkv = flat[: 3 * D * D].reshape(D, 3 * D)
    w_out = flat[3 * D * D : 4 * D * D].reshape(D, D)
    w_up = flat[4 * D * D : 4 * D * D + D * FF].reshape(D, FF)
    w_down = flat[4 * D * D + D * FF : mats].reshape(FF, D)
    vectors = flat[mats : mats + 8 * D].reshape(8, D)
    bias_up = flat[mats + 8 * D :]
    return (w_qkv, w_out, w_up, w_down, vectors, bias_up)


def split_heads(values):
    return values.reshape(values.shape[0], HEADS, HEAD_DIM).transpose(1, 0, 2)


def join_heads(values):
    return values.transpose(1, 0, 2).reshape(values.shape[1], D)


def product(left, right):
    return jnp.dot(left, right, preferred_element_type=jnp.float32)


def plain_shards(tokens, cotangent, keep_index, clip_ids, flat_params, first_moment, second_moment):
    shard_len = flat_params.shape[0]
    mats = 4 * D * D + 2 * D * FF
    score_scale = HEAD_DIM ** (-0.5)
    sent = flat_params.astype(jnp.bfloat16)
    gathered = lax.all_gather(sent, "fsdp", axis=0, tiled=True)
    w_qkv, w_out, w_up, w_down, vectors_low, bias_up_low = unpack_flat(gathered)
    vectors = vectors_low.astype(jnp.float32)
    bias_up = bias_up_low.astype(jnp.float32)
    embedded = tokens.astype(jnp.float32) + positions(keep_index.reshape(-1))
    normed, norm_back = jax.vjp(layer_norm, embedded, vectors[0], vectors[1])
    normed_low = normed.astype(jnp.bfloat16)
    mixed_qkv = product(normed_low, w_qkv)
    query_low = (mixed_qkv[:, :D] + vectors[2]).astype(jnp.bfloat16)
    key_low = mixed_qkv[:, D : 2 * D].astype(jnp.bfloat16)
    value_low = (mixed_qkv[:, 2 * D :] + vectors[3]).astype(jnp.bfloat16)
    query_heads = split_heads(query_low)
    key_heads = split_heads(key_low)
    value_heads = split_heads(value_low)
    clip_tok = jnp.repeat(clip_ids.reshape(-1), KEEP)
    same_clip = clip_tok[:, None] == clip_tok[None, :]

    def attend(head_item):
        q_head, k_head, v_head = head_item
        scores = jnp.where(same_clip, product(q_head, k_head.T) * score_scale, -1e30)
        row_top = jnp.max(scores, axis=1, keepdims=True)
        weight_exp = jnp.exp(scores - row_top)
        row_total = jnp.sum(weight_exp, axis=1, keepdims=True)
        soft_low = (weight_exp / row_total).astype(jnp.bfloat16)
        return (product(soft_low, v_head), row_top + jnp.log(row_total))

    attended_heads, log_total = lax.map(attend, (query_heads, key_heads, value_heads))
    attended_low = join_heads(attended_heads).astype(jnp.bfloat16)
    resid = embedded + product(attended_low, w_out) + vectors[4]
    normed_two, norm_two_back = jax.vjp(layer_norm, resid, vectors[5], vectors[6])
    normed_two_low = normed_two.astype(jnp.bfloat16)
    pre_act = product(normed_two_low, w_up) + bias_up
    activated, gelu_back = jax.vjp(gelu_exact, pre_act)
    activated_low = activated.astype(jnp.bfloat16)
    layer_out = (resid + product(activated_low, w_down) + vectors[7]).astype(jnp.bfloat16)
    w_qkv, w_out, w_up, w_down, vectors_low, bias_up_low = unpack_flat(
        lax.all_gather(sent, "fsdp", axis=0, tiled=True)
    )
    grad_out = cotangent.astype(jnp.float32)
    grad_w_down = product(activated_low.T, cotangent)
    grad_bias_down = jnp.sum(grad_out, axis=0)
    grad_act = product(cotangent, w_down.T)
    grad_pre_low = gelu_back(grad_act)[0].astype(jnp.bfloat16)
    grad_w_up = product(normed_two_low.T, grad_pre_low)
    grad_bias_up = jnp.sum(grad_pre_low.astype(jnp.float32), axis=0)
    grad_normed_two = product(grad_pre_low, w_up.T)
    grad_resid_norm, grad_gain_two, grad_shift_two = norm_two_back(grad_normed_two)
    grad_resid = grad_out + grad_resid_norm
    grad_branch_low = grad_resid.astype(jnp.bfloat16)
    grad_w_out = product(attended_low.T, grad_branch_low)
    grad_bias_out = jnp.sum(grad_branch_low.astype(jnp.float32), axis=0)
    grad_attended_low = product(grad_branch_low, w_out.T).astype(jnp.bfloat16)

    def attend_back(head_item):
        q_head, k_head, v_head, g_head, lse_head = head_item
        soft = jnp.where(
            same_clip, jnp.exp(product(q_head, k_head.T) * score_scale - lse_head), 0.0
        )
        grad_soft = product(g_head, v_head.T)
        grad_value = product(soft.astype(jnp.bfloat16).T, g_head)
        inner = jnp.sum(soft * grad_soft, axis=1, keepdims=True)
        grad_raw = (score_scale * soft * (grad_soft - inner)).astype(jnp.bfloat16)
        return (product(grad_raw, k_head), product(grad_raw.T, q_head), grad_value)

    grad_query, grad_key, grad_value = lax.map(
        attend_back,
        (query_heads, key_heads, value_heads, split_heads(grad_attended_low), log_total),
    )
    grad_mixed = jnp.concatenate(
        [join_heads(grad_query), join_heads(grad_key), join_heads(grad_value)], axis=1
    ).astype(jnp.bfloat16)
    grad_w_qkv = product(normed_low.T, grad_mixed)
    mixed_sums = jnp.sum(grad_mixed.astype(jnp.float32), axis=0)
    grad_normed = product(grad_mixed, w_qkv.T)
    grad_embedded, grad_gain_one, grad_shift_one = norm_back(grad_normed)
    grad_tokens = grad_resid + grad_embedded
    full_grad = jnp.concatenate(
        [
            grad_w_qkv.reshape(-1),
            grad_w_out.reshape(-1),
            grad_w_up.reshape(-1),
            grad_w_down.reshape(-1),
            grad_gain_one,
            grad_shift_one,
            mixed_sums[:D],
            mixed_sums[2 * D :],
            grad_bias_out,
            grad_gain_two,
            grad_shift_two,
            grad_bias_down,
            grad_bias_up,
        ]
    )
    replicas = lax.axis_size("dp")
    owners = lax.axis_size("fsdp")
    reordered = full_grad.reshape(owners, replicas, -1).transpose(1, 0, 2).reshape(-1)
    own_piece = lax.psum_scatter(reordered, ("dp", "fsdp"), scatter_dimension=0, tiled=True)
    own_grad = lax.all_gather(own_piece.astype(jnp.bfloat16), "dp", axis=0, tiled=True).astype(
        own_piece.dtype
    )
    squares = lax.psum(jnp.sum(own_grad * own_grad), "fsdp")
    clip_factor = jnp.minimum(1.0, 1.0 / (jnp.sqrt(squares) + 1e-06))
    clipped = own_grad * clip_factor
    new_first = 0.9 * first_moment + 0.1 * clipped
    new_second = 0.999 * second_moment + 0.001 * clipped * clipped
    first_hat = new_first / first_correct
    second_hat = new_second / second_correct
    position = lax.axis_index("fsdp") * shard_len + jnp.arange(shard_len, dtype=jnp.int32)
    decay_mask = (position < mats).astype(jnp.float32)
    step_rate = 0.001 * 0.75**6
    param_change = step_rate * (
        first_hat / (jnp.sqrt(second_hat) + 1e-08) + 0.05 * decay_mask * flat_params
    )
    return (layer_out, grad_tokens, own_grad, param_change, new_first, new_second)


def solution(mesh):
    placed = (
        P(("dp", "fsdp"), None),
        P(("dp", "fsdp"), None),
        P(("dp", "fsdp"), None),
        P(("dp", "fsdp"), None),
        P("fsdp"),
        P("fsdp"),
        P("fsdp"),
    )
    staged = mesh.shape["dp"] == 4 and mesh.shape["fsdp"] == 8
    return jax.shard_map(
        shards if staged else plain_shards,
        mesh=mesh,
        in_specs=placed,
        out_specs=(
            P(("dp", "fsdp"), None),
            P(("dp", "fsdp"), None),
            P("fsdp"),
            P("fsdp"),
            P("fsdp"),
            P("fsdp"),
        ),
        check_vma=False,
    )
```

```python
import functools

import jax
import jax.numpy as jnp
import numpy as np
from jax import lax
from jax.experimental import pallas as pl
from jax.experimental.pallas import tpu as pltpu
from jax.sharding import PartitionSpec as P

D = 768
FF = 3072
HEADS = 12
HEAD_DIM = 64
GRID = 14
KEEP = 49
MATS = 4 * D * D + 2 * D * FF

first_correct = 0.9999734386011124
second_correct = 0.09520785288629106

F32 = jnp.float32
BF16 = jnp.bfloat16
MESH = pl.DeviceIdType.MESH
LIMIT = 66_000_000

ROWS = 400
CHUNK = 80
PIECE = 96
PIECES = 12
LANES = 128
TAIL = 72


def ge(s, k):
    return (s + 8 - k) // 8


def piece_of(s, i):
    g5 = (i + 4) // 8
    forms = (
        8 * (i // 4) + i % 4,
        8 * (i // 4) + 4 + i % 4,
        24 + i + (i // 8) * (7 * i - 56),
        33 + 8 * (i // 3) + i % 3,
        36 + 8 * (i // 3) + i % 3,
        (1 - g5) * (39 + 8 * i) + g5 * (60 + i),
        72 + i,
        84 + i,
    )
    out = 0
    for k, form in enumerate(forms):
        out = out + (ge(s, k) - ge(s, k + 1)) * form
    return out


def dot(a, b):
    return lax.dot_general(a, b, (((1,), (0,)), ((), ())), preferred_element_type=F32)


def dot_nt(a, b):
    return lax.dot_general(a, b, (((1,), (1,)), ((), ())), preferred_element_type=F32)


def dot_tn(a, b):
    return lax.dot_general(a, b, (((0,), (0,)), ((), ())), preferred_element_type=F32)


def loop(start, stop, body):
    def step(i, carry):
        body(i)
        return carry

    lax.fori_loop(start, stop, step, 0)


def chunks(body):
    loop(0, ROWS // CHUNK, lambda n: body(pl.ds(pl.multiple_of(n * CHUNK, CHUNK), CHUNK)))


class Place:
    def __init__(self):
        self.dp = lax.axis_index("dp")
        self.s = lax.axis_index("fsdp")
        self.x, self.y = self.dp % 2, self.dp // 2
        self.z, self.c = self.s // 2, self.s % 2
        self.sib = self.at(self.dp, self.s + 1 - 2 * self.c)
        self.xn = self.at(self.dp + 1 - 2 * self.x, self.s)
        self.yn = self.at(self.dp + 2 - 4 * self.y, self.s)
        self.up = self.at(self.dp, self.s + 2)
        self.down = self.at(self.dp, self.s - 2)

    def at(self, dp, s):
        return (dp, s)

    def barrier(self):
        sem = pltpu.get_barrier_semaphore()
        for n in range(1, 8):
            pl.semaphore_signal(sem, inc=1, device_id=self.at(self.dp, (self.s + n) % 8), device_id_type=MESH)
        for peer in (self.xn, self.yn):
            pl.semaphore_signal(sem, inc=1, device_id=peer, device_id_type=MESH)
        pl.semaphore_wait(sem, 9)


def remote(src, dst, send, recv, to):
    return pltpu.make_async_remote_copy(
        src_ref=src, dst_ref=dst, send_sem=send, recv_sem=recv, device_id=to, device_id_type=MESH
    )


def weave(s, body):
    @pl.when(s <= 1)
    def _():
        loop(0, 12, lambda i: body(i, 18, (i % 4) * (96 * 18) + (i // 4) * 6))

    @pl.when(s == 2)
    def _():
        loop(0, 8, lambda i: body(i, 6, i * (96 * 6)))
        loop(8, 12, lambda i: body(i, 24, 4608 + (i - 8) * 6))

    @pl.when((s == 3) | (s == 4))
    def _():
        loop(0, 12, lambda i: body(i, 24, (i % 3) * (96 * 24) + (i // 3) * 6))

    @pl.when(s == 5)
    def _():
        loop(0, 4, lambda i: body(i, 24, i * 6))
        loop(4, 12, lambda i: body(i, 6, 2304 + (i - 4) * (96 * 6)))

    @pl.when(s >= 6)
    def _():
        loop(0, 12, lambda i: body(i, 6, i * (96 * 6)))


def gather_kernel(own_ref, g_ref, v_ref, buf, tail, vbuf, edge_sem, v_send, v_recv, z_send, z_recv, p_send, p_recv, c_send, c_recv):
    me = Place()
    s, z, c = me.s, me.z, me.c
    q = me.dp
    rows = own_ref.shape[0]
    tail[...] = own_ref[rows - TAIL : rows, :]
    me.barrier()

    edge = remote(tail, buf.at[pl.ds(0, TAIL)], edge_sem.at[0], edge_sem.at[1], me.at(me.dp, (s + 1) % 8))

    @pl.when(s < 7)
    def _():
        edge.start()

    @pl.when(s == 7)
    def _():
        for n in range(7):
            remote(tail, vbuf, v_send.at[n], v_recv, me.at(me.dp, n)).start()
        vbuf[...] = tail[...]

    full = rows // 8
    loop(0, full // 5, lambda n: buf.__setitem__((pl.ds(pl.multiple_of(TAIL + n * 40, 8), 40), slice(None)), own_ref[pl.ds(pl.multiple_of(n * 40, 8), 40), :]))
    buf[TAIL + full * 8 : TAIL + rows, :] = own_ref[full * 8 : rows, :]

    @pl.when(s > 0)
    def _():
        edge.wait_recv()

    def to_sib(p, i):
        piece = piece_of(2 * p + c, i)
        remote(g_ref.at[piece], g_ref.at[piece], c_send.at[p, i], c_recv.at[p, i], me.sib).start()

    def z_copy(p, k, way, to):
        piece = piece_of(2 * p + c, 3 * q + k)
        return remote(g_ref.at[piece], g_ref.at[piece], z_send.at[way, p, k], z_recv.at[p, k], to)

    def plane_copy(kind, p, quarter, k, to):
        piece = piece_of(2 * p + c, 3 * quarter + k)
        ref = g_ref.at[piece]
        if kind >= 2:
            ref = g_ref.at[piece, pl.ds(48 * (kind - 2), 48)]
        return remote(ref, ref, p_send.at[kind, p, k], p_recv.at[kind, p, k], to)

    def place_piece(i, stride, first):
        piece = piece_of(s, i)
        for j in range(6):
            g_ref[piece, :, LANES * j : LANES * (j + 1)] = buf[pl.ds(TAIL - 9 * s + first + j, PIECE, stride=stride), :].astype(BF16)

    weave(s, place_piece)

    def own_sends(k):
        @pl.when(z < 3)
        def _():
            z_copy(z, k, 0, me.up).start()

        @pl.when(z > 0)
        def _():
            z_copy(z, k, 1, me.down).start()

    loop(0, 3, own_sends)
    loop(0, 12, lambda i: to_sib(z, i))

    qx = me.dp + 1 - 2 * me.x
    qy = me.dp + 2 - 4 * me.y
    qd = 3 - me.dp

    def both(d, body):
        @pl.when(z >= d)
        def _():
            loop(0, 3, lambda k: body(z - d, k, 0))

        @pl.when(z + d <= 3)
        def _():
            loop(0, 3, lambda k: body(z + d, k, 1))

    def z_arrive(p, k, way):
        z_copy(p, k, way, me.up).wait_recv()
        if way == 0:

            @pl.when(z < 3)
            def _():
                z_copy(p, k, 0, me.up).start()
        else:

            @pl.when(z > 0)
            def _():
                z_copy(p, k, 1, me.down).start()

        plane_copy(0, p, q, k, me.xn).start()
        plane_copy(1, p, q, k, me.yn).start()
        to_sib(p, 3 * q + k)

    def xy_arrive(p, k, way):
        plane_copy(0, p, qx, k, me.xn).wait_recv()
        plane_copy(3, p, qx, k, me.yn).start()
        to_sib(p, 3 * qx + k)
        plane_copy(1, p, qy, k, me.yn).wait_recv()
        plane_copy(2, p, qy, k, me.xn).start()
        to_sib(p, 3 * qy + k)

    def d_arrive(p, k, way):
        plane_copy(2, p, qd, k, me.xn).wait_recv()
        plane_copy(3, p, qd, k, me.yn).wait_recv()
        to_sib(p, 3 * qd + k)

    both(1, z_arrive)
    both(2, z_arrive)
    both(1, xy_arrive)
    both(3, z_arrive)
    both(2, xy_arrive)
    both(1, d_arrive)
    both(3, xy_arrive)
    both(2, d_arrive)
    both(3, d_arrive)

    @pl.when(s < 7)
    def _():
        remote(tail, vbuf, v_send.at[0], v_recv, me.sib).wait_recv()
        edge.wait_send()

    @pl.when(s == 7)
    def _():
        for n in range(7):
            remote(tail, vbuf, v_send.at[n], v_recv, me.sib).wait_send()

    for j in range(6):
        v_ref[0:12, LANES * j : LANES * (j + 1)] = vbuf[pl.ds(j, 12, stride=6), :].astype(BF16).astype(F32)

    def own_done(k):
        @pl.when(z < 3)
        def _():
            z_copy(z, k, 0, me.up).wait_send()

        @pl.when(z > 0)
        def _():
            z_copy(z, k, 1, me.down).wait_send()

    loop(0, 3, own_done)

    def far_done(p, k, way):
        if way == 0:

            @pl.when(z < 3)
            def _():
                z_copy(p, k, 0, me.up).wait_send()
        else:

            @pl.when(z > 0)
            def _():
                z_copy(p, k, 1, me.down).wait_send()

        plane_copy(0, p, q, k, me.xn).wait_send()
        plane_copy(1, p, q, k, me.yn).wait_send()
        plane_copy(2, p, qy, k, me.xn).wait_send()
        plane_copy(3, p, qx, k, me.yn).wait_send()

    for d in (1, 2, 3):
        both(d, far_done)

    def sib_done(n):
        p, i = n // 12, n % 12
        piece = piece_of(2 * p + c, i)
        copy = remote(g_ref.at[piece], g_ref.at[piece], c_send.at[p, i], c_recv.at[p, i], me.sib)
        copy.wait_send()
        copy.wait_recv()

    loop(0, 48, sib_done)


def gather(own):
    dma = pltpu.SemaphoreType.DMA
    return pl.pallas_call(
        gather_kernel,
        name="gather",
        out_shape=(jax.ShapeDtypeStruct((96, PIECE, D), BF16), jax.ShapeDtypeStruct((16, D), F32)),
        in_specs=[pl.BlockSpec(memory_space=pltpu.VMEM)],
        out_specs=(pl.BlockSpec(memory_space=pltpu.VMEM), pl.BlockSpec(memory_space=pltpu.VMEM)),
        scratch_shapes=[
            pltpu.VMEM((7000, LANES), F32),
            pltpu.VMEM((TAIL, LANES), F32),
            pltpu.VMEM((TAIL, LANES), F32),
            dma((2,)),
            dma((7,)),
            dma,
            dma((2, 4, 3)),
            dma((4, 3)),
            dma((4, 4, 3)),
            dma((4, 4, 3)),
            dma((4, 12)),
            dma((4, 12)),
        ],
        compiler_params=pltpu.CompilerParams(collective_id=0, has_side_effects=True, vmem_limit_bytes=LIMIT),
    )(own)


def position_table():
    quarter = D // 4
    exponent = np.arange(quarter, dtype=np.float32) / np.float32(quarter)
    frequency = np.float32(1.0) / np.power(np.float32(10000.0), exponent).astype(np.float32)
    angle = (np.arange(GRID, dtype=np.float32)[:, None] * frequency).astype(np.float64)
    waves = np.concatenate([np.sin(angle), np.cos(angle)], axis=1).astype(np.float32)
    table = np.zeros((32, D), np.float32)
    table[:GRID, : D // 2] = waves
    table[16 : 16 + GRID, D // 2 :] = waves
    parts = []
    for _ in range(3):
        part = table.astype(jnp.bfloat16)
        parts.append(part)
        table = table - part.astype(np.float32)
    return np.stack(parts)


def norm_stats(v):
    mean = jnp.mean(v, axis=-1, keepdims=True)
    centered = v - mean
    rstd = lax.rsqrt(jnp.mean(centered * centered, axis=-1, keepdims=True) + 1e-06)
    return centered * rstd, rstd


def block(g_ref, b):
    return g_ref[pl.ds(8 * b, 8)].reshape(D, D)


def slabs(ref, first):
    return jnp.concatenate([ref[first + j] for j in range(6)], axis=1)


def embed(tok_ref, keep_ref, table_ref, v_ref, emb, n1):
    real = tok_ref.shape[0]
    emb[0:real, :] = tok_ref[...].astype(F32)
    emb[real:, :] = jnp.zeros((ROWS - real, D), F32)
    gain, shift = v_ref[0:1, :], v_ref[1:2, :]

    def body(at):
        keep = keep_ref[at, :]
        row = (keep * 4682) >> 16
        col = keep - GRID * row + 16
        lane = lax.broadcasted_iota(jnp.int32, (CHUNK, 32), 1)
        hot = jnp.where((lane == row) | (lane == col), 1.0, 0.0).astype(BF16)
        spot = dot(hot, table_ref[0]) + (dot(hot, table_ref[1]) + dot(hot, table_ref[2]))
        value = emb[at, :] + spot
        emb[at, :] = value
        n1[at, :] = (norm_stats(value)[0] * gain + shift).astype(BF16)

    chunks(body)


def project(n1, g_ref, v_ref, qkv):
    for b in range(3):
        mixed = dot(n1[...], block(g_ref, b))
        if b != 1:
            mixed = mixed + v_ref[2 + b // 2 : 3 + b // 2, :]
        for j in range(6):
            qkv[6 * b + j] = mixed[:, LANES * j : LANES * (j + 1)].astype(BF16)


def attend(j, same_of, qkv, att, lse):
    query, key, value = qkv[j], qkv[6 + j], qkv[12 + j]
    first = lax.broadcasted_iota(jnp.int32, (ROWS, LANES), 1) < HEAD_DIM
    turned = value.T
    parts = []
    for h in range(2):
        own = jnp.where(first if h == 0 else ~first, query, jnp.zeros_like(query))
        scores = jnp.where(same_of(), dot_nt(key, own) * 0.125, -1e30)
        top = jnp.max(scores, axis=0, keepdims=True)
        weight = jnp.exp(scores - top)
        total = jnp.sum(weight, axis=0, keepdims=True)
        soft = (weight * (1.0 / total)).astype(BF16)
        lse[2 * j + h] = top + jnp.log(total)
        parts.append(dot(turned[HEAD_DIM * h : HEAD_DIM * (h + 1), :], soft))
    att[j] = jnp.concatenate(parts, axis=0).T.astype(BF16)


def out_project(att, g_ref, v_ref, emb, resid, n2):
    resid[...] = dot(slabs(att, 0), block(g_ref, 3))
    bias, gain, shift = v_ref[4:5, :], v_ref[5:6, :], v_ref[6:7, :]

    def body(at):
        value = emb[at, :] + resid[at, :] + bias
        resid[at, :] = value
        n2[at, :] = (norm_stats(value)[0] * gain + shift).astype(BF16)

    chunks(body)


def expand(j, n2, g_ref, v_ref, work, act, slope):
    work[...] = dot(n2[...], block(g_ref, 4 + j))

    def body(at):
        pre = work[at, :] + v_ref[pl.ds(8 + j, 1), :]
        phi = 0.5 * (1.0 + lax.erf(pre * 0.7071067811865476))
        act[j, at, :] = (pre * phi).astype(BF16)
        slope[j, at, :] = (phi + pre * (0.3989422804014327 * jnp.exp(-0.5 * pre * pre))).astype(BF16)

    chunks(body)


def contract(j, act, g_ref, work):
    part = dot(act[j], block(g_ref, 8 + j))

    @pl.when(j == 0)
    def _():
        work[...] = part

    @pl.when(j > 0)
    def _():
        work[...] += part


def forward_kernel(tok_ref, keep_ref, clip_col, clip_row, table_ref, g_ref, v_ref, out_ref, emb, n1, qkv, att, lse, resid, n2, act, slope, work):
    same_of = lambda: clip_col[...] == clip_row[...]
    embed(tok_ref, keep_ref, table_ref, v_ref, emb, n1)
    project(n1, g_ref, v_ref, qkv)
    loop(0, 6, lambda j: attend(j, same_of, qkv, att, lse))
    out_project(att, g_ref, v_ref, emb, resid, n2)
    loop(0, 4, lambda j: expand(j, n2, g_ref, v_ref, work, act, slope))
    loop(0, 4, lambda j: contract(j, act, g_ref, work))
    real = out_ref.shape[0]
    out_ref[...] = (resid[0:real, :] + work[0:real, :] + v_ref[7:8, :]).astype(BF16)


def kept_shapes():
    return [
        ((ROWS, D), F32),
        ((ROWS, D), BF16),
        ((18, ROWS, LANES), BF16),
        ((6, ROWS, LANES), BF16),
        ((HEADS, 1, ROWS), F32),
        ((ROWS, D), F32),
        ((ROWS, D), BF16),
        ((4, ROWS, D), BF16),
        ((4, ROWS, D), BF16),
    ]


VM = pl.BlockSpec(memory_space=pltpu.VMEM)


def forward(tokens, keep, clip_col, clip_row, weights, vectors):
    table = jnp.asarray(position_table())
    return pl.pallas_call(
        forward_kernel,
        name="forward",
        out_shape=[jax.ShapeDtypeStruct(tokens.shape, BF16)] + [jax.ShapeDtypeStruct(*k) for k in kept_shapes()],
        in_specs=[VM] * 7,
        out_specs=[VM] * 10,
        scratch_shapes=[pltpu.VMEM((ROWS, D), F32)],
        compiler_params=pltpu.CompilerParams(vmem_limit_bytes=LIMIT),
    )(tokens, keep, clip_col, clip_row, table, weights, vectors)


def col_sums(dest, row, source):
    dest[row : row + 1, :] = jnp.sum(source, axis=0, keepdims=True)


def put_block(gw, b, value):
    gw[pl.ds(8 * b, 8)] = value.astype(BF16).reshape(8, PIECE, D)


def act_grad(j, cot, n2, down, up, slope, gw, gv, work, pre_low, gn):
    work[...] = dot_nt(cot[...], down())
    total = jnp.zeros((8, D), F32)

    def body(n, total):
        at = pl.ds(pl.multiple_of(n * CHUNK, CHUNK), CHUNK)
        low = (slope[j, at, :].astype(F32) * work[at, :]).astype(BF16)
        pre_low[at, :] = low
        return total + jnp.sum(low.astype(F32).reshape(CHUNK // 8, 8, D), axis=0)

    total = lax.fori_loop(0, ROWS // CHUNK, body, total)
    gv[8 + j : 9 + j, :] = jnp.sum(total, axis=0, keepdims=True)
    put_block(gw, 4 + j, dot_tn(n2[...], pre_low[...]))
    part = dot_nt(pre_low[...], up())
    gn[...] = part if j == 0 else gn[...] + part


def norm_back(value_ref, gn, gain, extra, store, gv, row):
    def body(n, sums):
        at = pl.ds(pl.multiple_of(n * CHUNK, CHUNK), CHUNK)
        hat, rstd = norm_stats(value_ref[at, :])
        grad = gn[at, :]
        fold = lambda v: jnp.sum(v.reshape(CHUNK // 8, 8, D), axis=0)
        sums = (sums[0] + fold(grad * hat), sums[1] + fold(grad))
        grad = grad * gain
        inner = jnp.mean(grad * hat, axis=-1, keepdims=True)
        store(at, extra(at) + rstd * (grad - jnp.mean(grad, axis=-1, keepdims=True) - hat * inner))
        return sums

    zero = jnp.zeros((8, D), F32)
    one, two = lax.fori_loop(0, ROWS // CHUNK, body, (zero, zero))
    gv[row : row + 1, :] = jnp.sum(one, axis=0, keepdims=True)
    gv[row + 1 : row + 2, :] = jnp.sum(two, axis=0, keepdims=True)


def attend_back(j, same_of, qkv, lse, ga, gm):
    query, key, value, grad = qkv[j], qkv[6 + j], qkv[12 + j], ga[j]
    first = lax.broadcasted_iota(jnp.int32, (ROWS, LANES), 1) < HEAD_DIM
    turned = key.T
    parts, grad_key, grad_value = [], None, None
    for h in range(2):
        mine = first if h == 0 else ~first
        own = jnp.where(mine, query, jnp.zeros_like(query))
        own_grad = jnp.where(mine, grad, jnp.zeros_like(grad))
        soft = jnp.where(same_of(), jnp.exp(dot_nt(key, own) * 0.125 - lse[2 * j + h]), 0.0)
        grad_soft = dot_nt(value, own_grad)
        inner = jnp.sum(soft * grad_soft, axis=0, keepdims=True)
        raw = (0.125 * soft * (grad_soft - inner)).astype(BF16)
        one = dot(soft.astype(BF16), own_grad)
        two = dot(raw, own)
        grad_value = one if h == 0 else grad_value + one
        grad_key = two if h == 0 else grad_key + two
        parts.append(dot(turned[HEAD_DIM * h : HEAD_DIM * (h + 1), :], raw))
    gm[j] = jnp.concatenate(parts, axis=0).T.astype(BF16)
    gm[6 + j] = grad_key.astype(BF16)
    gm[12 + j] = grad_value.astype(BF16)


FLAT = 7240
HALF = PIECE // 2


def backward_kernel(
    cot_ref, clip_col, clip_row, g_hbm, v_ref, *refs
):
    kept_hbm, refs = refs[:9], refs[9:]
    gtok_ref, flat_ref, norm_ref = refs[:3]
    kept, refs = refs[3:12], refs[12:]
    (
        cot, work, low_rows, gn, ga, gm, gv, slots, tok_out,
        gw, sib, xa, ya, yb, xb, zu, zd, shard, vsum, vpart, norms,
        load_sem, slot_sem, tok_sem,
        sib_send, sib_recv, h_send, h_recv, t_send, t_recv, z_send, z_recv, g_send, g_recv, v_send, v_recv, e_sem, n_send, n_recv,
    ) = refs
    emb, n1, qkv, att, lse, resid, n2, act, slope = kept
    me = Place()
    s, z, c, x, y = me.s, me.z, me.c, me.x, me.y
    q = me.dp

    def load(n):
        return pltpu.make_async_copy(kept_hbm[n], kept[n], load_sem.at[n])

    def fetch(n):
        return pltpu.make_async_copy(g_hbm.at[pl.ds(8 * WEIGHT_ORDER[n], 8)], slots.at[n % 3], slot_sem.at[n % 3])

    def weight(n):
        fetch(n).wait()
        if n >= 1 and n + 2 < len(WEIGHT_ORDER):
            fetch(n + 2).start()
        return slots[n % 3].reshape(D, D)

    for n in (7, 8, 6):
        load(n).start()
    for n in range(3):
        fetch(n).start()
    for n in (5, 3, 2, 4, 1, 0):
        load(n).start()
    flat_ref[6912:, :] = jnp.zeros((FLAT - 6912, LANES), F32)
    real = cot_ref.shape[0]
    gv[...] = jnp.zeros_like(gv)
    cot[...] = jnp.concatenate([cot_ref[...].astype(F32), jnp.zeros((ROWS - real, D), F32)], axis=0).astype(BF16)
    me.barrier()

    def add_into(piece, rows, got):
        gw[piece, rows, :] = (gw[piece, rows, :].astype(F32) + got.astype(F32)).astype(BF16)

    low, high, whole = pl.ds(0, HALF), pl.ds(HALF, HALF), pl.ds(0, PIECE)

    def sib_copy(p, i):
        piece = piece_of(2 * p + 1 - c, i)
        return remote(gw.at[piece], sib.at[p, i], sib_send.at[p, i], sib_recv.at[p, i], me.sib)

    def send_block(b):
        for parity in range(2):
            pieces = [(w // 2, i) for w in range(parity, 8, 2) for i in range(12) if piece_of(w, i) // 8 == b]
            if pieces:

                @pl.when(c == 1 - parity)
                def _(pieces=pieces):
                    for p, i in pieces:
                        sib_copy(p, i).start()

    partners = (me.sib, me.xn, me.yn, me.at(me.dp, (s + 2 - 4 * (z % 2)) % 8), me.at(me.dp, (s + 4) % 8))

    def v_step(n):
        copy = remote(vsum.at[n], vpart.at[n], v_send.at[n], v_recv.at[n], partners[n])
        return copy

    def xa_copy(p, yy, k):
        piece = piece_of(2 * p + c, 3 * (2 * yy + 1 - x) + k)
        return remote(gw.at[piece, low], xa.at[p, yy, k], h_send.at[0, p, yy, k], h_recv.at[0, p, yy, k], me.xn)

    def yb_copy(p, xx, k):
        piece = piece_of(2 * p + c, 3 * (2 * (1 - y) + xx) + k)
        return remote(gw.at[piece, high], yb.at[p, xx, k], h_send.at[1, p, xx, k], h_recv.at[1, p, xx, k], me.yn)

    def ya_copy(p, k):
        piece = piece_of(2 * p + c, 3 * (2 * (1 - y) + x) + k)
        return remote(gw.at[piece, low], ya.at[p, k], t_send.at[0, p, k], t_recv.at[0, p, k], me.yn)

    def xb_copy(p, k):
        piece = piece_of(2 * p + c, 3 * (2 * y + 1 - x) + k)
        return remote(gw.at[piece, high], xb.at[p, k], t_send.at[1, p, k], t_recv.at[1, p, k], me.xn)

    def from_sib(p):
        def body(i):
            sib_copy(p, i).wait_recv()
            piece = piece_of(2 * p + c, i)
            add_into(piece, whole, sib[p, i])

        loop(0, 12, body)

        def send(k):
            for n in range(2):
                xa_copy(p, n, k).start()
                yb_copy(p, n, k).start()

        loop(0, 3, send)

    def first_half(p):
        def body(k):
            xa_copy(p, 1 - y, k).wait_recv()
            add_into(piece_of(2 * p + c, 3 * (2 * (1 - y) + x) + k), low, xa[p, 1 - y, k])
            ya_copy(p, k).start()
            yb_copy(p, 1 - x, k).wait_recv()
            add_into(piece_of(2 * p + c, 3 * (2 * y + 1 - x) + k), high, yb[p, 1 - x, k])
            xb_copy(p, k).start()
            own = piece_of(2 * p + c, 3 * q + k)
            xa_copy(p, y, k).wait_recv()
            add_into(own, low, xa[p, y, k])
            yb_copy(p, x, k).wait_recv()
            add_into(own, high, yb[p, x, k])

        loop(0, 3, body)

    def z_copy(p, k, way):
        piece = piece_of(2 * p + c, 3 * q + k)
        return remote(gw.at[piece], (zu, zd)[way].at[p, k], z_send.at[way, p, k], z_recv.at[way, p, k], (me.up, me.down)[way])

    def second_half(p):
        def body(k):
            own = piece_of(2 * p + c, 3 * q + k)
            ya_copy(p, k).wait_recv()
            add_into(own, low, ya[p, k])
            xb_copy(p, k).wait_recv()
            add_into(own, high, xb[p, k])

            @pl.when((z == 0) & (p > 0))
            def _():
                z_copy(p, k, 0).start()

            @pl.when((z == 3) & (p < 3))
            def _():
                z_copy(p, k, 1).start()

        loop(0, 3, body)

    def along_z(p):
        def body(k):
            own = piece_of(2 * p + c, 3 * q + k)

            @pl.when((z > 0) & (z < p))
            def _():
                z_copy(p, k, 0).wait_recv()
                add_into(own, whole, zu[p, k])
                z_copy(p, k, 0).start()

            @pl.when((z < 3) & (z > p))
            def _():
                z_copy(p, k, 1).wait_recv()
                add_into(own, whole, zd[p, k])
                z_copy(p, k, 1).start()

        loop(0, 3, body)

    def share(kind, quarter, k):
        at = 3 * quarter + k
        ref = shard.at[at] if kind < 2 else shard.at[at, (low, high)[kind - 2]]
        to = (me.xn, me.yn, me.xn, me.yn)[kind]
        return remote(ref, ref, g_send.at[kind, k], g_recv.at[kind, k], to)

    def finish(k):
        own = piece_of(2 * z + c, 3 * q + k)

        @pl.when(z > 0)
        def _():
            z_copy(z, k, 0).wait_recv()
            add_into(own, whole, zu[z, k])

        @pl.when(z < 3)
        def _():
            z_copy(z, k, 1).wait_recv()
            add_into(own, whole, zd[z, k])

        shard[3 * q + k] = gw[own]
        share(0, q, k).start()
        share(1, q, k).start()

    same_of = lambda: clip_col[...] == clip_row[...]
    load(7).wait()
    for j in (1, 2, 3, 0):
        put_block(gw, 8 + j, dot_tn(act[j], cot[...]))
        send_block(8 + j)
    col_sums(gv, 7, cot[...].astype(F32))
    load(8).wait()
    load(6).wait()

    def act_step(j):
        act_grad(j, cot, n2, lambda: weight(2 * j), lambda: weight(2 * j + 1), slope, gw, gv, work, low_rows, gn)
        send_block(4 + j)

    act_step(0)
    from_sib(3)
    act_step(1)
    act_step(2)
    act_step(3)
    first_half(3)

    def keep_resid(at, value):
        work[at, :] = value
        low_rows[at, :] = value.astype(BF16)

    load(5).wait()
    norm_back(resid, gn, v_ref[5:6, :], lambda at: cot[at, :].astype(F32), keep_resid, gv, 5)
    from_sib(2)
    second_half(3)
    col_sums(gv, 4, low_rows[...].astype(F32))
    load(3).wait()
    put_block(gw, 3, dot_tn(slabs(att, 0), low_rows[...]))
    send_block(3)
    grad = dot_nt(low_rows[...], weight(8))
    for j in range(6):
        ga[j] = grad[:, LANES * j : LANES * (j + 1)].astype(BF16)
    load(2).wait()
    load(4).wait()
    loop(0, 2, lambda j: attend_back(j, same_of, qkv, lse, ga, gm))
    from_sib(1)
    along_z(3)
    loop(2, 4, lambda j: attend_back(j, same_of, qkv, lse, ga, gm))
    first_half(2)
    loop(4, 6, lambda j: attend_back(j, same_of, qkv, lse, ga, gm))
    load(1).wait()
    for b in range(3):
        mixed = slabs(gm, 6 * b)
        if b != 1:
            col_sums(gv, 2 + b // 2, mixed.astype(F32))
        put_block(gw, b, dot_tn(n1[...], mixed))
        send_block(b)
        part = dot_nt(mixed, weight(9 + b))
        gn[...] = part if b == 0 else gn[...] + part
        if b == 0:
            second_half(2)
            along_z(2)
        if b == 1:
            first_half(1)

    def keep_tokens(at, value):
        tok_out[at, :] = value

    load(0).wait()
    norm_back(emb, gn, v_ref[0:1, :], lambda at: work[at, :], keep_tokens, gv, 0)
    tok_copy = pltpu.make_async_copy(tok_out.at[pl.ds(0, real)], gtok_ref, tok_sem)
    tok_copy.start()
    vsum[0] = gv[...]

    def v_turn(n):
        v_step(n).wait_recv()
        vsum[n + 1] = vsum[n] + vpart[n]
        if n < 4:
            v_step(n + 1).start()

    v_step(0).start()
    from_sib(0)
    second_half(1)
    v_turn(0)
    along_z(1)
    first_half(0)
    v_turn(1)
    second_half(0)
    v_turn(2)
    along_z(0)
    v_turn(3)
    loop(0, 3, finish)

    qx, qy, qd = q + 1 - 2 * x, q + 2 - 4 * y, 3 - q

    def pass_on(k):
        share(0, qx, k).wait_recv()
        share(3, qx, k).start()
        share(1, qy, k).wait_recv()
        share(2, qy, k).start()

    loop(0, 3, pass_on)
    v_turn(4)

    def last(k):
        share(2, qd, k).wait_recv()
        share(3, qd, k).wait_recv()

    loop(0, 3, last)

    norms[0] = jnp.zeros((8, LANES), F32)

    def lay(i, stride, first):
        total = norms[0]
        for j in range(6):
            part = shard[i, :, LANES * j : LANES * (j + 1)].astype(F32)
            flat_ref[pl.ds(first + j, PIECE, stride=stride), :] = part
            total = total + jnp.sum((part * part).reshape(PIECE // 8, 8, LANES), axis=0)
        norms[0] = total

    weave(s, lay)

    @pl.when(s == 7)
    def _():
        total = norms[0]
        for j in range(6):
            part = vsum[5, 0:12, LANES * j : LANES * (j + 1)]
            flat_ref[pl.ds(6912 + j, 12, stride=6), :] = part
            total = total + jnp.concatenate([part[0:8] * part[0:8], jnp.zeros((8, LANES), F32)], axis=0)[0:8]
            total = total + jnp.concatenate([part[8:12] * part[8:12], jnp.zeros((4, LANES), F32)], axis=0)
        norms[0] = total

    edge = remote(flat_ref.at[pl.ds(0, TAIL)], flat_ref.at[pl.ds(6912, TAIL)], e_sem.at[0], e_sem.at[1], me.at(me.dp, (s + 7) % 8))

    @pl.when(s > 0)
    def _():
        edge.start()

    def norm_copy(n):
        return remote(norms.at[0], norms.at[n], n_send.at[n], n_recv.at[n], me.at(me.dp, (s + n) % 8))

    for n in range(1, 8):
        norm_copy(n).start()

    def sent_sib(n):
        sib_copy(n // 12, n % 12).wait_send()

    loop(0, 48, sent_sib)

    def sent_plane(n):
        p, k = n // 3, n % 3
        for m in range(2):
            xa_copy(p, m, k).wait_send()
            yb_copy(p, m, k).wait_send()
        ya_copy(p, k).wait_send()
        xb_copy(p, k).wait_send()

        @pl.when(z < p)
        def _():
            z_copy(p, k, 0).wait_send()

        @pl.when(z > p)
        def _():
            z_copy(p, k, 1).wait_send()

    loop(0, 12, sent_plane)

    def sent_share(k):
        share(0, q, k).wait_send()
        share(1, q, k).wait_send()
        share(2, qy, k).wait_send()
        share(3, qx, k).wait_send()

    loop(0, 3, sent_share)
    for n in range(5):
        v_step(n).wait_send()

    tok_copy.wait()
    total = norms[0]
    for n in range(1, 8):
        norm_copy(n).wait()
        total = total + norms[n]
    norm_ref[...] = total

    @pl.when(s > 0)
    def _():
        edge.wait_send()

    @pl.when(s < 7)
    def _():
        edge.wait_recv()


WEIGHT_ORDER = (8, 4, 9, 5, 10, 6, 11, 7, 3, 0, 1, 2)


def backward(cotangent, clip_col, clip_row, weights, vectors, kept):
    dma = pltpu.SemaphoreType.DMA
    anywhere = pl.BlockSpec(memory_space=pl.ANY)
    return pl.pallas_call(
        backward_kernel,
        name="backward",
        out_shape=[
            jax.ShapeDtypeStruct(cotangent.shape, F32),
            jax.ShapeDtypeStruct((FLAT, LANES), F32),
            jax.ShapeDtypeStruct((8, LANES), F32),
        ],
        in_specs=[VM, VM, VM, anywhere, VM] + [anywhere] * 9,
        out_specs=[anywhere, VM, VM],
        scratch_shapes=[pltpu.VMEM(*k) for k in kept_shapes()]
        + [
            pltpu.VMEM((ROWS, D), BF16),
            pltpu.VMEM((ROWS, D), F32),
            pltpu.VMEM((ROWS, D), BF16),
            pltpu.VMEM((ROWS, D), F32),
            pltpu.VMEM((6, ROWS, LANES), BF16),
            pltpu.VMEM((18, ROWS, LANES), BF16),
            pltpu.VMEM((16, D), F32),
            pltpu.VMEM((3, 8, PIECE, D), BF16),
            pltpu.VMEM((ROWS, D), F32),
            pltpu.VMEM((96, PIECE, D), BF16),
            pltpu.VMEM((4, 12, PIECE, D), BF16),
            pltpu.VMEM((4, 2, 3, HALF, D), BF16),
            pltpu.VMEM((4, 3, HALF, D), BF16),
            pltpu.VMEM((4, 2, 3, HALF, D), BF16),
            pltpu.VMEM((4, 3, HALF, D), BF16),
            pltpu.VMEM((4, 3, PIECE, D), BF16),
            pltpu.VMEM((4, 3, PIECE, D), BF16),
            pltpu.VMEM((12, PIECE, D), BF16),
            pltpu.VMEM((6, 16, D), F32),
            pltpu.VMEM((5, 16, D), F32),
            pltpu.VMEM((8, 8, LANES), F32),
            dma((9,)),
            dma((3,)),
            dma,
            dma((4, 12)),
            dma((4, 12)),
            dma((2, 4, 2, 3)),
            dma((2, 4, 2, 3)),
            dma((2, 4, 3)),
            dma((2, 4, 3)),
            dma((2, 4, 3)),
            dma((2, 4, 3)),
            dma((4, 3)),
            dma((4, 3)),
            dma((5,)),
            dma((5,)),
            dma((2,)),
            dma((8,)),
            dma((8,)),
        ],
        compiler_params=pltpu.CompilerParams(collective_id=1, has_side_effects=True, vmem_limit_bytes=LIMIT),
    )(cotangent, clip_col, clip_row, weights, vectors, *kept)


STEP_ROWS = 1024


def update_kernel(flat_ref, norm_ref, param_ref, first_ref, second_ref, grad_out, change_out, first_out, second_out):
    s = lax.axis_index("fsdp")
    n = pl.program_id(0)
    rows = param_ref.shape[0]
    grad = flat_ref[pl.ds(n * rows + 9 * s, rows), :]
    squares = jnp.sum(jnp.sum(norm_ref[...], axis=0, keepdims=True), axis=1, keepdims=True)
    factor = jnp.minimum(1.0, 1.0 / (jnp.sqrt(squares) + 1e-06))
    clipped = grad * factor
    new_first = 0.9 * first_ref[...] + 0.1 * clipped
    new_second = 0.999 * second_ref[...] + 0.001 * clipped * clipped
    first_hat = new_first * (1.0 / first_correct)
    second_hat = new_second * (1.0 / second_correct)
    row = s * 6921 + n * rows + lax.broadcasted_iota(jnp.int32, (rows, LANES), 0)
    decay = jnp.where(row < MATS // LANES, 0.05, 0.0)
    step_rate = 0.001 * 0.75**6
    grad_out[...] = grad
    first_out[...] = new_first
    second_out[...] = new_second
    change_out[...] = step_rate * (first_hat / (jnp.sqrt(second_hat) + 1e-08) + decay * param_ref[...])


def update(flat, norm, params, first, second):
    rows = params.shape[0]
    spec = pl.BlockSpec((STEP_ROWS, LANES), lambda n: (n, 0))
    return pl.pallas_call(
        update_kernel,
        name="update",
        grid=(pl.cdiv(rows, STEP_ROWS),),
        out_shape=[jax.ShapeDtypeStruct((rows, LANES), F32)] * 4,
        in_specs=[VM, VM, spec, spec, spec],
        out_specs=[spec] * 4,
        compiler_params=pltpu.CompilerParams(vmem_limit_bytes=LIMIT),
    )(flat, norm, params, first, second)


def shards(tokens, cotangent, keep_index, clip_ids, flat_params, first_moment, second_moment):
    flat = flat_params.reshape(-1, LANES)
    weights, vectors = gather(flat)
    pad = ROWS - tokens.shape[0]
    keep = jnp.pad(keep_index.reshape(-1, 1), ((0, pad), (0, 0)))
    clip = jnp.pad(jnp.repeat(clip_ids.reshape(-1), KEEP), (0, pad), constant_values=-1)
    clip_col, clip_row = clip[:, None], clip[None, :]
    layer_out, *kept = forward(tokens, keep, clip_col, clip_row, weights, vectors)
    grad_tokens, summed, norm = backward(cotangent, clip_col, clip_row, weights, vectors, kept)
    outs = update(summed, norm, flat, first_moment.reshape(-1, LANES), second_moment.reshape(-1, LANES))
    grad, change, first, second = (o.reshape(-1) for o in outs)
    return (layer_out, grad_tokens, grad, change, first, second)


def layer_norm(values, gain_vec, shift_vec):
    row_mean = jnp.mean(values, axis=-1, keepdims=True)
    centered = values - row_mean
    variance = jnp.mean(centered * centered, axis=-1, keepdims=True)
    return centered * lax.rsqrt(variance + 1e-06) * gain_vec + shift_vec


def gelu_exact(values):
    return jax.nn.gelu(values, approximate=False)


def positions(keep_flat):
    quarter = D // 4
    frequency = 1.0 / 10000.0 ** (jnp.arange(quarter).astype(jnp.float32) / quarter)
    row_angle = (keep_flat // GRID).astype(jnp.float32)[:, None] * frequency
    col_angle = (keep_flat % GRID).astype(jnp.float32)[:, None] * frequency
    return jnp.concatenate(
        [jnp.sin(row_angle), jnp.cos(row_angle), jnp.sin(col_angle), jnp.cos(col_angle)], axis=1
    )


def unpack_flat(flat):
    mats = 4 * D * D + 2 * D * FF
    w_qkv = flat[: 3 * D * D].reshape(D, 3 * D)
    w_out = flat[3 * D * D : 4 * D * D].reshape(D, D)
    w_up = flat[4 * D * D : 4 * D * D + D * FF].reshape(D, FF)
    w_down = flat[4 * D * D + D * FF : mats].reshape(FF, D)
    vectors = flat[mats : mats + 8 * D].reshape(8, D)
    bias_up = flat[mats + 8 * D :]
    return (w_qkv, w_out, w_up, w_down, vectors, bias_up)


def split_heads(values):
    return values.reshape(values.shape[0], HEADS, HEAD_DIM).transpose(1, 0, 2)


def join_heads(values):
    return values.transpose(1, 0, 2).reshape(values.shape[1], D)


def product(left, right):
    return jnp.dot(left, right, preferred_element_type=jnp.float32)


def plain_shards(tokens, cotangent, keep_index, clip_ids, flat_params, first_moment, second_moment):
    shard_len = flat_params.shape[0]
    mats = 4 * D * D + 2 * D * FF
    score_scale = HEAD_DIM ** (-0.5)
    sent = flat_params.astype(jnp.bfloat16)
    gathered = lax.all_gather(sent, "fsdp", axis=0, tiled=True)
    w_qkv, w_out, w_up, w_down, vectors_low, bias_up_low = unpack_flat(gathered)
    vectors = vectors_low.astype(jnp.float32)
    bias_up = bias_up_low.astype(jnp.float32)
    embedded = tokens.astype(jnp.float32) + positions(keep_index.reshape(-1))
    normed, norm_back = jax.vjp(layer_norm, embedded, vectors[0], vectors[1])
    normed_low = normed.astype(jnp.bfloat16)
    mixed_qkv = product(normed_low, w_qkv)
    query_low = (mixed_qkv[:, :D] + vectors[2]).astype(jnp.bfloat16)
    key_low = mixed_qkv[:, D : 2 * D].astype(jnp.bfloat16)
    value_low = (mixed_qkv[:, 2 * D :] + vectors[3]).astype(jnp.bfloat16)
    query_heads = split_heads(query_low)
    key_heads = split_heads(key_low)
    value_heads = split_heads(value_low)
    clip_tok = jnp.repeat(clip_ids.reshape(-1), KEEP)
    same_clip = clip_tok[:, None] == clip_tok[None, :]

    def attend(head_item):
        q_head, k_head, v_head = head_item
        scores = jnp.where(same_clip, product(q_head, k_head.T) * score_scale, -1e30)
        row_top = jnp.max(scores, axis=1, keepdims=True)
        weight_exp = jnp.exp(scores - row_top)
        row_total = jnp.sum(weight_exp, axis=1, keepdims=True)
        soft_low = (weight_exp / row_total).astype(jnp.bfloat16)
        return (product(soft_low, v_head), row_top + jnp.log(row_total))

    attended_heads, log_total = lax.map(attend, (query_heads, key_heads, value_heads))
    attended_low = join_heads(attended_heads).astype(jnp.bfloat16)
    resid = embedded + product(attended_low, w_out) + vectors[4]
    normed_two, norm_two_back = jax.vjp(layer_norm, resid, vectors[5], vectors[6])
    normed_two_low = normed_two.astype(jnp.bfloat16)
    pre_act = product(normed_two_low, w_up) + bias_up
    activated, gelu_back = jax.vjp(gelu_exact, pre_act)
    activated_low = activated.astype(jnp.bfloat16)
    layer_out = (resid + product(activated_low, w_down) + vectors[7]).astype(jnp.bfloat16)
    w_qkv, w_out, w_up, w_down, vectors_low, bias_up_low = unpack_flat(
        lax.all_gather(sent, "fsdp", axis=0, tiled=True)
    )
    grad_out = cotangent.astype(jnp.float32)
    grad_w_down = product(activated_low.T, cotangent)
    grad_bias_down = jnp.sum(grad_out, axis=0)
    grad_act = product(cotangent, w_down.T)
    grad_pre_low = gelu_back(grad_act)[0].astype(jnp.bfloat16)
    grad_w_up = product(normed_two_low.T, grad_pre_low)
    grad_bias_up = jnp.sum(grad_pre_low.astype(jnp.float32), axis=0)
    grad_normed_two = product(grad_pre_low, w_up.T)
    grad_resid_norm, grad_gain_two, grad_shift_two = norm_two_back(grad_normed_two)
    grad_resid = grad_out + grad_resid_norm
    grad_branch_low = grad_resid.astype(jnp.bfloat16)
    grad_w_out = product(attended_low.T, grad_branch_low)
    grad_bias_out = jnp.sum(grad_branch_low.astype(jnp.float32), axis=0)
    grad_attended_low = product(grad_branch_low, w_out.T).astype(jnp.bfloat16)

    def attend_back(head_item):
        q_head, k_head, v_head, g_head, lse_head = head_item
        soft = jnp.where(
            same_clip, jnp.exp(product(q_head, k_head.T) * score_scale - lse_head), 0.0
        )
        grad_soft = product(g_head, v_head.T)
        grad_value = product(soft.astype(jnp.bfloat16).T, g_head)
        inner = jnp.sum(soft * grad_soft, axis=1, keepdims=True)
        grad_raw = (score_scale * soft * (grad_soft - inner)).astype(jnp.bfloat16)
        return (product(grad_raw, k_head), product(grad_raw.T, q_head), grad_value)

    grad_query, grad_key, grad_value = lax.map(
        attend_back,
        (query_heads, key_heads, value_heads, split_heads(grad_attended_low), log_total),
    )
    grad_mixed = jnp.concatenate(
        [join_heads(grad_query), join_heads(grad_key), join_heads(grad_value)], axis=1
    ).astype(jnp.bfloat16)
    grad_w_qkv = product(normed_low.T, grad_mixed)
    mixed_sums = jnp.sum(grad_mixed.astype(jnp.float32), axis=0)
    grad_normed = product(grad_mixed, w_qkv.T)
    grad_embedded, grad_gain_one, grad_shift_one = norm_back(grad_normed)
    grad_tokens = grad_resid + grad_embedded
    full_grad = jnp.concatenate(
        [
            grad_w_qkv.reshape(-1),
            grad_w_out.reshape(-1),
            grad_w_up.reshape(-1),
            grad_w_down.reshape(-1),
            grad_gain_one,
            grad_shift_one,
            mixed_sums[:D],
            mixed_sums[2 * D :],
            grad_bias_out,
            grad_gain_two,
            grad_shift_two,
            grad_bias_down,
            grad_bias_up,
        ]
    )
    replicas = lax.axis_size("dp")
    owners = lax.axis_size("fsdp")
    reordered = full_grad.reshape(owners, replicas, -1).transpose(1, 0, 2).reshape(-1)
    own_piece = lax.psum_scatter(reordered, ("dp", "fsdp"), scatter_dimension=0, tiled=True)
    own_grad = lax.all_gather(own_piece.astype(jnp.bfloat16), "dp", axis=0, tiled=True).astype(
        own_piece.dtype
    )
    squares = lax.psum(jnp.sum(own_grad * own_grad), "fsdp")
    clip_factor = jnp.minimum(1.0, 1.0 / (jnp.sqrt(squares) + 1e-06))
    clipped = own_grad * clip_factor
    new_first = 0.9 * first_moment + 0.1 * clipped
    new_second = 0.999 * second_moment + 0.001 * clipped * clipped
    first_hat = new_first / first_correct
    second_hat = new_second / second_correct
    position = lax.axis_index("fsdp") * shard_len + jnp.arange(shard_len, dtype=jnp.int32)
    decay_mask = (position < mats).astype(jnp.float32)
    step_rate = 0.001 * 0.75**6
    param_change = step_rate * (
        first_hat / (jnp.sqrt(second_hat) + 1e-08) + 0.05 * decay_mask * flat_params
    )
    return (layer_out, grad_tokens, own_grad, param_change, new_first, new_second)


def solution(mesh):
    placed = (
        P(("dp", "fsdp"), None),
        P(("dp", "fsdp"), None),
        P(("dp", "fsdp"), None),
        P(("dp", "fsdp"), None),
        P("fsdp"),
        P("fsdp"),
        P("fsdp"),
    )
    staged = mesh.shape["dp"] == 4 and mesh.shape["fsdp"] == 8
    return jax.shard_map(
        shards if staged else plain_shards,
        mesh=mesh,
        in_specs=placed,
        out_specs=(
            P(("dp", "fsdp"), None),
            P(("dp", "fsdp"), None),
            P("fsdp"),
            P("fsdp"),
            P("fsdp"),
            P("fsdp"),
        ),
        check_vma=False,
    )
```

```python
import functools

import jax
import jax.numpy as jnp
import numpy as np
from jax import lax
from jax.experimental import pallas as pl
from jax.experimental.pallas import tpu as pltpu
from jax.sharding import PartitionSpec as P

D = 768
FF = 3072
HEADS = 12
HEAD_DIM = 64
GRID = 14
KEEP = 49
MATS = 4 * D * D + 2 * D * FF

first_correct = 0.9999734386011124
second_correct = 0.09520785288629106

F32 = jnp.float32
BF16 = jnp.bfloat16
MESH = pl.DeviceIdType.MESH
LIMIT = 66_000_000

ROWS = 400
CHUNK = 80
PIECE = 96
PIECES = 12
LANES = 128
TAIL = 72


def ge(s, k):
    return (s + 8 - k) // 8


def piece_of(s, i):
    g5 = (i + 4) // 8
    forms = (
        8 * (i // 4) + i % 4,
        8 * (i // 4) + 4 + i % 4,
        24 + i + (i // 8) * (7 * i - 56),
        33 + 8 * (i // 3) + i % 3,
        36 + 8 * (i // 3) + i % 3,
        (1 - g5) * (39 + 8 * i) + g5 * (60 + i),
        72 + i,
        84 + i,
    )
    out = 0
    for k, form in enumerate(forms):
        out = out + (ge(s, k) - ge(s, k + 1)) * form
    return out


def grad_piece(s, i):
    return piece_of(s, i) + 24 * ge(s, 6)


def grad_block(b):
    return 8 * b + 24 * ((b + 7) // 16)


ARRIVALS = (
    ((1, 0), (1, 1), (1, 2), (2, 0), (2, 1), (2, 2), (3, 0), (3, 1), (3, 2)),
    ((0, 0), (0, 1), (0, 2), (2, 0), (2, 1), (2, 2), (3, 0), (3, 1), (3, 2)),
    ((3, 0), (1, 0), (0, 0), (0, 1), (0, 2), (1, 1), (1, 2), (3, 1), (3, 2)),
    ((2, 0), (1, 0), (0, 0), (0, 1), (0, 2), (1, 1), (1, 2), (2, 1), (2, 2)),
)


def arrival(z, n):
    out = []
    for m in range(2):
        row = [ARRIVALS[plane][n][m] for plane in range(4)]
        value = row[0]
        for plane in range(1, 4):
            value = value + (row[plane] - row[plane - 1]) * ((z + 4 - plane) // 4)
        out.append(value)
    return out


def dot(a, b):
    return lax.dot_general(a, b, (((1,), (0,)), ((), ())), preferred_element_type=F32)


def dot_nt(a, b):
    return lax.dot_general(a, b, (((1,), (1,)), ((), ())), preferred_element_type=F32)


def dot_tn(a, b):
    return lax.dot_general(a, b, (((0,), (0,)), ((), ())), preferred_element_type=F32)


def loop(start, stop, body):
    def step(i, carry):
        body(i)
        return carry

    lax.fori_loop(start, stop, step, 0)


def chunks(body):
    loop(0, ROWS // CHUNK, lambda n: body(pl.ds(pl.multiple_of(n * CHUNK, CHUNK), CHUNK)))


class Place:
    def __init__(self):
        self.dp = lax.axis_index("dp")
        self.s = lax.axis_index("fsdp")
        self.x, self.y = self.dp % 2, self.dp // 2
        self.z, self.c = self.s // 2, self.s % 2
        self.sib = self.at(self.dp, self.s + 1 - 2 * self.c)
        self.xn = self.at(self.dp + 1 - 2 * self.x, self.s)
        self.yn = self.at(self.dp + 2 - 4 * self.y, self.s)
        self.up = self.at(self.dp, self.s + 2)
        self.down = self.at(self.dp, self.s - 2)

    def at(self, dp, s):
        return (dp, s)

    def barrier(self):
        sem = pltpu.get_barrier_semaphore()
        for n in range(1, 8):
            pl.semaphore_signal(sem, inc=1, device_id=self.at(self.dp, (self.s + n) % 8), device_id_type=MESH)
        for peer in (self.xn, self.yn):
            pl.semaphore_signal(sem, inc=1, device_id=peer, device_id_type=MESH)
        pl.semaphore_wait(sem, 9)


def remote(src, dst, send, recv, to):
    return pltpu.make_async_remote_copy(
        src_ref=src, dst_ref=dst, send_sem=send, recv_sem=recv, device_id=to, device_id_type=MESH
    )


def weave(s, body):
    @pl.when(s <= 1)
    def _():
        loop(0, 12, lambda i: body(i, 18, (i % 4) * (96 * 18) + (i // 4) * 6))

    @pl.when(s == 2)
    def _():
        loop(0, 8, lambda i: body(i, 6, i * (96 * 6)))
        loop(8, 12, lambda i: body(i, 24, 4608 + (i - 8) * 6))

    @pl.when((s == 3) | (s == 4))
    def _():
        loop(0, 12, lambda i: body(i, 24, (i % 3) * (96 * 24) + (i // 3) * 6))

    @pl.when(s == 5)
    def _():
        loop(0, 4, lambda i: body(i, 24, i * 6))
        loop(4, 12, lambda i: body(i, 6, 2304 + (i - 4) * (96 * 6)))

    @pl.when(s >= 6)
    def _():
        loop(0, 12, lambda i: body(i, 6, i * (96 * 6)))


def position_table():
    quarter = D // 4
    exponent = np.arange(quarter, dtype=np.float32) / np.float32(quarter)
    frequency = np.float32(1.0) / np.power(np.float32(10000.0), exponent).astype(np.float32)
    angle = (np.arange(GRID, dtype=np.float32)[:, None] * frequency).astype(np.float64)
    waves = np.concatenate([np.sin(angle), np.cos(angle)], axis=1).astype(np.float32)
    table = np.zeros((32, D), np.float32)
    table[:GRID, : D // 2] = waves
    table[16 : 16 + GRID, D // 2 :] = waves
    parts = []
    for _ in range(3):
        part = table.astype(jnp.bfloat16)
        parts.append(part)
        table = table - part.astype(np.float32)
    return np.stack(parts)


def norm_stats(v):
    mean = jnp.mean(v, axis=-1, keepdims=True)
    centered = v - mean
    rstd = lax.rsqrt(jnp.mean(centered * centered, axis=-1, keepdims=True) + 1e-06)
    return centered * rstd, rstd


def block(g_ref, b):
    return g_ref[pl.ds(8 * b, 8)].reshape(D, D)


def slabs(ref, first):
    return jnp.concatenate([ref[first + j] for j in range(6)], axis=1)


def embed(tok_ref, keep_ref, table_ref, emb):
    real = tok_ref.shape[0]
    emb[0:real, :] = tok_ref[...].astype(F32)
    emb[real:, :] = jnp.zeros((ROWS - real, D), F32)

    def body(at):
        keep = keep_ref[at, :]
        row = (keep * 4682) >> 16
        col = keep - GRID * row + 16
        lane = lax.broadcasted_iota(jnp.int32, (CHUNK, 32), 1)
        hot = jnp.where((lane == row) | (lane == col), 1.0, 0.0).astype(BF16)
        spot = dot(hot, table_ref[0]) + (dot(hot, table_ref[1]) + dot(hot, table_ref[2]))
        emb[at, :] = emb[at, :] + spot

    chunks(body)


def norm_one(emb, v_ref, n1):
    gain, shift = v_ref[0:1, :], v_ref[1:2, :]

    def body(at):
        n1[at, :] = (norm_stats(emb[at, :])[0] * gain + shift).astype(BF16)

    chunks(body)


def project(b, n1, g_ref, v_ref, qkv):
    mixed = dot(n1[...], block(g_ref, b)) + v_ref[pl.ds(2 + b // 2, 1), :] * jnp.where(b == 1, 0.0, 1.0)
    for j in range(6):
        qkv[6 * b + j] = mixed[:, LANES * j : LANES * (j + 1)].astype(BF16)


def attend(j, same_of, qkv, att, lse):
    query, key, value = qkv[j], qkv[6 + j], qkv[12 + j]
    first = lax.broadcasted_iota(jnp.int32, (ROWS, LANES), 1) < HEAD_DIM
    turned = value.T
    parts = []
    for h in range(2):
        own = jnp.where(first if h == 0 else ~first, query, jnp.zeros_like(query))
        scores = jnp.where(same_of(), dot_nt(key, own) * 0.125, -1e30)
        top = jnp.max(scores, axis=0, keepdims=True)
        weight = jnp.exp(scores - top)
        total = jnp.sum(weight, axis=0, keepdims=True)
        soft = (weight * (1.0 / total)).astype(BF16)
        lse[2 * j + h] = top + jnp.log(total)
        parts.append(dot(turned[HEAD_DIM * h : HEAD_DIM * (h + 1), :], soft))
    att[j] = jnp.concatenate(parts, axis=0).T.astype(BF16)


def out_project(att, g_ref, v_ref, emb, resid, n2):
    resid[...] = dot(slabs(att, 0), block(g_ref, 3))
    bias, gain, shift = v_ref[4:5, :], v_ref[5:6, :], v_ref[6:7, :]

    def body(at):
        value = emb[at, :] + resid[at, :] + bias
        resid[at, :] = value
        n2[at, :] = (norm_stats(value)[0] * gain + shift).astype(BF16)

    chunks(body)


def expand(j, n2, g_ref, v_ref, work, act, slope):
    work[...] = dot(n2[...], block(g_ref, 4 + j))

    def body(at):
        pre = work[at, :] + v_ref[pl.ds(8 + j, 1), :]
        phi = 0.5 * (1.0 + lax.erf(pre * 0.7071067811865476))
        act[j, at, :] = (pre * phi).astype(BF16)
        slope[j, at, :] = (phi + pre * (0.3989422804014327 * jnp.exp(-0.5 * pre * pre))).astype(BF16)

    chunks(body)


def contract(j, act, g_ref, work):
    add_part(j, work, dot(act[j], block(g_ref, 8 + j)))


def kept_shapes():
    return [
        ((ROWS, D), F32),
        ((ROWS, D), BF16),
        ((18, ROWS, LANES), BF16),
        ((6, ROWS, LANES), BF16),
        ((HEADS, 1, ROWS), F32),
        ((ROWS, D), F32),
        ((ROWS, D), BF16),
        ((4, ROWS, D), BF16),
        ((4, ROWS, D), BF16),
    ]


VM = pl.BlockSpec(memory_space=pltpu.VMEM)


def col_sums(dest, row, source):
    dest[row : row + 1, :] = jnp.sum(source, axis=0, keepdims=True)


def put_block(gw, b, value):
    gw[pl.ds(grad_block(b), 8)] = value.astype(BF16).reshape(8, PIECE, D)


def act_grad(j, cot, g_ref, slope, gv, work, pre_low, gn):
    work[...] = dot_nt(cot[...], block(g_ref, 8 + j))
    total = jnp.zeros((8, D), F32)

    def body(n, total):
        at = pl.ds(pl.multiple_of(n * CHUNK, CHUNK), CHUNK)
        low = (slope[j, at, :].astype(F32) * work[at, :]).astype(BF16)
        pre_low[at, :] = low
        return total + jnp.sum(low.astype(F32).reshape(CHUNK // 8, 8, D), axis=0)

    total = lax.fori_loop(0, ROWS // CHUNK, body, total)
    gv[pl.ds(8 + j, 1), :] = jnp.sum(total, axis=0, keepdims=True)
    add_part(j, gn, dot_nt(pre_low[...], block(g_ref, 4 + j)))


def add_part(j, total, part):
    @pl.when(j == 0)
    def _():
        total[...] = part

    @pl.when(j > 0)
    def _():
        total[...] += part


def norm_back(value_ref, gn, gain, extra, store, gv, row):
    def body(n, sums):
        at = pl.ds(pl.multiple_of(n * CHUNK, CHUNK), CHUNK)
        hat, rstd = norm_stats(value_ref[at, :])
        grad = gn[at, :]
        fold = lambda v: jnp.sum(v.reshape(CHUNK // 8, 8, D), axis=0)
        sums = (sums[0] + fold(grad * hat), sums[1] + fold(grad))
        grad = grad * gain
        inner = jnp.mean(grad * hat, axis=-1, keepdims=True)
        store(at, extra(at) + rstd * (grad - jnp.mean(grad, axis=-1, keepdims=True) - hat * inner))
        return sums

    zero = jnp.zeros((8, D), F32)
    one, two = lax.fori_loop(0, ROWS // CHUNK, body, (zero, zero))
    gv[row : row + 1, :] = jnp.sum(one, axis=0, keepdims=True)
    gv[row + 1 : row + 2, :] = jnp.sum(two, axis=0, keepdims=True)


def attend_back(j, same_of, qkv, lse, ga, gm):
    query, key, value, grad = qkv[j], qkv[6 + j], qkv[12 + j], ga[j]
    first = lax.broadcasted_iota(jnp.int32, (ROWS, LANES), 1) < HEAD_DIM
    turned = key.T
    parts, grad_key, grad_value = [], None, None
    for h in range(2):
        mine = first if h == 0 else ~first
        own = jnp.where(mine, query, jnp.zeros_like(query))
        own_grad = jnp.where(mine, grad, jnp.zeros_like(grad))
        soft = jnp.where(same_of(), jnp.exp(dot_nt(key, own) * 0.125 - lse[2 * j + h]), 0.0)
        grad_soft = dot_nt(value, own_grad)
        inner = jnp.sum(soft * grad_soft, axis=0, keepdims=True)
        raw = (0.125 * soft * (grad_soft - inner)).astype(BF16)
        one = dot(soft.astype(BF16), own_grad)
        two = dot(raw, own)
        grad_value = one if h == 0 else grad_value + one
        grad_key = two if h == 0 else grad_key + two
        parts.append(dot(turned[HEAD_DIM * h : HEAD_DIM * (h + 1), :], raw))
    gm[j] = jnp.concatenate(parts, axis=0).T.astype(BF16)
    gm[6 + j] = grad_key.astype(BF16)
    gm[12 + j] = grad_value.astype(BF16)


FLAT = 7240
HALF = PIECE // 2


def step_kernel(own_hbm, tok_ref, keep_ref, clip_col, clip_row, table_ref, cot_ref, *refs):
    out_ref, gtok_ref, flat_ref, norm_ref = refs[:4]
    emb, n1, qkv, att, lse, resid, n2, act, slope = refs[4:13]
    (
        cot, work, low_rows, gn, ga, gm, gv, g, v_ref, tail, vbuf,
        sib, xa, ya, yb, xb, zu, zd, shard, vsum, vpart, norms,
        own_sem, edge_sem, gv_send, gv_recv, gz_send, gz_recv, gp_send, gp_recv, gc_send, gc_recv, tok_sem,
        sib_send, sib_recv, h_send, h_recv, t_send, t_recv, z_send, z_recv, g_send, g_recv, v_send, v_recv, e_sem, n_send, n_recv,
    ) = refs[13:]
    me = Place()
    s, z, c, x, y = me.s, me.z, me.c, me.x, me.y
    q = me.dp
    qx, qy, qd = q + 1 - 2 * x, q + 2 - 4 * y, 3 - q
    rows = own_hbm.shape[0]
    real = cot_ref.shape[0]

    own_copy = pltpu.make_async_copy(own_hbm, flat_ref.at[pl.ds(TAIL, rows)], own_sem)
    own_copy.start()
    gv[...] = jnp.zeros_like(gv)
    cot[...] = jnp.concatenate([cot_ref[...].astype(F32), jnp.zeros((ROWS - real, D), F32)], axis=0).astype(BF16)
    me.barrier()
    own_copy.wait()
    tail[...] = flat_ref[rows : rows + TAIL, :]
    edge = remote(tail, flat_ref.at[pl.ds(0, TAIL)], edge_sem.at[0], edge_sem.at[1], me.at(me.dp, (s + 1) % 8))

    @pl.when(s < 7)
    def _():
        edge.start()

    @pl.when(s == 7)
    def _():
        for n in range(7):
            remote(tail, vbuf, gv_send.at[n], gv_recv, me.at(me.dp, n)).start()
        vbuf[...] = tail[...]

    embed(tok_ref, keep_ref, table_ref, emb)

    @pl.when(s > 0)
    def _():
        edge.wait_recv()

    def to_sib(p, i):
        piece = piece_of(2 * p + c, i)
        return remote(g.at[piece], g.at[piece], gc_send.at[p, i], gc_recv.at[p, i], me.sib)

    def line_copy(p, k, way):
        piece = piece_of(2 * p + c, q + 4 * k)
        return remote(g.at[piece], g.at[piece], gz_send.at[way, p, k], gz_recv.at[p, k], (me.up, me.down)[way])

    def plane_copy(kind, p, quarter, k):
        piece = piece_of(2 * p + c, quarter + 4 * k)
        ref = g.at[piece]
        if kind >= 2:
            ref = g.at[piece, pl.ds(HALF * (kind - 2), HALF)]
        return remote(ref, ref, gp_send.at[kind, p, k], gp_recv.at[kind, p, k], (me.xn, me.yn)[kind % 2])

    def place_piece(i, stride, first):
        piece = piece_of(s, i)
        for j in range(6):
            g[piece, :, LANES * j : LANES * (j + 1)] = flat_ref[pl.ds(TAIL - 9 * s + first + j, PIECE, stride=stride), :].astype(BF16)

    weave(s, place_piece)
    flat_ref[6912:, :] = jnp.zeros((FLAT - 6912, LANES), F32)

    def own_up(k):
        line_copy(z, k, 0).start()

    @pl.when(z < 3)
    def _():
        own_up(0)

    @pl.when(z > 0)
    def _():
        loop(0, 3, lambda k: line_copy(z, k, 1).start())

    @pl.when(z == 0)
    def _():
        loop(1, 3, own_up)

    loop(0, 12, lambda i: to_sib(z, i).start())

    @pl.when(s < 7)
    def _():
        remote(tail, vbuf, gv_send.at[0], gv_recv, me.sib).wait_recv()

    for j in range(6):
        v_ref[0:12, LANES * j : LANES * (j + 1)] = vbuf[pl.ds(j, 12, stride=6), :].astype(BF16).astype(F32)

    def line_step(n):
        p, k = arrival(z, n)

        @pl.when(p < z)
        def _():
            line_copy(p, k, 0).wait_recv()

            @pl.when(z < 3)
            def _():
                line_copy(p, k, 0).start()

        @pl.when(p > z)
        def _():
            line_copy(p, k, 1).wait_recv()

            @pl.when(z > 0)
            def _():
                line_copy(p, k, 1).start()

        plane_copy(0, p, q, k).start()
        plane_copy(1, p, q, k).start()
        to_sib(p, q + 4 * k).start()
        if n in (2, 6):

            @pl.when(z == (1 if n == 2 else 2))
            def _():
                loop(1, 3, own_up)

    def plane_step(n):
        p, k = arrival(z, n)
        plane_copy(0, p, qx, k).wait_recv()
        plane_copy(3, p, qx, k).start()
        to_sib(p, qx + 4 * k).start()
        plane_copy(1, p, qy, k).wait_recv()
        plane_copy(2, p, qy, k).start()
        to_sib(p, qy + 4 * k).start()

    def far_step(n):
        p, k = arrival(z, n)
        plane_copy(2, p, qd, k).wait_recv()
        plane_copy(3, p, qd, k).wait_recv()
        to_sib(p, qd + 4 * k).start()

    def have(p, k):
        for quarter in range(4):
            to_sib(p, quarter + 4 * k).wait_recv()

    same_of = lambda: clip_col[...] == clip_row[...]
    norm_one(emb, v_ref, n1)
    line_step(0)
    line_step(1)
    plane_step(0)
    line_step(2)
    plane_step(1)
    line_step(3)
    far_step(0)
    line_step(4)
    plane_step(2)
    far_step(1)
    line_step(5)
    plane_step(3)
    line_step(6)
    far_step(2)

    def qkv_step(b):
        @pl.when(b == 1)
        def _():
            line_step(7)
            plane_step(4)
            far_step(3)

        @pl.when(b == 2)
        def _():
            line_step(8)
            plane_step(5)
            far_step(4)

        have(0, b)
        project(b, n1, g, v_ref, qkv)

    loop(0, 3, qkv_step)

    def attend_step(j):
        @pl.when(j == 1)
        def _():
            plane_step(6)
            far_step(5)

        @pl.when(j == 3)
        def _():
            plane_step(7)
            far_step(6)

        @pl.when(j == 5)
        def _():
            plane_step(8)
            far_step(7)

        attend(j, same_of, qkv, att, lse)

    loop(0, 6, attend_step)
    have(1, 0)
    have(1, 1)
    out_project(att, g, v_ref, emb, resid, n2)
    have(1, 2)

    def expand_step(j):
        @pl.when(j == 2)
        def _():
            far_step(8)

        @pl.when(j < 3)
        def _():
            have(2, j)

        expand(j, n2, g, v_ref, work, act, slope)

    loop(0, 4, expand_step)
    for k in range(3):
        have(3, k)
    loop(0, 4, lambda j: contract(j, act, g, work))
    out_ref[...] = (resid[0:real, :] + work[0:real, :] + v_ref[7:8, :]).astype(BF16)

    @pl.when(s < 7)
    def _():
        edge.wait_send()

    @pl.when(s == 7)
    def _():
        for n in range(7):
            remote(tail, vbuf, gv_send.at[n], gv_recv, me.sib).wait_send()

    def line_sent(p, k):
        @pl.when((p <= z) & (z < 3))
        def _():
            line_copy(p, k, 0).wait_send()

        @pl.when((p >= z) & (z > 0))
        def _():
            line_copy(p, k, 1).wait_send()

        @pl.when(p != z)
        def _():
            plane_copy(0, p, q, k).wait_send()
            plane_copy(1, p, q, k).wait_send()
            plane_copy(2, p, qy, k).wait_send()
            plane_copy(3, p, qx, k).wait_send()

    loop(0, 12, lambda n: line_sent(n // 3, n % 3))
    loop(0, 48, lambda n: to_sib(n // 12, n % 12).wait_send())

    def add_into(piece, rows, got):
        g[piece, rows, :] = (g[piece, rows, :].astype(F32) + got.astype(F32)).astype(BF16)

    low, high, whole = pl.ds(0, HALF), pl.ds(HALF, HALF), pl.ds(0, PIECE)

    def sib_copy(p, i):
        piece = grad_piece(2 * p + 1 - c, i)
        return remote(g.at[piece], sib.at[p, i], sib_send.at[p, i], sib_recv.at[p, i], me.sib)

    def send_span(parity, p, first, count):
        @pl.when(c == 1 - parity)
        def _():
            loop(0, count, lambda r: sib_copy(p, first + r).start())

    partners = (me.sib, me.xn, me.yn, me.at(me.dp, (s + 2 - 4 * (z % 2)) % 8), me.at(me.dp, (s + 4) % 8))

    def v_step(n):
        copy = remote(vsum.at[n], vpart.at[n], v_send.at[n], v_recv.at[n], partners[n])
        return copy

    def xa_copy(p, yy, k):
        piece = grad_piece(2 * p + c, 3 * (2 * yy + 1 - x) + k)
        return remote(g.at[piece, low], xa.at[p, yy, k], h_send.at[0, p, yy, k], h_recv.at[0, p, yy, k], me.xn)

    def yb_copy(p, xx, k):
        piece = grad_piece(2 * p + c, 3 * (2 * (1 - y) + xx) + k)
        return remote(g.at[piece, high], yb.at[p, xx, k], h_send.at[1, p, xx, k], h_recv.at[1, p, xx, k], me.yn)

    def ya_copy(p, k):
        piece = grad_piece(2 * p + c, 3 * (2 * (1 - y) + x) + k)
        return remote(g.at[piece, low], ya.at[p, k], t_send.at[0, p, k], t_recv.at[0, p, k], me.yn)

    def xb_copy(p, k):
        piece = grad_piece(2 * p + c, 3 * (2 * y + 1 - x) + k)
        return remote(g.at[piece, high], xb.at[p, k], t_send.at[1, p, k], t_recv.at[1, p, k], me.xn)

    def from_sib(p):
        def body(i):
            sib_copy(p, i).wait_recv()
            piece = grad_piece(2 * p + c, i)
            add_into(piece, whole, sib[p, i])

        loop(0, 12, body)

        def send(k):
            for n in range(2):
                xa_copy(p, n, k).start()
                yb_copy(p, n, k).start()

        loop(0, 3, send)

    def first_half(p):
        def body(k):
            xa_copy(p, 1 - y, k).wait_recv()
            add_into(grad_piece(2 * p + c, 3 * (2 * (1 - y) + x) + k), low, xa[p, 1 - y, k])
            ya_copy(p, k).start()
            yb_copy(p, 1 - x, k).wait_recv()
            add_into(grad_piece(2 * p + c, 3 * (2 * y + 1 - x) + k), high, yb[p, 1 - x, k])
            xb_copy(p, k).start()
            own = grad_piece(2 * p + c, 3 * q + k)
            xa_copy(p, y, k).wait_recv()
            add_into(own, low, xa[p, y, k])
            yb_copy(p, x, k).wait_recv()
            add_into(own, high, yb[p, x, k])

        loop(0, 3, body)

    def z_copy(p, k, way):
        piece = grad_piece(2 * p + c, 3 * q + k)
        return remote(g.at[piece], (zu, zd)[way].at[p, k], z_send.at[way, p, k], z_recv.at[way, p, k], (me.up, me.down)[way])

    def second_half(p):
        def body(k):
            own = grad_piece(2 * p + c, 3 * q + k)
            ya_copy(p, k).wait_recv()
            add_into(own, low, ya[p, k])
            xb_copy(p, k).wait_recv()
            add_into(own, high, xb[p, k])

            @pl.when((z == 0) & (p > 0))
            def _():
                z_copy(p, k, 0).start()

            @pl.when((z == 3) & (p < 3))
            def _():
                z_copy(p, k, 1).start()

        loop(0, 3, body)

    def along_z(p):
        def body(k):
            own = grad_piece(2 * p + c, 3 * q + k)

            @pl.when((z > 0) & (z < p))
            def _():
                z_copy(p, k, 0).wait_recv()
                add_into(own, whole, zu[p, k])
                z_copy(p, k, 0).start()

            @pl.when((z < 3) & (z > p))
            def _():
                z_copy(p, k, 1).wait_recv()
                add_into(own, whole, zd[p, k])
                z_copy(p, k, 1).start()

        loop(0, 3, body)

    def share(kind, quarter, k):
        at = 3 * quarter + k
        ref = shard.at[at] if kind < 2 else shard.at[at, (low, high)[kind - 2]]
        to = (me.xn, me.yn, me.xn, me.yn)[kind]
        return remote(ref, ref, g_send.at[kind, k], g_recv.at[kind, k], to)

    def finish(k):
        own = grad_piece(2 * z + c, 3 * q + k)

        @pl.when(z > 0)
        def _():
            z_copy(z, k, 0).wait_recv()
            add_into(own, whole, zu[z, k])

        @pl.when(z < 3)
        def _():
            z_copy(z, k, 1).wait_recv()
            add_into(own, whole, zd[z, k])

        shard[3 * q + k] = g[own]
        share(0, q, k).start()
        share(1, q, k).start()


    def down_step(j):
        put_block(g, 8 + j, dot_tn(act[j], cot[...]))

        def send(r):
            at = 8 * (j - 1) + r

            @pl.when(at // 12 == 1 - c)
            def _():
                sib_copy(3, at % 12).start()

        loop(0, 8, send)

    loop(1, 4, down_step)
    col_sums(gv, 7, cot[...].astype(F32))

    def act_step(j):
        @pl.when(j == 1)
        def _():
            put_block(g, 8, dot_tn(act[0], cot[...]))
            send_span(1, 2, 4, 8)
            from_sib(3)

        act_grad(j, cot, g, slope, gv, work, low_rows, gn)
        put_block(g, 4 + j, dot_tn(n2[...], low_rows[...]))
        send_span(0, 1, 8 + j, 1)
        send_span(0, 2, 3 * j, 3)
        send_span(1, 1, 3 * j, 3)
        send_span(1, 2, j, 1)

    loop(0, 4, act_step)
    first_half(3)

    def keep_resid(at, value):
        work[at, :] = value
        low_rows[at, :] = value.astype(BF16)

    norm_back(resid, gn, v_ref[5:6, :], lambda at: cot[at, :].astype(F32), keep_resid, gv, 5)
    from_sib(2)
    second_half(3)
    col_sums(gv, 4, low_rows[...].astype(F32))
    grad = dot_nt(low_rows[...], block(g, 3))
    for j in range(6):
        ga[j] = grad[:, LANES * j : LANES * (j + 1)].astype(BF16)
    put_block(g, 3, dot_tn(slabs(att, 0), low_rows[...]))
    send_span(0, 1, 0, 8)

    def attend_back_step(j):
        @pl.when(j == 2)
        def _():
            from_sib(1)
            along_z(3)

        @pl.when(j == 4)
        def _():
            first_half(2)

        attend_back(j, same_of, qkv, lse, ga, gm)

    loop(0, 6, attend_back_step)

    def qkv_back_step(b):
        mixed = slabs(gm, 6 * b)

        @pl.when(b != 1)
        def _():
            gv[pl.ds(2 + b // 2, 1), :] = jnp.sum(mixed.astype(F32), axis=0, keepdims=True)

        add_part(b, gn, dot_nt(mixed, block(g, b)))
        put_block(g, b, dot_tn(n1[...], mixed))
        send_span(0, 0, 4 * b, 4)
        send_span(1, 0, 4 * b, 4)

        @pl.when(b == 0)
        def _():
            second_half(2)
            along_z(2)

        @pl.when(b == 1)
        def _():
            first_half(1)

    loop(0, 3, qkv_back_step)

    def keep_tokens(at, value):
        work[at, :] = value

    norm_back(emb, gn, v_ref[0:1, :], lambda at: work[at, :], keep_tokens, gv, 0)
    tok_copy = pltpu.make_async_copy(work.at[pl.ds(0, real)], gtok_ref, tok_sem)
    tok_copy.start()
    vsum[0] = gv[...]

    def v_turn(n):
        v_step(n).wait_recv()
        vsum[n + 1] = vsum[n] + vpart[n]
        if n < 4:
            v_step(n + 1).start()

    v_step(0).start()
    from_sib(0)
    second_half(1)
    v_turn(0)
    along_z(1)
    first_half(0)
    v_turn(1)
    second_half(0)
    v_turn(2)
    along_z(0)
    v_turn(3)
    loop(0, 3, finish)

    def pass_on(k):
        share(0, qx, k).wait_recv()
        share(3, qx, k).start()
        share(1, qy, k).wait_recv()
        share(2, qy, k).start()

    loop(0, 3, pass_on)
    v_turn(4)

    def last(k):
        share(2, qd, k).wait_recv()
        share(3, qd, k).wait_recv()

    loop(0, 3, last)

    norms[0] = jnp.zeros((8, LANES), F32)

    def lay(i, stride, first):
        total = norms[0]
        for j in range(6):
            part = shard[i, :, LANES * j : LANES * (j + 1)].astype(F32)
            flat_ref[pl.ds(first + j, PIECE, stride=stride), :] = part
            total = total + jnp.sum((part * part).reshape(PIECE // 8, 8, LANES), axis=0)
        norms[0] = total

    weave(s, lay)

    @pl.when(s == 7)
    def _():
        total = norms[0]
        for j in range(6):
            part = vsum[5, 0:12, LANES * j : LANES * (j + 1)]
            flat_ref[pl.ds(6912 + j, 12, stride=6), :] = part
            total = total + jnp.concatenate([part[0:8] * part[0:8], jnp.zeros((8, LANES), F32)], axis=0)[0:8]
            total = total + jnp.concatenate([part[8:12] * part[8:12], jnp.zeros((4, LANES), F32)], axis=0)
        norms[0] = total

    edge = remote(flat_ref.at[pl.ds(0, TAIL)], flat_ref.at[pl.ds(6912, TAIL)], e_sem.at[0], e_sem.at[1], me.at(me.dp, (s + 7) % 8))

    @pl.when(s > 0)
    def _():
        edge.start()

    def norm_copy(n):
        return remote(norms.at[0], norms.at[n], n_send.at[n], n_recv.at[n], me.at(me.dp, (s + n) % 8))

    for n in range(1, 8):
        norm_copy(n).start()

    def sent_sib(n):
        sib_copy(n // 12, n % 12).wait_send()

    loop(0, 48, sent_sib)

    def sent_plane(n):
        p, k = n // 3, n % 3
        for m in range(2):
            xa_copy(p, m, k).wait_send()
            yb_copy(p, m, k).wait_send()
        ya_copy(p, k).wait_send()
        xb_copy(p, k).wait_send()

        @pl.when(z < p)
        def _():
            z_copy(p, k, 0).wait_send()

        @pl.when(z > p)
        def _():
            z_copy(p, k, 1).wait_send()

    loop(0, 12, sent_plane)

    def sent_share(k):
        share(0, q, k).wait_send()
        share(1, q, k).wait_send()
        share(2, qy, k).wait_send()
        share(3, qx, k).wait_send()

    loop(0, 3, sent_share)
    for n in range(5):
        v_step(n).wait_send()

    tok_copy.wait()
    total = norms[0]
    for n in range(1, 8):
        norm_copy(n).wait()
        total = total + norms[n]
    norm_ref[...] = total

    @pl.when(s > 0)
    def _():
        edge.wait_send()

    @pl.when(s < 7)
    def _():
        edge.wait_recv()


def step(own, tokens, keep, clip_col, clip_row, cotangent):
    dma = pltpu.SemaphoreType.DMA
    anywhere = pl.BlockSpec(memory_space=pl.ANY)
    table = jnp.asarray(position_table())
    return pl.pallas_call(
        step_kernel,
        name="step",
        out_shape=[
            jax.ShapeDtypeStruct(tokens.shape, BF16),
            jax.ShapeDtypeStruct(cotangent.shape, F32),
            jax.ShapeDtypeStruct((FLAT, LANES), F32),
            jax.ShapeDtypeStruct((8, LANES), F32),
        ],
        in_specs=[anywhere] + [VM] * 6,
        out_specs=[VM, anywhere, VM, VM],
        scratch_shapes=[pltpu.VMEM(*k) for k in kept_shapes()]
        + [
            pltpu.VMEM((ROWS, D), BF16),
            pltpu.VMEM((ROWS, D), F32),
            pltpu.VMEM((ROWS, D), BF16),
            pltpu.VMEM((ROWS, D), F32),
            pltpu.VMEM((6, ROWS, LANES), BF16),
            pltpu.VMEM((18, ROWS, LANES), BF16),
            pltpu.VMEM((16, D), F32),
            pltpu.VMEM((120, PIECE, D), BF16),
            pltpu.VMEM((16, D), F32),
            pltpu.VMEM((TAIL, LANES), F32),
            pltpu.VMEM((TAIL, LANES), F32),
            pltpu.VMEM((4, 12, PIECE, D), BF16),
            pltpu.VMEM((4, 2, 3, HALF, D), BF16),
            pltpu.VMEM((4, 3, HALF, D), BF16),
            pltpu.VMEM((4, 2, 3, HALF, D), BF16),
            pltpu.VMEM((4, 3, HALF, D), BF16),
            pltpu.VMEM((4, 3, PIECE, D), BF16),
            pltpu.VMEM((4, 3, PIECE, D), BF16),
            pltpu.VMEM((12, PIECE, D), BF16),
            pltpu.VMEM((6, 16, D), F32),
            pltpu.VMEM((5, 16, D), F32),
            pltpu.VMEM((8, 8, LANES), F32),
            dma,
            dma((2,)),
            dma((7,)),
            dma,
            dma((2, 4, 3)),
            dma((4, 3)),
            dma((4, 4, 3)),
            dma((4, 4, 3)),
            dma((4, 12)),
            dma((4, 12)),
            dma,
            dma((4, 12)),
            dma((4, 12)),
            dma((2, 4, 2, 3)),
            dma((2, 4, 2, 3)),
            dma((2, 4, 3)),
            dma((2, 4, 3)),
            dma((2, 4, 3)),
            dma((2, 4, 3)),
            dma((4, 3)),
            dma((4, 3)),
            dma((5,)),
            dma((5,)),
            dma((2,)),
            dma((8,)),
            dma((8,)),
        ],
        compiler_params=pltpu.CompilerParams(collective_id=0, has_side_effects=True, vmem_limit_bytes=LIMIT),
    )(own, tokens, keep, clip_col, clip_row, table, cotangent)


STEP_ROWS = 1024


def update_kernel(flat_ref, norm_ref, param_ref, first_ref, second_ref, grad_out, change_out, first_out, second_out):
    s = lax.axis_index("fsdp")
    n = pl.program_id(0)
    rows = param_ref.shape[0]
    grad = flat_ref[pl.ds(n * rows + 9 * s, rows), :]
    squares = jnp.sum(jnp.sum(norm_ref[...], axis=0, keepdims=True), axis=1, keepdims=True)
    factor = jnp.minimum(1.0, 1.0 / (jnp.sqrt(squares) + 1e-06))
    clipped = grad * factor
    new_first = 0.9 * first_ref[...] + 0.1 * clipped
    new_second = 0.999 * second_ref[...] + 0.001 * clipped * clipped
    first_hat = new_first * (1.0 / first_correct)
    second_hat = new_second * (1.0 / second_correct)
    row = s * 6921 + n * rows + lax.broadcasted_iota(jnp.int32, (rows, LANES), 0)
    decay = jnp.where(row < MATS // LANES, 0.05, 0.0)
    step_rate = 0.001 * 0.75**6
    grad_out[...] = grad
    first_out[...] = new_first
    second_out[...] = new_second
    change_out[...] = step_rate * (first_hat / (jnp.sqrt(second_hat) + 1e-08) + decay * param_ref[...])


def update(flat, norm, params, first, second):
    rows = params.shape[0]
    spec = pl.BlockSpec((STEP_ROWS, LANES), lambda n: (n, 0))
    return pl.pallas_call(
        update_kernel,
        name="update",
        grid=(pl.cdiv(rows, STEP_ROWS),),
        out_shape=[jax.ShapeDtypeStruct((rows, LANES), F32)] * 4,
        in_specs=[VM, VM, spec, spec, spec],
        out_specs=[spec] * 4,
        compiler_params=pltpu.CompilerParams(vmem_limit_bytes=LIMIT),
    )(flat, norm, params, first, second)


def shards(tokens, cotangent, keep_index, clip_ids, flat_params, first_moment, second_moment):
    flat = flat_params.reshape(-1, LANES)
    pad = ROWS - tokens.shape[0]
    keep = jnp.pad(keep_index.reshape(-1, 1), ((0, pad), (0, 0)))
    clip = jnp.pad(jnp.repeat(clip_ids.reshape(-1), KEEP), (0, pad), constant_values=-1)
    clip_col, clip_row = clip[:, None], clip[None, :]
    layer_out, grad_tokens, summed, norm = step(flat, tokens, keep, clip_col, clip_row, cotangent)
    outs = update(summed, norm, flat, first_moment.reshape(-1, LANES), second_moment.reshape(-1, LANES))
    grad, change, first, second = (o.reshape(-1) for o in outs)
    return (layer_out, grad_tokens, grad, change, first, second)


def layer_norm(values, gain_vec, shift_vec):
    row_mean = jnp.mean(values, axis=-1, keepdims=True)
    centered = values - row_mean
    variance = jnp.mean(centered * centered, axis=-1, keepdims=True)
    return centered * lax.rsqrt(variance + 1e-06) * gain_vec + shift_vec


def gelu_exact(values):
    return jax.nn.gelu(values, approximate=False)


def positions(keep_flat):
    quarter = D // 4
    frequency = 1.0 / 10000.0 ** (jnp.arange(quarter).astype(jnp.float32) / quarter)
    row_angle = (keep_flat // GRID).astype(jnp.float32)[:, None] * frequency
    col_angle = (keep_flat % GRID).astype(jnp.float32)[:, None] * frequency
    return jnp.concatenate(
        [jnp.sin(row_angle), jnp.cos(row_angle), jnp.sin(col_angle), jnp.cos(col_angle)], axis=1
    )


def unpack_flat(flat):
    mats = 4 * D * D + 2 * D * FF
    w_qkv = flat[: 3 * D * D].reshape(D, 3 * D)
    w_out = flat[3 * D * D : 4 * D * D].reshape(D, D)
    w_up = flat[4 * D * D : 4 * D * D + D * FF].reshape(D, FF)
    w_down = flat[4 * D * D + D * FF : mats].reshape(FF, D)
    vectors = flat[mats : mats + 8 * D].reshape(8, D)
    bias_up = flat[mats + 8 * D :]
    return (w_qkv, w_out, w_up, w_down, vectors, bias_up)


def split_heads(values):
    return values.reshape(values.shape[0], HEADS, HEAD_DIM).transpose(1, 0, 2)


def join_heads(values):
    return values.transpose(1, 0, 2).reshape(values.shape[1], D)


def product(left, right):
    return jnp.dot(left, right, preferred_element_type=jnp.float32)


def plain_shards(tokens, cotangent, keep_index, clip_ids, flat_params, first_moment, second_moment):
    shard_len = flat_params.shape[0]
    mats = 4 * D * D + 2 * D * FF
    score_scale = HEAD_DIM ** (-0.5)
    sent = flat_params.astype(jnp.bfloat16)
    gathered = lax.all_gather(sent, "fsdp", axis=0, tiled=True)
    w_qkv, w_out, w_up, w_down, vectors_low, bias_up_low = unpack_flat(gathered)
    vectors = vectors_low.astype(jnp.float32)
    bias_up = bias_up_low.astype(jnp.float32)
    embedded = tokens.astype(jnp.float32) + positions(keep_index.reshape(-1))
    normed, norm_back = jax.vjp(layer_norm, embedded, vectors[0], vectors[1])
    normed_low = normed.astype(jnp.bfloat16)
    mixed_qkv = product(normed_low, w_qkv)
    query_low = (mixed_qkv[:, :D] + vectors[2]).astype(jnp.bfloat16)
    key_low = mixed_qkv[:, D : 2 * D].astype(jnp.bfloat16)
    value_low = (mixed_qkv[:, 2 * D :] + vectors[3]).astype(jnp.bfloat16)
    query_heads = split_heads(query_low)
    key_heads = split_heads(key_low)
    value_heads = split_heads(value_low)
    clip_tok = jnp.repeat(clip_ids.reshape(-1), KEEP)
    same_clip = clip_tok[:, None] == clip_tok[None, :]

    def attend(head_item):
        q_head, k_head, v_head = head_item
        scores = jnp.where(same_clip, product(q_head, k_head.T) * score_scale, -1e30)
        row_top = jnp.max(scores, axis=1, keepdims=True)
        weight_exp = jnp.exp(scores - row_top)
        row_total = jnp.sum(weight_exp, axis=1, keepdims=True)
        soft_low = (weight_exp / row_total).astype(jnp.bfloat16)
        return (product(soft_low, v_head), row_top + jnp.log(row_total))

    attended_heads, log_total = lax.map(attend, (query_heads, key_heads, value_heads))
    attended_low = join_heads(attended_heads).astype(jnp.bfloat16)
    resid = embedded + product(attended_low, w_out) + vectors[4]
    normed_two, norm_two_back = jax.vjp(layer_norm, resid, vectors[5], vectors[6])
    normed_two_low = normed_two.astype(jnp.bfloat16)
    pre_act = product(normed_two_low, w_up) + bias_up
    activated, gelu_back = jax.vjp(gelu_exact, pre_act)
    activated_low = activated.astype(jnp.bfloat16)
    layer_out = (resid + product(activated_low, w_down) + vectors[7]).astype(jnp.bfloat16)
    w_qkv, w_out, w_up, w_down, vectors_low, bias_up_low = unpack_flat(
        lax.all_gather(sent, "fsdp", axis=0, tiled=True)
    )
    grad_out = cotangent.astype(jnp.float32)
    grad_w_down = product(activated_low.T, cotangent)
    grad_bias_down = jnp.sum(grad_out, axis=0)
    grad_act = product(cotangent, w_down.T)
    grad_pre_low = gelu_back(grad_act)[0].astype(jnp.bfloat16)
    grad_w_up = product(normed_two_low.T, grad_pre_low)
    grad_bias_up = jnp.sum(grad_pre_low.astype(jnp.float32), axis=0)
    grad_normed_two = product(grad_pre_low, w_up.T)
    grad_resid_norm, grad_gain_two, grad_shift_two = norm_two_back(grad_normed_two)
    grad_resid = grad_out + grad_resid_norm
    grad_branch_low = grad_resid.astype(jnp.bfloat16)
    grad_w_out = product(attended_low.T, grad_branch_low)
    grad_bias_out = jnp.sum(grad_branch_low.astype(jnp.float32), axis=0)
    grad_attended_low = product(grad_branch_low, w_out.T).astype(jnp.bfloat16)

    def attend_back(head_item):
        q_head, k_head, v_head, g_head, lse_head = head_item
        soft = jnp.where(
            same_clip, jnp.exp(product(q_head, k_head.T) * score_scale - lse_head), 0.0
        )
        grad_soft = product(g_head, v_head.T)
        grad_value = product(soft.astype(jnp.bfloat16).T, g_head)
        inner = jnp.sum(soft * grad_soft, axis=1, keepdims=True)
        grad_raw = (score_scale * soft * (grad_soft - inner)).astype(jnp.bfloat16)
        return (product(grad_raw, k_head), product(grad_raw.T, q_head), grad_value)

    grad_query, grad_key, grad_value = lax.map(
        attend_back,
        (query_heads, key_heads, value_heads, split_heads(grad_attended_low), log_total),
    )
    grad_mixed = jnp.concatenate(
        [join_heads(grad_query), join_heads(grad_key), join_heads(grad_value)], axis=1
    ).astype(jnp.bfloat16)
    grad_w_qkv = product(normed_low.T, grad_mixed)
    mixed_sums = jnp.sum(grad_mixed.astype(jnp.float32), axis=0)
    grad_normed = product(grad_mixed, w_qkv.T)
    grad_embedded, grad_gain_one, grad_shift_one = norm_back(grad_normed)
    grad_tokens = grad_resid + grad_embedded
    full_grad = jnp.concatenate(
        [
            grad_w_qkv.reshape(-1),
            grad_w_out.reshape(-1),
            grad_w_up.reshape(-1),
            grad_w_down.reshape(-1),
            grad_gain_one,
            grad_shift_one,
            mixed_sums[:D],
            mixed_sums[2 * D :],
            grad_bias_out,
            grad_gain_two,
            grad_shift_two,
            grad_bias_down,
            grad_bias_up,
        ]
    )
    replicas = lax.axis_size("dp")
    owners = lax.axis_size("fsdp")
    reordered = full_grad.reshape(owners, replicas, -1).transpose(1, 0, 2).reshape(-1)
    own_piece = lax.psum_scatter(reordered, ("dp", "fsdp"), scatter_dimension=0, tiled=True)
    own_grad = lax.all_gather(own_piece.astype(jnp.bfloat16), "dp", axis=0, tiled=True).astype(
        own_piece.dtype
    )
    squares = lax.psum(jnp.sum(own_grad * own_grad), "fsdp")
    clip_factor = jnp.minimum(1.0, 1.0 / (jnp.sqrt(squares) + 1e-06))
    clipped = own_grad * clip_factor
    new_first = 0.9 * first_moment + 0.1 * clipped
    new_second = 0.999 * second_moment + 0.001 * clipped * clipped
    first_hat = new_first / first_correct
    second_hat = new_second / second_correct
    position = lax.axis_index("fsdp") * shard_len + jnp.arange(shard_len, dtype=jnp.int32)
    decay_mask = (position < mats).astype(jnp.float32)
    step_rate = 0.001 * 0.75**6
    param_change = step_rate * (
        first_hat / (jnp.sqrt(second_hat) + 1e-08) + 0.05 * decay_mask * flat_params
    )
    return (layer_out, grad_tokens, own_grad, param_change, new_first, new_second)


def solution(mesh):
    placed = (
        P(("dp", "fsdp"), None),
        P(("dp", "fsdp"), None),
        P(("dp", "fsdp"), None),
        P(("dp", "fsdp"), None),
        P("fsdp"),
        P("fsdp"),
        P("fsdp"),
    )
    staged = mesh.shape["dp"] == 4 and mesh.shape["fsdp"] == 8
    return jax.shard_map(
        shards if staged else plain_shards,
        mesh=mesh,
        in_specs=placed,
        out_specs=(
            P(("dp", "fsdp"), None),
            P(("dp", "fsdp"), None),
            P("fsdp"),
            P("fsdp"),
            P("fsdp"),
            P("fsdp"),
        ),
        check_vma=False,
    )
```

```python
import functools

import jax
import jax.numpy as jnp
import numpy as np
from jax import lax
from jax.experimental import pallas as pl
from jax.experimental.pallas import tpu as pltpu
from jax.sharding import PartitionSpec as P

D = 768
FF = 3072
HEADS = 12
HEAD_DIM = 64
GRID = 14
KEEP = 49
MATS = 4 * D * D + 2 * D * FF

first_correct = 0.9999734386011124
second_correct = 0.09520785288629106

F32 = jnp.float32
BF16 = jnp.bfloat16
MESH = pl.DeviceIdType.MESH
LIMIT = 66_000_000

ROWS = 400
CHUNK = 80
PIECE = 96
PIECES = 12
LANES = 128
TAIL = 72


def div(a, b):
    return a // b if isinstance(a, int) else lax.div(a, np.int32(b))


def ge(s, k):
    return div(s + 8 - k, 8)


def piece_of(s, i):
    g5, by3, by4, by8 = div(i + 4, 8), div(i, 3), div(i, 4), div(i, 8)
    forms = (
        4 * by4 + i,
        4 * by4 + 4 + i,
        24 + i + by8 * (7 * i - 56),
        33 + 5 * by3 + i,
        36 + 5 * by3 + i,
        (1 - g5) * (39 + 8 * i) + g5 * (60 + i),
        72 + i,
        84 + i,
    )
    out = forms[0]
    for k in range(1, 8):
        out = out + ge(s, k) * (forms[k] - forms[k - 1])
    return out


def grad_piece(s, i):
    return piece_of(s, i) + 24 * ge(s, 6)


def grad_block(b):
    return 8 * b + 24 * div(b + 7, 16)


ARRIVALS = (
    ((1, 0), (1, 1), (1, 2), (2, 0), (2, 1), (2, 2), (3, 0), (3, 1), (3, 2)),
    ((0, 0), (0, 1), (0, 2), (2, 0), (2, 1), (2, 2), (3, 0), (3, 1), (3, 2)),
    ((3, 0), (1, 0), (0, 0), (0, 1), (0, 2), (1, 1), (1, 2), (3, 1), (3, 2)),
    ((2, 0), (1, 0), (0, 0), (0, 1), (0, 2), (1, 1), (1, 2), (2, 1), (2, 2)),
)


def arrival(z, n):
    out = []
    for m in range(2):
        row = [ARRIVALS[plane][n][m] for plane in range(4)]
        value = row[0]
        for plane in range(1, 4):
            value = value + (row[plane] - row[plane - 1]) * div(z + 4 - plane, 4)
        out.append(value)
    return out


def dot(a, b):
    return lax.dot_general(a, b, (((1,), (0,)), ((), ())), preferred_element_type=F32)


def dot_nt(a, b):
    return lax.dot_general(a, b, (((1,), (1,)), ((), ())), preferred_element_type=F32)


def dot_tn(a, b):
    return lax.dot_general(a, b, (((0,), (0,)), ((), ())), preferred_element_type=F32)


def loop(start, stop, body):
    def step(i, carry):
        body(i)
        return carry

    lax.fori_loop(start, stop, step, 0)


def chunks(body):
    loop(0, ROWS // CHUNK, lambda n: body(pl.ds(pl.multiple_of(n * CHUNK, CHUNK), CHUNK)))


class Place:
    def __init__(self):
        self.dp = lax.axis_index("dp")
        self.s = lax.axis_index("fsdp")
        self.x, self.y = self.dp % 2, self.dp // 2
        self.z, self.c = self.s // 2, self.s % 2
        self.sib = self.at(self.dp, self.s + 1 - 2 * self.c)
        self.xn = self.at(self.dp + 1 - 2 * self.x, self.s)
        self.yn = self.at(self.dp + 2 - 4 * self.y, self.s)
        self.up = self.at(self.dp, self.s + 2)
        self.down = self.at(self.dp, self.s - 2)

    def at(self, dp, s):
        return (dp, s)

    def barrier(self):
        sem = pltpu.get_barrier_semaphore()
        for n in range(1, 8):
            pl.semaphore_signal(sem, inc=1, device_id=self.at(self.dp, (self.s + n) % 8), device_id_type=MESH)
        for peer in (self.xn, self.yn):
            pl.semaphore_signal(sem, inc=1, device_id=peer, device_id_type=MESH)
        pl.semaphore_wait(sem, 9)


def remote(src, dst, send, recv, to):
    return pltpu.make_async_remote_copy(
        src_ref=src, dst_ref=dst, send_sem=send, recv_sem=recv, device_id=to, device_id_type=MESH
    )


def weave(s, body):
    @pl.when(s <= 1)
    def _():
        loop(0, 12, lambda i: body(i, 18, (i % 4) * (96 * 18) + (i // 4) * 6))

    @pl.when(s == 2)
    def _():
        loop(0, 8, lambda i: body(i, 6, i * (96 * 6)))
        loop(8, 12, lambda i: body(i, 24, 4608 + (i - 8) * 6))

    @pl.when((s == 3) | (s == 4))
    def _():
        loop(0, 12, lambda i: body(i, 24, (i % 3) * (96 * 24) + (i // 3) * 6))

    @pl.when(s == 5)
    def _():
        loop(0, 4, lambda i: body(i, 24, i * 6))
        loop(4, 12, lambda i: body(i, 6, 2304 + (i - 4) * (96 * 6)))

    @pl.when(s >= 6)
    def _():
        loop(0, 12, lambda i: body(i, 6, i * (96 * 6)))


def position_table():
    quarter = D // 4
    exponent = np.arange(quarter, dtype=np.float32) / np.float32(quarter)
    frequency = np.float32(1.0) / np.power(np.float32(10000.0), exponent).astype(np.float32)
    angle = (np.arange(GRID, dtype=np.float32)[:, None] * frequency).astype(np.float64)
    waves = np.concatenate([np.sin(angle), np.cos(angle)], axis=1).astype(np.float32)
    table = np.zeros((32, D), np.float32)
    table[:GRID, : D // 2] = waves
    table[16 : 16 + GRID, D // 2 :] = waves
    parts = []
    for _ in range(3):
        part = table.astype(jnp.bfloat16)
        parts.append(part)
        table = table - part.astype(np.float32)
    return np.stack(parts)


def norm_stats(v):
    mean = jnp.mean(v, axis=-1, keepdims=True)
    centered = v - mean
    rstd = lax.rsqrt(jnp.mean(centered * centered, axis=-1, keepdims=True) + 1e-06)
    return centered * rstd, rstd


def block(g_ref, b):
    return g_ref[pl.ds(8 * b, 8)].reshape(D, D)


def slabs(ref, first):
    return jnp.concatenate([ref[first + j] for j in range(6)], axis=1)


def place_tokens(keep_ref, clip_ref, keep_col, clip_col, clip_row):
    token = lax.broadcasted_iota(jnp.int32, (ROWS, KEEP), 0)
    lane = lax.broadcasted_iota(jnp.int32, (ROWS, KEEP), 1)
    down = lax.broadcasted_iota(jnp.int32, (ROWS, 1), 0)
    across = lax.broadcasted_iota(jnp.int32, (1, ROWS), 1)
    patches = jnp.zeros((ROWS, KEEP), F32)
    col = jnp.full((ROWS, 1), -1, jnp.int32)
    row = jnp.full((1, ROWS), -1, jnp.int32)
    for i in range(keep_ref.shape[0]):
        first, last = KEEP * i, KEEP * i + KEEP
        patches = jnp.where(token == lane + first, keep_ref[i : i + 1, :].astype(F32), patches)
        clip = clip_ref[0:1, i : i + 1]
        col = jnp.where((down >= first) & (down < last), clip, col)
        row = jnp.where((across >= first) & (across < last), clip, row)
    keep_col[...] = jnp.sum(patches, axis=1, keepdims=True).astype(jnp.int32)
    clip_col[...] = col
    clip_row[...] = row


def embed(tok_ref, keep_ref, table_ref, emb):
    real = tok_ref.shape[0]
    emb[0:real, :] = tok_ref[...].astype(F32)
    emb[real:, :] = jnp.zeros((ROWS - real, D), F32)

    def body(at):
        keep = keep_ref[at, :]
        row = (keep * 4682) >> 16
        col = keep - GRID * row + 16
        lane = lax.broadcasted_iota(jnp.int32, (CHUNK, 32), 1)
        hot = jnp.where((lane == row) | (lane == col), 1.0, 0.0).astype(BF16)
        spot = dot(hot, table_ref[0]) + (dot(hot, table_ref[1]) + dot(hot, table_ref[2]))
        emb[at, :] = emb[at, :] + spot

    chunks(body)


def norm_one(emb, v_ref, n1):
    gain, shift = v_ref[0:1, :], v_ref[1:2, :]

    def body(at):
        n1[at, :] = (norm_stats(emb[at, :])[0] * gain + shift).astype(BF16)

    chunks(body)


def project(b, n1, g_ref, v_ref, qkv):
    mixed = dot(n1[...], block(g_ref, b)) + v_ref[pl.ds(2 + b // 2, 1), :] * jnp.where(b == 1, 0.0, 1.0)
    for j in range(6):
        qkv[6 * b + j] = mixed[:, LANES * j : LANES * (j + 1)].astype(BF16)


def attend(j, same_of, qkv, att, lse):
    query, key, value = qkv[j], qkv[6 + j], qkv[12 + j]
    first = lax.broadcasted_iota(jnp.int32, (ROWS, LANES), 1) < HEAD_DIM
    turned = value.T
    parts = []
    for h in range(2):
        own = jnp.where(first if h == 0 else ~first, query, jnp.zeros_like(query))
        scores = jnp.where(same_of(), dot_nt(key, own) * 0.125, -1e30)
        top = jnp.max(scores, axis=0, keepdims=True)
        weight = jnp.exp(scores - top)
        total = jnp.sum(weight, axis=0, keepdims=True)
        soft = (weight * (1.0 / total)).astype(BF16)
        lse[2 * j + h] = top + jnp.log(total)
        parts.append(dot(turned[HEAD_DIM * h : HEAD_DIM * (h + 1), :], soft))
    att[j] = jnp.concatenate(parts, axis=0).T.astype(BF16)


def out_project(att, g_ref, v_ref, emb, resid, n2):
    resid[...] = dot(slabs(att, 0), block(g_ref, 3))
    bias, gain, shift = v_ref[4:5, :], v_ref[5:6, :], v_ref[6:7, :]

    def body(at):
        value = emb[at, :] + resid[at, :] + bias
        resid[at, :] = value
        n2[at, :] = (norm_stats(value)[0] * gain + shift).astype(BF16)

    chunks(body)


def expand(j, n2, g_ref, v_ref, work, act, slope):
    work[...] = dot(n2[...], block(g_ref, 4 + j))

    def body(at):
        pre = work[at, :] + v_ref[pl.ds(8 + j, 1), :]
        phi = 0.5 * (1.0 + lax.erf(pre * 0.7071067811865476))
        act[j, at, :] = (pre * phi).astype(BF16)
        slope[j, at, :] = (phi + pre * (0.3989422804014327 * jnp.exp(-0.5 * pre * pre))).astype(BF16)

    chunks(body)


def contract(j, act, g_ref, work):
    add_part(j, work, dot(act[j], block(g_ref, 8 + j)))


def kept_shapes():
    return [
        ((ROWS, D), F32),
        ((ROWS, D), BF16),
        ((18, ROWS, LANES), BF16),
        ((6, ROWS, LANES), BF16),
        ((HEADS, 1, ROWS), F32),
        ((ROWS, D), F32),
        ((ROWS, D), BF16),
        ((4, ROWS, D), BF16),
        ((4, ROWS, D), BF16),
    ]


VM = pl.BlockSpec(memory_space=pltpu.VMEM)


def col_sums(dest, row, source):
    dest[row : row + 1, :] = jnp.sum(source, axis=0, keepdims=True)


def put_block(gw, b, value):
    gw[pl.ds(grad_block(b), 8)] = value.astype(BF16).reshape(8, PIECE, D)


def act_grad(j, cot, g_ref, slope, gv, work, pre_low, gn):
    work[...] = dot_nt(cot[...], block(g_ref, 8 + j))
    total = jnp.zeros((8, D), F32)

    def body(n, total):
        at = pl.ds(pl.multiple_of(n * CHUNK, CHUNK), CHUNK)
        low = (slope[j, at, :].astype(F32) * work[at, :]).astype(BF16)
        pre_low[at, :] = low
        return total + jnp.sum(low.astype(F32).reshape(CHUNK // 8, 8, D), axis=0)

    total = lax.fori_loop(0, ROWS // CHUNK, body, total)
    gv[pl.ds(8 + j, 1), :] = jnp.sum(total, axis=0, keepdims=True)
    add_part(j, gn, dot_nt(pre_low[...], block(g_ref, 4 + j)))


def add_part(j, total, part):
    @pl.when(j == 0)
    def _():
        total[...] = part

    @pl.when(j > 0)
    def _():
        total[...] += part


def norm_back(value_ref, gn, gain, extra, store, gv, row):
    def body(n, sums):
        at = pl.ds(pl.multiple_of(n * CHUNK, CHUNK), CHUNK)
        hat, rstd = norm_stats(value_ref[at, :])
        grad = gn[at, :]
        fold = lambda v: jnp.sum(v.reshape(CHUNK // 8, 8, D), axis=0)
        sums = (sums[0] + fold(grad * hat), sums[1] + fold(grad))
        grad = grad * gain
        inner = jnp.mean(grad * hat, axis=-1, keepdims=True)
        store(at, extra(at) + rstd * (grad - jnp.mean(grad, axis=-1, keepdims=True) - hat * inner))
        return sums

    zero = jnp.zeros((8, D), F32)
    one, two = lax.fori_loop(0, ROWS // CHUNK, body, (zero, zero))
    gv[row : row + 1, :] = jnp.sum(one, axis=0, keepdims=True)
    gv[row + 1 : row + 2, :] = jnp.sum(two, axis=0, keepdims=True)


def attend_back(j, same_of, qkv, lse, ga, gm):
    query, key, value, grad = qkv[j], qkv[6 + j], qkv[12 + j], ga[j]
    first = lax.broadcasted_iota(jnp.int32, (ROWS, LANES), 1) < HEAD_DIM
    turned = key.T
    parts, grad_key, grad_value = [], None, None
    for h in range(2):
        mine = first if h == 0 else ~first
        own = jnp.where(mine, query, jnp.zeros_like(query))
        own_grad = jnp.where(mine, grad, jnp.zeros_like(grad))
        soft = jnp.where(same_of(), jnp.exp(dot_nt(key, own) * 0.125 - lse[2 * j + h]), 0.0)
        grad_soft = dot_nt(value, own_grad)
        inner = jnp.sum(soft * grad_soft, axis=0, keepdims=True)
        raw = (0.125 * soft * (grad_soft - inner)).astype(BF16)
        one = dot(soft.astype(BF16), own_grad)
        two = dot(raw, own)
        grad_value = one if h == 0 else grad_value + one
        grad_key = two if h == 0 else grad_key + two
        parts.append(dot(turned[HEAD_DIM * h : HEAD_DIM * (h + 1), :], raw))
    gm[j] = jnp.concatenate(parts, axis=0).T.astype(BF16)
    gm[6 + j] = grad_key.astype(BF16)
    gm[12 + j] = grad_value.astype(BF16)


FLAT = 7240
HALF = PIECE // 2


def step_kernel(own_hbm, tok_hbm, keep_ref, clip_ref, table_hbm, cot_hbm, *refs):
    out_ref, gtok_ref, flat_ref, norm_ref = refs[:4]
    emb, n1, qkv, att, lse, resid, n2, act, slope = refs[4:13]
    (
        tok_ref, table_ref, cot_ref, keep_col, clip_col, clip_row, in_sem,
        cot, work, low_rows, gn, ga, gm, gv, g, v_ref, tail, vbuf,
        sib, xa, ya, yb, xb, zu, zd, shard, vsum, vpart, norms,
        own_sem, edge_sem, gv_send, gv_recv, gz_send, gz_recv, gp_send, gp_recv, gc_send, gc_recv, tok_sem,
        sib_send, sib_recv, h_send, h_recv, t_send, t_recv, z_send, z_recv, g_send, g_recv, v_send, v_recv, e_sem, n_send, n_recv,
    ) = refs[13:]
    me = Place()
    s, z, c, x, y = me.s, me.z, me.c, me.x, me.y
    q = me.dp
    qx, qy, qd = q + 1 - 2 * x, q + 2 - 4 * y, 3 - q
    rows = own_hbm.shape[0]
    real = cot_ref.shape[0]

    own_copy = pltpu.make_async_copy(own_hbm, flat_ref.at[pl.ds(TAIL, rows)], own_sem)
    own_copy.start()
    loads = [
        pltpu.make_async_copy(src, dst, in_sem.at[n])
        for n, (src, dst) in enumerate(((tok_hbm, tok_ref), (table_hbm, table_ref), (cot_hbm, cot_ref)))
    ]
    for load in loads:
        load.start()
    gv[...] = jnp.zeros_like(gv)
    me.barrier()
    own_copy.wait()
    tail[...] = flat_ref[rows : rows + TAIL, :]
    edge = remote(tail, flat_ref.at[pl.ds(0, TAIL)], edge_sem.at[0], edge_sem.at[1], me.at(me.dp, (s + 1) % 8))

    @pl.when(s < 7)
    def _():
        edge.start()

    @pl.when(s == 7)
    def _():
        for n in range(7):
            remote(tail, vbuf, gv_send.at[n], gv_recv, me.at(me.dp, n)).start()
        vbuf[...] = tail[...]

    place_tokens(keep_ref, clip_ref, keep_col, clip_col, clip_row)
    loads[0].wait()
    loads[1].wait()
    embed(tok_ref, keep_col, table_ref, emb)

    @pl.when(s > 0)
    def _():
        edge.wait_recv()

    def to_sib(p, i):
        piece = piece_of(2 * p + c, i)
        return remote(g.at[piece], g.at[piece], gc_send.at[p, i], gc_recv.at[p, i], me.sib)

    def line_copy(p, k, way):
        piece = piece_of(2 * p + c, q + 4 * k)
        return remote(g.at[piece], g.at[piece], gz_send.at[way, p, k], gz_recv.at[p, k], (me.up, me.down)[way])

    def plane_copy(kind, p, quarter, k):
        piece = piece_of(2 * p + c, quarter + 4 * k)
        ref = g.at[piece]
        if kind >= 2:
            ref = g.at[piece, pl.ds(HALF * (kind - 2), HALF)]
        return remote(ref, ref, gp_send.at[kind, p, k], gp_recv.at[kind, p, k], (me.xn, me.yn)[kind % 2])

    def place_piece(i, stride, first):
        piece = piece_of(s, i)
        for j in range(6):
            g[piece, :, LANES * j : LANES * (j + 1)] = flat_ref[pl.ds(TAIL - 9 * s + first + j, PIECE, stride=stride), :].astype(BF16)

    weave(s, place_piece)
    flat_ref[6912:, :] = jnp.zeros((FLAT - 6912, LANES), F32)

    def own_up(k):
        line_copy(z, k, 0).start()

    @pl.when(z < 3)
    def _():
        own_up(0)

    @pl.when(z > 0)
    def _():
        loop(0, 3, lambda k: line_copy(z, k, 1).start())

    @pl.when(z == 0)
    def _():
        loop(1, 3, own_up)

    loop(0, 12, lambda i: to_sib(z, i).start())

    @pl.when(s < 7)
    def _():
        remote(tail, vbuf, gv_send.at[0], gv_recv, me.sib).wait_recv()

    for j in range(6):
        v_ref[0:12, LANES * j : LANES * (j + 1)] = vbuf[pl.ds(j, 12, stride=6), :].astype(BF16).astype(F32)

    def line_step(n):
        p, k = arrival(z, n)

        @pl.when(p < z)
        def _():
            line_copy(p, k, 0).wait_recv()

            @pl.when(z < 3)
            def _():
                line_copy(p, k, 0).start()

        @pl.when(p > z)
        def _():
            line_copy(p, k, 1).wait_recv()

            @pl.when(z > 0)
            def _():
                line_copy(p, k, 1).start()

        plane_copy(0, p, q, k).start()
        plane_copy(1, p, q, k).start()
        to_sib(p, q + 4 * k).start()
        if n in (2, 6):

            @pl.when(z == (1 if n == 2 else 2))
            def _():
                loop(1, 3, own_up)

    def plane_step(n):
        p, k = arrival(z, n)
        plane_copy(0, p, qx, k).wait_recv()
        plane_copy(3, p, qx, k).start()
        to_sib(p, qx + 4 * k).start()
        plane_copy(1, p, qy, k).wait_recv()
        plane_copy(2, p, qy, k).start()
        to_sib(p, qy + 4 * k).start()

    def far_step(n):
        p, k = arrival(z, n)
        plane_copy(2, p, qd, k).wait_recv()
        plane_copy(3, p, qd, k).wait_recv()
        to_sib(p, qd + 4 * k).start()

    def have(p, k):
        for quarter in range(4):
            to_sib(p, quarter + 4 * k).wait_recv()

    same_of = lambda: clip_col[...] == clip_row[...]
    norm_one(emb, v_ref, n1)
    line_step(0)
    line_step(1)
    plane_step(0)
    line_step(2)
    plane_step(1)
    line_step(3)
    far_step(0)
    line_step(4)
    plane_step(2)
    far_step(1)
    line_step(5)
    plane_step(3)
    line_step(6)
    far_step(2)

    def qkv_step(b):
        @pl.when(b == 1)
        def _():
            line_step(7)
            plane_step(4)
            far_step(3)

        @pl.when(b == 2)
        def _():
            line_step(8)
            plane_step(5)
            far_step(4)

        have(0, b)
        project(b, n1, g, v_ref, qkv)

    loop(0, 3, qkv_step)

    def attend_step(j):
        @pl.when(j == 2)
        def _():
            plane_step(6)
            far_step(5)

        attend(j, same_of, qkv, att, lse)

    loop(0, 6, attend_step)
    plane_step(7)
    far_step(6)
    have(1, 0)
    have(1, 1)
    out_project(att, g, v_ref, emb, resid, n2)
    have(1, 2)

    def expand_step(j):
        @pl.when(j == 1)
        def _():
            plane_step(8)
            far_step(7)

        @pl.when(j == 2)
        def _():
            far_step(8)

        @pl.when(j < 3)
        def _():
            have(2, j)

        expand(j, n2, g, v_ref, work, act, slope)

    loop(0, 4, expand_step)
    for k in range(3):
        have(3, k)
    loop(0, 4, lambda j: contract(j, act, g, work))
    out_ref[...] = (resid[0:real, :] + work[0:real, :] + v_ref[7:8, :]).astype(BF16)

    @pl.when(s < 7)
    def _():
        edge.wait_send()

    @pl.when(s == 7)
    def _():
        for n in range(7):
            remote(tail, vbuf, gv_send.at[n], gv_recv, me.sib).wait_send()

    def line_sent(p, k):
        @pl.when((p <= z) & (z < 3))
        def _():
            line_copy(p, k, 0).wait_send()

        @pl.when((p >= z) & (z > 0))
        def _():
            line_copy(p, k, 1).wait_send()

        @pl.when(p != z)
        def _():
            plane_copy(0, p, q, k).wait_send()
            plane_copy(1, p, q, k).wait_send()
            plane_copy(2, p, qy, k).wait_send()
            plane_copy(3, p, qx, k).wait_send()

    loop(0, 12, lambda n: line_sent(n // 3, n % 3))
    loop(0, 48, lambda n: to_sib(n // 12, n % 12).wait_send())

    def add_into(piece, rows, got):
        g[piece, rows, :] = (g[piece, rows, :].astype(F32) + got.astype(F32)).astype(BF16)

    low, high, whole = pl.ds(0, HALF), pl.ds(HALF, HALF), pl.ds(0, PIECE)

    def sib_copy(p, i):
        piece = grad_piece(2 * p + 1 - c, i)
        return remote(g.at[piece], sib.at[p, i], sib_send.at[p, i], sib_recv.at[p, i], me.sib)

    def send_span(parity, p, first, count):
        @pl.when(c == 1 - parity)
        def _():
            loop(0, count, lambda r: sib_copy(p, first + r).start())

    partners = (me.sib, me.xn, me.yn, me.at(me.dp, (s + 2 - 4 * (z % 2)) % 8), me.at(me.dp, (s + 4) % 8))

    def v_step(n):
        copy = remote(vsum.at[n], vpart.at[n], v_send.at[n], v_recv.at[n], partners[n])
        return copy

    def xa_copy(p, yy, k):
        piece = grad_piece(2 * p + c, 3 * (2 * yy + 1 - x) + k)
        return remote(g.at[piece, low], xa.at[p, yy, k], h_send.at[0, p, yy, k], h_recv.at[0, p, yy, k], me.xn)

    def yb_copy(p, xx, k):
        piece = grad_piece(2 * p + c, 3 * (2 * (1 - y) + xx) + k)
        return remote(g.at[piece, high], yb.at[p, xx, k], h_send.at[1, p, xx, k], h_recv.at[1, p, xx, k], me.yn)

    def ya_copy(p, k):
        piece = grad_piece(2 * p + c, 3 * (2 * (1 - y) + x) + k)
        return remote(g.at[piece, low], ya.at[p, k], t_send.at[0, p, k], t_recv.at[0, p, k], me.yn)

    def xb_copy(p, k):
        piece = grad_piece(2 * p + c, 3 * (2 * y + 1 - x) + k)
        return remote(g.at[piece, high], xb.at[p, k], t_send.at[1, p, k], t_recv.at[1, p, k], me.xn)

    def sib_third(p, k):
        def body(n):
            i = 3 * n + k
            sib_copy(p, i).wait_recv()
            add_into(grad_piece(2 * p + c, i), whole, sib[p, i])

        loop(0, 4, body)
        for n in range(2):
            xa_copy(p, n, k).start()
            yb_copy(p, n, k).start()

    def first_third(p, k):
        xa_copy(p, 1 - y, k).wait_recv()
        add_into(grad_piece(2 * p + c, 3 * (2 * (1 - y) + x) + k), low, xa[p, 1 - y, k])
        ya_copy(p, k).start()
        yb_copy(p, 1 - x, k).wait_recv()
        add_into(grad_piece(2 * p + c, 3 * (2 * y + 1 - x) + k), high, yb[p, 1 - x, k])
        xb_copy(p, k).start()
        own = grad_piece(2 * p + c, 3 * q + k)
        xa_copy(p, y, k).wait_recv()
        add_into(own, low, xa[p, y, k])
        yb_copy(p, x, k).wait_recv()
        add_into(own, high, yb[p, x, k])

    from_sib = lambda p: loop(0, 3, lambda k: sib_third(p, k))
    first_half = lambda p: loop(0, 3, lambda k: first_third(p, k))

    def z_copy(p, k, h, way):
        piece = grad_piece(2 * p + c, 3 * q + k)
        rows = (low, high)[h]
        return remote(g.at[piece, rows], (zu, zd)[way].at[p, k, rows], z_send.at[way, p, k, h], z_recv.at[way, p, k, h], (me.up, me.down)[way])

    def second_third(p, k):
        own = grad_piece(2 * p + c, 3 * q + k)
        for h in range(2):
            (ya_copy, xb_copy)[h](p, k).wait_recv()
            add_into(own, (low, high)[h], (ya, xb)[h][p, k])

            @pl.when((z == 0) & (p > 0))
            def _():
                z_copy(p, k, h, 0).start()

            @pl.when((z == 3) & (p < 3))
            def _():
                z_copy(p, k, h, 1).start()

    def line_third(p, k):
        own = grad_piece(2 * p + c, 3 * q + k)
        for h in range(2):
            rows = (low, high)[h]

            @pl.when((z > 0) & (z < p))
            def _():
                z_copy(p, k, h, 0).wait_recv()
                add_into(own, rows, zu[p, k, rows])
                z_copy(p, k, h, 0).start()

            @pl.when((z < 3) & (z > p))
            def _():
                z_copy(p, k, h, 1).wait_recv()
                add_into(own, rows, zd[p, k, rows])
                z_copy(p, k, h, 1).start()

    second_half = lambda p: loop(0, 3, lambda k: second_third(p, k))
    along_z = lambda p: loop(0, 3, lambda k: line_third(p, k))

    def share(kind, quarter, k):
        at = 3 * quarter + k
        ref = shard.at[at] if kind < 2 else shard.at[at, (low, high)[kind - 2]]
        to = (me.xn, me.yn, me.xn, me.yn)[kind]
        return remote(ref, ref, g_send.at[kind, k], g_recv.at[kind, k], to)

    def finish(k):
        own = grad_piece(2 * z + c, 3 * q + k)

        for h in range(2):
            rows = (low, high)[h]

            @pl.when(z > 0)
            def _():
                z_copy(z, k, h, 0).wait_recv()
                add_into(own, rows, zu[z, k, rows])

            @pl.when(z < 3)
            def _():
                z_copy(z, k, h, 1).wait_recv()
                add_into(own, rows, zd[z, k, rows])

        shard[3 * q + k] = g[own]
        share(0, q, k).start()
        share(1, q, k).start()


    loads[2].wait()
    cot[...] = jnp.concatenate([cot_ref[...].astype(F32), jnp.zeros((ROWS - real, D), F32)], axis=0).astype(BF16)

    def down_step(j):
        put_block(g, 8 + j, dot_tn(act[j], cot[...]))

        def send(r):
            at = 8 * (j - 1) + r

            @pl.when(at // 12 == 1 - c)
            def _():
                sib_copy(3, at % 12).start()

        loop(0, 8, send)

    loop(1, 4, down_step)
    col_sums(gv, 7, cot[...].astype(F32))

    def act_step(j):
        @pl.when(j == 1)
        def _():
            put_block(g, 8, dot_tn(act[0], cot[...]))
            send_span(1, 2, 4, 8)
            from_sib(3)

        act_grad(j, cot, g, slope, gv, work, low_rows, gn)
        put_block(g, 4 + j, dot_tn(n2[...], low_rows[...]))
        send_span(0, 1, 8 + j, 1)
        send_span(0, 2, 3 * j, 3)
        send_span(1, 1, 3 * j, 3)
        send_span(1, 2, j, 1)

    loop(0, 4, act_step)
    first_half(3)

    def keep_resid(at, value):
        work[at, :] = value
        low_rows[at, :] = value.astype(BF16)

    norm_back(resid, gn, v_ref[5:6, :], lambda at: cot[at, :].astype(F32), keep_resid, gv, 5)
    from_sib(2)
    second_half(3)
    col_sums(gv, 4, low_rows[...].astype(F32))
    grad = dot_nt(low_rows[...], block(g, 3))
    for j in range(6):
        ga[j] = grad[:, LANES * j : LANES * (j + 1)].astype(BF16)
    put_block(g, 3, dot_tn(slabs(att, 0), low_rows[...]))
    send_span(0, 1, 0, 8)

    def attend_back_step(j):
        @pl.when(j == 2)
        def _():
            from_sib(1)
            along_z(3)

        @pl.when(j == 4)
        def _():
            first_half(2)

        attend_back(j, same_of, qkv, lse, ga, gm)

    loop(0, 6, attend_back_step)

    def qkv_back_step(b):
        mixed = slabs(gm, 6 * b)

        @pl.when(b != 1)
        def _():
            gv[pl.ds(2 + b // 2, 1), :] = jnp.sum(mixed.astype(F32), axis=0, keepdims=True)

        add_part(b, gn, dot_nt(mixed, block(g, b)))
        put_block(g, b, dot_tn(n1[...], mixed))
        send_span(0, 0, 4 * b, 4)
        send_span(1, 0, 4 * b, 4)

        @pl.when(b == 0)
        def _():
            second_half(2)
            along_z(2)

        @pl.when(b == 1)
        def _():
            first_half(1)

    loop(0, 3, qkv_back_step)

    def keep_tokens(at, value):
        work[at, :] = value

    norm_back(emb, gn, v_ref[0:1, :], lambda at: work[at, :], keep_tokens, gv, 0)
    tok_copy = pltpu.make_async_copy(work.at[pl.ds(0, real)], gtok_ref, tok_sem)
    tok_copy.start()
    vsum[0] = gv[...]

    def v_turn(n):
        v_step(n).wait_recv()
        vsum[n + 1] = vsum[n] + vpart[n]
        if n < 4:
            v_step(n + 1).start()

    v_step(0).start()
    sib_third(0, 0)
    sib_third(0, 1)
    second_half(1)
    v_turn(0)
    first_third(0, 0)
    sib_third(0, 2)
    line_third(1, 0)
    v_turn(1)
    first_third(0, 1)
    line_third(1, 1)
    second_third(0, 0)
    v_turn(2)
    first_third(0, 2)
    line_third(1, 2)
    second_third(0, 1)
    line_third(0, 0)
    second_third(0, 2)
    line_third(0, 1)
    line_third(0, 2)
    v_turn(3)
    loop(0, 3, finish)

    def pass_on(k):
        share(0, qx, k).wait_recv()
        share(3, qx, k).start()
        share(1, qy, k).wait_recv()
        share(2, qy, k).start()

    loop(0, 3, pass_on)
    v_turn(4)

    def last(k):
        share(2, qd, k).wait_recv()
        share(3, qd, k).wait_recv()

    loop(0, 3, last)

    norms[0] = jnp.zeros((8, LANES), F32)

    def lay(i, stride, first):
        total = norms[0]
        for j in range(6):
            part = shard[i, :, LANES * j : LANES * (j + 1)].astype(F32)
            flat_ref[pl.ds(first + j, PIECE, stride=stride), :] = part
            total = total + jnp.sum((part * part).reshape(PIECE // 8, 8, LANES), axis=0)
        norms[0] = total

    weave(s, lay)

    @pl.when(s == 7)
    def _():
        total = norms[0]
        for j in range(6):
            part = vsum[5, 0:12, LANES * j : LANES * (j + 1)]
            flat_ref[pl.ds(6912 + j, 12, stride=6), :] = part
            total = total + jnp.concatenate([part[0:8] * part[0:8], jnp.zeros((8, LANES), F32)], axis=0)[0:8]
            total = total + jnp.concatenate([part[8:12] * part[8:12], jnp.zeros((4, LANES), F32)], axis=0)
        norms[0] = total

    edge = remote(flat_ref.at[pl.ds(0, TAIL)], flat_ref.at[pl.ds(6912, TAIL)], e_sem.at[0], e_sem.at[1], me.at(me.dp, (s + 7) % 8))

    @pl.when(s > 0)
    def _():
        edge.start()

    def norm_copy(n):
        return remote(norms.at[0], norms.at[n], n_send.at[n], n_recv.at[n], me.at(me.dp, (s + n) % 8))

    for n in range(1, 8):
        norm_copy(n).start()

    def sent_sib(n):
        sib_copy(n // 12, n % 12).wait_send()

    loop(0, 48, sent_sib)

    def sent_plane(n):
        p, k = n // 3, n % 3
        for m in range(2):
            xa_copy(p, m, k).wait_send()
            yb_copy(p, m, k).wait_send()
        ya_copy(p, k).wait_send()
        xb_copy(p, k).wait_send()

        for h in range(2):

            @pl.when(z < p)
            def _():
                z_copy(p, k, h, 0).wait_send()

            @pl.when(z > p)
            def _():
                z_copy(p, k, h, 1).wait_send()

    loop(0, 12, sent_plane)

    def sent_share(k):
        share(0, q, k).wait_send()
        share(1, q, k).wait_send()
        share(2, qy, k).wait_send()
        share(3, qx, k).wait_send()

    loop(0, 3, sent_share)
    for n in range(5):
        v_step(n).wait_send()

    tok_copy.wait()
    total = norms[0]
    for n in range(1, 8):
        norm_copy(n).wait()
        total = total + norms[n]
    norm_ref[...] = total

    @pl.when(s > 0)
    def _():
        edge.wait_send()

    @pl.when(s < 7)
    def _():
        edge.wait_recv()


def step(own, tokens, keep, clip, cotangent):
    dma = pltpu.SemaphoreType.DMA
    anywhere = pl.BlockSpec(memory_space=pl.ANY)
    table = jnp.asarray(position_table())
    return pl.pallas_call(
        step_kernel,
        name="step",
        out_shape=[
            jax.ShapeDtypeStruct(tokens.shape, BF16),
            jax.ShapeDtypeStruct(cotangent.shape, F32),
            jax.ShapeDtypeStruct((FLAT, LANES), F32),
            jax.ShapeDtypeStruct((8, LANES), F32),
        ],
        in_specs=[anywhere, anywhere, VM, VM, anywhere, anywhere],
        out_specs=[VM, anywhere, VM, VM],
        scratch_shapes=[pltpu.VMEM(*k) for k in kept_shapes()]
        + [
            pltpu.VMEM(tokens.shape, BF16),
            pltpu.VMEM(table.shape, BF16),
            pltpu.VMEM(cotangent.shape, BF16),
            pltpu.VMEM((ROWS, 1), jnp.int32),
            pltpu.VMEM((ROWS, 1), jnp.int32),
            pltpu.VMEM((1, ROWS), jnp.int32),
            dma((3,)),
            pltpu.VMEM((ROWS, D), BF16),
            pltpu.VMEM((ROWS, D), F32),
            pltpu.VMEM((ROWS, D), BF16),
            pltpu.VMEM((ROWS, D), F32),
            pltpu.VMEM((6, ROWS, LANES), BF16),
            pltpu.VMEM((18, ROWS, LANES), BF16),
            pltpu.VMEM((16, D), F32),
            pltpu.VMEM((120, PIECE, D), BF16),
            pltpu.VMEM((16, D), F32),
            pltpu.VMEM((TAIL, LANES), F32),
            pltpu.VMEM((TAIL, LANES), F32),
            pltpu.VMEM((4, 12, PIECE, D), BF16),
            pltpu.VMEM((4, 2, 3, HALF, D), BF16),
            pltpu.VMEM((4, 3, HALF, D), BF16),
            pltpu.VMEM((4, 2, 3, HALF, D), BF16),
            pltpu.VMEM((4, 3, HALF, D), BF16),
            pltpu.VMEM((4, 3, PIECE, D), BF16),
            pltpu.VMEM((4, 3, PIECE, D), BF16),
            pltpu.VMEM((12, PIECE, D), BF16),
            pltpu.VMEM((6, 16, D), F32),
            pltpu.VMEM((5, 16, D), F32),
            pltpu.VMEM((8, 8, LANES), F32),
            dma,
            dma((2,)),
            dma((7,)),
            dma,
            dma((2, 4, 3)),
            dma((4, 3)),
            dma((4, 4, 3)),
            dma((4, 4, 3)),
            dma((4, 12)),
            dma((4, 12)),
            dma,
            dma((4, 12)),
            dma((4, 12)),
            dma((2, 4, 2, 3)),
            dma((2, 4, 2, 3)),
            dma((2, 4, 3)),
            dma((2, 4, 3)),
            dma((2, 4, 3, 2)),
            dma((2, 4, 3, 2)),
            dma((4, 3)),
            dma((4, 3)),
            dma((5,)),
            dma((5,)),
            dma((2,)),
            dma((8,)),
            dma((8,)),
        ],
        compiler_params=pltpu.CompilerParams(collective_id=0, has_side_effects=True, vmem_limit_bytes=LIMIT),
    )(own, tokens, keep, clip, table, cotangent)


STEP_ROWS = 1024


def update_kernel(
    flat_ref, norm_ref, param_ref, first_ref, second_ref, layer_ref, tok_ref,
    grad_out, change_out, first_out, second_out, layer_out, tok_out,
):
    layer_out[...] = layer_ref[...]
    tok_out[...] = tok_ref[...]
    s = lax.axis_index("fsdp")
    n = pl.program_id(0)
    rows = param_ref.shape[0]
    grad = flat_ref[pl.ds(n * rows + 9 * s, rows), :]
    squares = jnp.sum(jnp.sum(norm_ref[...], axis=0, keepdims=True), axis=1, keepdims=True)
    factor = jnp.minimum(1.0, 1.0 / (jnp.sqrt(squares) + 1e-06))
    clipped = grad * factor
    new_first = 0.9 * first_ref[...] + 0.1 * clipped
    new_second = 0.999 * second_ref[...] + 0.001 * clipped * clipped
    first_hat = new_first * (1.0 / first_correct)
    second_hat = new_second * (1.0 / second_correct)
    row = s * 6921 + n * rows + lax.broadcasted_iota(jnp.int32, (rows, LANES), 0)
    decay = jnp.where(row < MATS // LANES, 0.05, 0.0)
    step_rate = 0.001 * 0.75**6
    grad_out[...] = grad
    first_out[...] = new_first
    second_out[...] = new_second
    change_out[...] = step_rate * (first_hat / (jnp.sqrt(second_hat) + 1e-08) + decay * param_ref[...])


def update(flat, norm, params, first, second, layer, grad_tokens):
    rows = params.shape[0]
    steps = pl.cdiv(rows, STEP_ROWS)
    spec = pl.BlockSpec((STEP_ROWS, LANES), lambda n: (n, 0))
    token_rows = 8 * pl.cdiv(layer.shape[0], 8 * steps)
    token_spec = pl.BlockSpec((token_rows, D), lambda n: (n, 0))
    return pl.pallas_call(
        update_kernel,
        name="update",
        grid=(steps,),
        out_shape=[jax.ShapeDtypeStruct((rows, LANES), F32)] * 4
        + [jax.ShapeDtypeStruct(layer.shape, BF16), jax.ShapeDtypeStruct(grad_tokens.shape, F32)],
        in_specs=[VM, VM, spec, spec, spec, token_spec, token_spec],
        out_specs=[spec] * 4 + [token_spec] * 2,
        compiler_params=pltpu.CompilerParams(vmem_limit_bytes=LIMIT),
    )(flat, norm, params, first, second, layer, grad_tokens)


def shards(tokens, cotangent, keep_index, clip_ids, flat_params, first_moment, second_moment):
    flat = flat_params.reshape(-1, LANES)
    layer_out, grad_tokens, summed, norm = step(flat, tokens, keep_index, clip_ids, cotangent)
    outs = update(summed, norm, flat, first_moment.reshape(-1, LANES), second_moment.reshape(-1, LANES), layer_out, grad_tokens)
    grad, change, first, second = (o.reshape(-1) for o in outs[:4])
    layer_out, grad_tokens = outs[4:]
    return (layer_out, grad_tokens, grad, change, first, second)


def layer_norm(values, gain_vec, shift_vec):
    row_mean = jnp.mean(values, axis=-1, keepdims=True)
    centered = values - row_mean
    variance = jnp.mean(centered * centered, axis=-1, keepdims=True)
    return centered * lax.rsqrt(variance + 1e-06) * gain_vec + shift_vec


def gelu_exact(values):
    return jax.nn.gelu(values, approximate=False)


def positions(keep_flat):
    quarter = D // 4
    frequency = 1.0 / 10000.0 ** (jnp.arange(quarter).astype(jnp.float32) / quarter)
    row_angle = (keep_flat // GRID).astype(jnp.float32)[:, None] * frequency
    col_angle = (keep_flat % GRID).astype(jnp.float32)[:, None] * frequency
    return jnp.concatenate(
        [jnp.sin(row_angle), jnp.cos(row_angle), jnp.sin(col_angle), jnp.cos(col_angle)], axis=1
    )


def unpack_flat(flat):
    mats = 4 * D * D + 2 * D * FF
    w_qkv = flat[: 3 * D * D].reshape(D, 3 * D)
    w_out = flat[3 * D * D : 4 * D * D].reshape(D, D)
    w_up = flat[4 * D * D : 4 * D * D + D * FF].reshape(D, FF)
    w_down = flat[4 * D * D + D * FF : mats].reshape(FF, D)
    vectors = flat[mats : mats + 8 * D].reshape(8, D)
    bias_up = flat[mats + 8 * D :]
    return (w_qkv, w_out, w_up, w_down, vectors, bias_up)


def split_heads(values):
    return values.reshape(values.shape[0], HEADS, HEAD_DIM).transpose(1, 0, 2)


def join_heads(values):
    return values.transpose(1, 0, 2).reshape(values.shape[1], D)


def product(left, right):
    return jnp.dot(left, right, preferred_element_type=jnp.float32)


def plain_shards(tokens, cotangent, keep_index, clip_ids, flat_params, first_moment, second_moment):
    shard_len = flat_params.shape[0]
    mats = 4 * D * D + 2 * D * FF
    score_scale = HEAD_DIM ** (-0.5)
    sent = flat_params.astype(jnp.bfloat16)
    gathered = lax.all_gather(sent, "fsdp", axis=0, tiled=True)
    w_qkv, w_out, w_up, w_down, vectors_low, bias_up_low = unpack_flat(gathered)
    vectors = vectors_low.astype(jnp.float32)
    bias_up = bias_up_low.astype(jnp.float32)
    embedded = tokens.astype(jnp.float32) + positions(keep_index.reshape(-1))
    normed, norm_back = jax.vjp(layer_norm, embedded, vectors[0], vectors[1])
    normed_low = normed.astype(jnp.bfloat16)
    mixed_qkv = product(normed_low, w_qkv)
    query_low = (mixed_qkv[:, :D] + vectors[2]).astype(jnp.bfloat16)
    key_low = mixed_qkv[:, D : 2 * D].astype(jnp.bfloat16)
    value_low = (mixed_qkv[:, 2 * D :] + vectors[3]).astype(jnp.bfloat16)
    query_heads = split_heads(query_low)
    key_heads = split_heads(key_low)
    value_heads = split_heads(value_low)
    clip_tok = jnp.repeat(clip_ids.reshape(-1), KEEP)
    same_clip = clip_tok[:, None] == clip_tok[None, :]

    def attend(head_item):
        q_head, k_head, v_head = head_item
        scores = jnp.where(same_clip, product(q_head, k_head.T) * score_scale, -1e30)
        row_top = jnp.max(scores, axis=1, keepdims=True)
        weight_exp = jnp.exp(scores - row_top)
        row_total = jnp.sum(weight_exp, axis=1, keepdims=True)
        soft_low = (weight_exp / row_total).astype(jnp.bfloat16)
        return (product(soft_low, v_head), row_top + jnp.log(row_total))

    attended_heads, log_total = lax.map(attend, (query_heads, key_heads, value_heads))
    attended_low = join_heads(attended_heads).astype(jnp.bfloat16)
    resid = embedded + product(attended_low, w_out) + vectors[4]
    normed_two, norm_two_back = jax.vjp(layer_norm, resid, vectors[5], vectors[6])
    normed_two_low = normed_two.astype(jnp.bfloat16)
    pre_act = product(normed_two_low, w_up) + bias_up
    activated, gelu_back = jax.vjp(gelu_exact, pre_act)
    activated_low = activated.astype(jnp.bfloat16)
    layer_out = (resid + product(activated_low, w_down) + vectors[7]).astype(jnp.bfloat16)
    w_qkv, w_out, w_up, w_down, vectors_low, bias_up_low = unpack_flat(
        lax.all_gather(sent, "fsdp", axis=0, tiled=True)
    )
    grad_out = cotangent.astype(jnp.float32)
    grad_w_down = product(activated_low.T, cotangent)
    grad_bias_down = jnp.sum(grad_out, axis=0)
    grad_act = product(cotangent, w_down.T)
    grad_pre_low = gelu_back(grad_act)[0].astype(jnp.bfloat16)
    grad_w_up = product(normed_two_low.T, grad_pre_low)
    grad_bias_up = jnp.sum(grad_pre_low.astype(jnp.float32), axis=0)
    grad_normed_two = product(grad_pre_low, w_up.T)
    grad_resid_norm, grad_gain_two, grad_shift_two = norm_two_back(grad_normed_two)
    grad_resid = grad_out + grad_resid_norm
    grad_branch_low = grad_resid.astype(jnp.bfloat16)
    grad_w_out = product(attended_low.T, grad_branch_low)
    grad_bias_out = jnp.sum(grad_branch_low.astype(jnp.float32), axis=0)
    grad_attended_low = product(grad_branch_low, w_out.T).astype(jnp.bfloat16)

    def attend_back(head_item):
        q_head, k_head, v_head, g_head, lse_head = head_item
        soft = jnp.where(
            same_clip, jnp.exp(product(q_head, k_head.T) * score_scale - lse_head), 0.0
        )
        grad_soft = product(g_head, v_head.T)
        grad_value = product(soft.astype(jnp.bfloat16).T, g_head)
        inner = jnp.sum(soft * grad_soft, axis=1, keepdims=True)
        grad_raw = (score_scale * soft * (grad_soft - inner)).astype(jnp.bfloat16)
        return (product(grad_raw, k_head), product(grad_raw.T, q_head), grad_value)

    grad_query, grad_key, grad_value = lax.map(
        attend_back,
        (query_heads, key_heads, value_heads, split_heads(grad_attended_low), log_total),
    )
    grad_mixed = jnp.concatenate(
        [join_heads(grad_query), join_heads(grad_key), join_heads(grad_value)], axis=1
    ).astype(jnp.bfloat16)
    grad_w_qkv = product(normed_low.T, grad_mixed)
    mixed_sums = jnp.sum(grad_mixed.astype(jnp.float32), axis=0)
    grad_normed = product(grad_mixed, w_qkv.T)
    grad_embedded, grad_gain_one, grad_shift_one = norm_back(grad_normed)
    grad_tokens = grad_resid + grad_embedded
    full_grad = jnp.concatenate(
        [
            grad_w_qkv.reshape(-1),
            grad_w_out.reshape(-1),
            grad_w_up.reshape(-1),
            grad_w_down.reshape(-1),
            grad_gain_one,
            grad_shift_one,
            mixed_sums[:D],
            mixed_sums[2 * D :],
            grad_bias_out,
            grad_gain_two,
            grad_shift_two,
            grad_bias_down,
            grad_bias_up,
        ]
    )
    replicas = lax.axis_size("dp")
    owners = lax.axis_size("fsdp")
    reordered = full_grad.reshape(owners, replicas, -1).transpose(1, 0, 2).reshape(-1)
    own_piece = lax.psum_scatter(reordered, ("dp", "fsdp"), scatter_dimension=0, tiled=True)
    own_grad = lax.all_gather(own_piece.astype(jnp.bfloat16), "dp", axis=0, tiled=True).astype(
        own_piece.dtype
    )
    squares = lax.psum(jnp.sum(own_grad * own_grad), "fsdp")
    clip_factor = jnp.minimum(1.0, 1.0 / (jnp.sqrt(squares) + 1e-06))
    clipped = own_grad * clip_factor
    new_first = 0.9 * first_moment + 0.1 * clipped
    new_second = 0.999 * second_moment + 0.001 * clipped * clipped
    first_hat = new_first / first_correct
    second_hat = new_second / second_correct
    position = lax.axis_index("fsdp") * shard_len + jnp.arange(shard_len, dtype=jnp.int32)
    decay_mask = (position < mats).astype(jnp.float32)
    step_rate = 0.001 * 0.75**6
    param_change = step_rate * (
        first_hat / (jnp.sqrt(second_hat) + 1e-08) + 0.05 * decay_mask * flat_params
    )
    return (layer_out, grad_tokens, own_grad, param_change, new_first, new_second)


def solution(mesh):
    placed = (
        P(("dp", "fsdp"), None),
        P(("dp", "fsdp"), None),
        P(("dp", "fsdp"), None),
        P(("dp", "fsdp"), None),
        P("fsdp"),
        P("fsdp"),
        P("fsdp"),
    )
    staged = mesh.shape["dp"] == 4 and mesh.shape["fsdp"] == 8
    return jax.shard_map(
        shards if staged else plain_shards,
        mesh=mesh,
        in_specs=placed,
        out_specs=(
            P(("dp", "fsdp"), None),
            P(("dp", "fsdp"), None),
            P("fsdp"),
            P("fsdp"),
            P("fsdp"),
            P("fsdp"),
        ),
        check_vma=False,
    )
```

```python
import functools

import jax
import jax.numpy as jnp
import numpy as np
from jax import lax
from jax.experimental import pallas as pl
from jax.experimental.pallas import tpu as pltpu
from jax.sharding import PartitionSpec as P

D = 768
FF = 3072
HEADS = 12
HEAD_DIM = 64
GRID = 14
KEEP = 49
MATS = 4 * D * D + 2 * D * FF

first_correct = 0.9999734386011124
second_correct = 0.09520785288629106

F32 = jnp.float32
BF16 = jnp.bfloat16
MESH = pl.DeviceIdType.MESH
LIMIT = 66_000_000

ROWS = 400
CHUNK = 80
PIECE = 96
PIECES = 12
LANES = 128
TAIL = 72


def div(a, b):
    return a // b if isinstance(a, int) else lax.div(a, np.int32(b))


def ge(s, k):
    return div(s + 8 - k, 8)


def piece_of(s, i):
    g5, by3, by4, by8 = div(i + 4, 8), div(i, 3), div(i, 4), div(i, 8)
    forms = (
        4 * by4 + i,
        4 * by4 + 4 + i,
        24 + i + by8 * (7 * i - 56),
        33 + 5 * by3 + i,
        36 + 5 * by3 + i,
        (1 - g5) * (39 + 8 * i) + g5 * (60 + i),
        72 + i,
        84 + i,
    )
    out = forms[0]
    for k in range(1, 8):
        out = out + ge(s, k) * (forms[k] - forms[k - 1])
    return out


def grad_piece(s, i):
    return piece_of(s, i) + 24 * ge(s, 6)


def grad_block(b):
    return 8 * b + 24 * div(b + 7, 16)


ARRIVALS = (
    ((1, 0), (1, 1), (1, 2), (2, 0), (2, 1), (2, 2), (3, 0), (3, 1), (3, 2)),
    ((0, 0), (0, 1), (0, 2), (2, 0), (2, 1), (2, 2), (3, 0), (3, 1), (3, 2)),
    ((3, 0), (1, 0), (0, 0), (0, 1), (0, 2), (1, 1), (1, 2), (3, 1), (3, 2)),
    ((2, 0), (1, 0), (0, 0), (0, 1), (0, 2), (1, 1), (1, 2), (2, 1), (2, 2)),
)


def arrival(z, n):
    out = []
    for m in range(2):
        row = [ARRIVALS[plane][n][m] for plane in range(4)]
        value = row[0]
        for plane in range(1, 4):
            value = value + (row[plane] - row[plane - 1]) * div(z + 4 - plane, 4)
        out.append(value)
    return out


def dot(a, b):
    return lax.dot_general(a, b, (((1,), (0,)), ((), ())), preferred_element_type=F32)


def dot_nt(a, b):
    return lax.dot_general(a, b, (((1,), (1,)), ((), ())), preferred_element_type=F32)


def dot_tn(a, b):
    return lax.dot_general(a, b, (((0,), (0,)), ((), ())), preferred_element_type=F32)


def loop(start, stop, body):
    def step(i, carry):
        body(i)
        return carry

    lax.fori_loop(start, stop, step, 0)


def chunks(body):
    loop(0, ROWS // CHUNK, lambda n: body(pl.ds(pl.multiple_of(n * CHUNK, CHUNK), CHUNK)))


class Place:
    def __init__(self):
        self.dp = lax.axis_index("dp")
        self.s = lax.axis_index("fsdp")
        self.x, self.y = self.dp % 2, self.dp // 2
        self.z, self.c = self.s // 2, self.s % 2
        self.sib = self.at(self.dp, self.s + 1 - 2 * self.c)
        self.xn = self.at(self.dp + 1 - 2 * self.x, self.s)
        self.yn = self.at(self.dp + 2 - 4 * self.y, self.s)
        self.up = self.at(self.dp, self.s + 2)
        self.down = self.at(self.dp, self.s - 2)

    def at(self, dp, s):
        return (dp, s)

    def barrier(self):
        sem = pltpu.get_barrier_semaphore()
        for n in range(1, 8):
            pl.semaphore_signal(sem, inc=1, device_id=self.at(self.dp, (self.s + n) % 8), device_id_type=MESH)
        for peer in (self.xn, self.yn):
            pl.semaphore_signal(sem, inc=1, device_id=peer, device_id_type=MESH)
        pl.semaphore_wait(sem, 9)


def remote(src, dst, send, recv, to):
    return pltpu.make_async_remote_copy(
        src_ref=src, dst_ref=dst, send_sem=send, recv_sem=recv, device_id=to, device_id_type=MESH
    )


def weave(s, body):
    @pl.when(s <= 1)
    def _():
        loop(0, 12, lambda i: body(i, 18, (i % 4) * (96 * 18) + (i // 4) * 6))

    @pl.when(s == 2)
    def _():
        loop(0, 8, lambda i: body(i, 6, i * (96 * 6)))
        loop(8, 12, lambda i: body(i, 24, 4608 + (i - 8) * 6))

    @pl.when((s == 3) | (s == 4))
    def _():
        loop(0, 12, lambda i: body(i, 24, (i % 3) * (96 * 24) + (i // 3) * 6))

    @pl.when(s == 5)
    def _():
        loop(0, 4, lambda i: body(i, 24, i * 6))
        loop(4, 12, lambda i: body(i, 6, 2304 + (i - 4) * (96 * 6)))

    @pl.when(s >= 6)
    def _():
        loop(0, 12, lambda i: body(i, 6, i * (96 * 6)))


def position_table():
    quarter = D // 4
    exponent = np.arange(quarter, dtype=np.float32) / np.float32(quarter)
    frequency = np.float32(1.0) / np.power(np.float32(10000.0), exponent).astype(np.float32)
    angle = (np.arange(GRID, dtype=np.float32)[:, None] * frequency).astype(np.float64)
    waves = np.concatenate([np.sin(angle), np.cos(angle)], axis=1).astype(np.float32)
    table = np.zeros((32, D), np.float32)
    table[:GRID, : D // 2] = waves
    table[16 : 16 + GRID, D // 2 :] = waves
    parts = []
    for _ in range(3):
        part = table.astype(jnp.bfloat16)
        parts.append(part)
        table = table - part.astype(np.float32)
    return np.stack(parts)


def norm_stats(v):
    mean = jnp.mean(v, axis=-1, keepdims=True)
    centered = v - mean
    rstd = lax.rsqrt(jnp.mean(centered * centered, axis=-1, keepdims=True) + 1e-06)
    return centered * rstd, rstd


def block(g_ref, b):
    return g_ref[pl.ds(8 * b, 8)].reshape(D, D)


def slabs(ref, first):
    return jnp.concatenate([ref[first + j] for j in range(6)], axis=1)


def place_tokens(keep_ref, clip_ref, keep_col, clip_col, clip_row):
    token = lax.broadcasted_iota(jnp.int32, (ROWS, KEEP), 0)
    lane = lax.broadcasted_iota(jnp.int32, (ROWS, KEEP), 1)
    down = lax.broadcasted_iota(jnp.int32, (ROWS, 1), 0)
    across = lax.broadcasted_iota(jnp.int32, (1, ROWS), 1)
    patches = jnp.zeros((ROWS, KEEP), F32)
    col = jnp.full((ROWS, 1), -1, jnp.int32)
    row = jnp.full((1, ROWS), -1, jnp.int32)
    for i in range(keep_ref.shape[0]):
        first, last = KEEP * i, KEEP * i + KEEP
        patches = jnp.where(token == lane + first, keep_ref[i : i + 1, :].astype(F32), patches)
        clip = clip_ref[0:1, i : i + 1]
        col = jnp.where((down >= first) & (down < last), clip, col)
        row = jnp.where((across >= first) & (across < last), clip, row)
    keep_col[...] = jnp.sum(patches, axis=1, keepdims=True).astype(jnp.int32)
    clip_col[...] = col
    clip_row[...] = row


def embed(tok_ref, keep_ref, table_ref, emb):
    real = tok_ref.shape[0]
    emb[0:real, :] = tok_ref[...].astype(F32)
    emb[real:, :] = jnp.zeros((ROWS - real, D), F32)

    def body(at):
        keep = keep_ref[at, :]
        row = (keep * 4682) >> 16
        col = keep - GRID * row + 16
        lane = lax.broadcasted_iota(jnp.int32, (CHUNK, 32), 1)
        hot = jnp.where((lane == row) | (lane == col), 1.0, 0.0).astype(BF16)
        spot = dot(hot, table_ref[0]) + (dot(hot, table_ref[1]) + dot(hot, table_ref[2]))
        emb[at, :] = emb[at, :] + spot

    chunks(body)


def norm_one(emb, v_ref, n1):
    gain, shift = v_ref[0:1, :], v_ref[1:2, :]

    def body(at):
        n1[at, :] = (norm_stats(emb[at, :])[0] * gain + shift).astype(BF16)

    chunks(body)


def project(b, n1, g_ref, v_ref, qkv):
    mixed = dot(n1[...], block(g_ref, b)) + v_ref[pl.ds(2 + b // 2, 1), :] * jnp.where(b == 1, 0.0, 1.0)
    for j in range(6):
        qkv[6 * b + j] = mixed[:, LANES * j : LANES * (j + 1)].astype(BF16)


def attend(j, same_of, qkv, att, lse):
    query, key, value = qkv[j], qkv[6 + j], qkv[12 + j]
    first = lax.broadcasted_iota(jnp.int32, (ROWS, LANES), 1) < HEAD_DIM
    turned = value.T
    parts = []
    for h in range(2):
        own = jnp.where(first if h == 0 else ~first, query, jnp.zeros_like(query))
        scores = jnp.where(same_of(), dot_nt(key, own) * 0.125, -1e30)
        top = jnp.max(scores, axis=0, keepdims=True)
        weight = jnp.exp(scores - top)
        total = jnp.sum(weight, axis=0, keepdims=True)
        soft = (weight * (1.0 / total)).astype(BF16)
        lse[2 * j + h] = top + jnp.log(total)
        parts.append(dot(turned[HEAD_DIM * h : HEAD_DIM * (h + 1), :], soft))
    att[j] = jnp.concatenate(parts, axis=0).T.astype(BF16)


def out_project(att, g_ref, v_ref, emb, resid, n2):
    resid[...] = dot(slabs(att, 0), block(g_ref, 3))
    bias, gain, shift = v_ref[4:5, :], v_ref[5:6, :], v_ref[6:7, :]

    def body(at):
        value = emb[at, :] + resid[at, :] + bias
        resid[at, :] = value
        n2[at, :] = (norm_stats(value)[0] * gain + shift).astype(BF16)

    chunks(body)


def expand(j, n2, g_ref, v_ref, work, act, slope):
    work[...] = dot(n2[...], block(g_ref, 4 + j))

    def body(at):
        pre = work[at, :] + v_ref[pl.ds(8 + j, 1), :]
        phi = 0.5 * (1.0 + lax.erf(pre * 0.7071067811865476))
        act[j, at, :] = (pre * phi).astype(BF16)
        slope[j, at, :] = (phi + pre * (0.3989422804014327 * jnp.exp(-0.5 * pre * pre))).astype(BF16)

    chunks(body)


def contract(j, act, g_ref, work):
    add_part(j, work, dot(act[j], block(g_ref, 8 + j)))


def kept_shapes():
    return [
        ((ROWS, D), F32),
        ((ROWS, D), BF16),
        ((18, ROWS, LANES), BF16),
        ((6, ROWS, LANES), BF16),
        ((HEADS, 1, ROWS), F32),
        ((ROWS, D), F32),
        ((ROWS, D), BF16),
        ((4, ROWS, D), BF16),
        ((4, ROWS, D), BF16),
    ]


VM = pl.BlockSpec(memory_space=pltpu.VMEM)


def col_sums(dest, row, source):
    dest[row : row + 1, :] = jnp.sum(source, axis=0, keepdims=True)


def put_block(gw, b, value):
    gw[pl.ds(grad_block(b), 8)] = value.astype(BF16).reshape(8, PIECE, D)


def act_grad(j, cot, g_ref, slope, gv, work, pre_low, gn):
    work[...] = dot_nt(cot[...], block(g_ref, 8 + j))
    total = jnp.zeros((8, D), F32)

    def body(n, total):
        at = pl.ds(pl.multiple_of(n * CHUNK, CHUNK), CHUNK)
        low = (slope[j, at, :].astype(F32) * work[at, :]).astype(BF16)
        pre_low[at, :] = low
        return total + jnp.sum(low.astype(F32).reshape(CHUNK // 8, 8, D), axis=0)

    total = lax.fori_loop(0, ROWS // CHUNK, body, total)
    gv[pl.ds(8 + j, 1), :] = jnp.sum(total, axis=0, keepdims=True)
    add_part(j, gn, dot_nt(pre_low[...], block(g_ref, 4 + j)))


def add_part(j, total, part):
    @pl.when(j == 0)
    def _():
        total[...] = part

    @pl.when(j > 0)
    def _():
        total[...] += part


def norm_back(value_ref, gn, gain, extra, store, gv, row):
    def body(n, sums):
        at = pl.ds(pl.multiple_of(n * CHUNK, CHUNK), CHUNK)
        hat, rstd = norm_stats(value_ref[at, :])
        grad = gn[at, :]
        fold = lambda v: jnp.sum(v.reshape(CHUNK // 8, 8, D), axis=0)
        sums = (sums[0] + fold(grad * hat), sums[1] + fold(grad))
        grad = grad * gain
        inner = jnp.mean(grad * hat, axis=-1, keepdims=True)
        store(at, extra(at) + rstd * (grad - jnp.mean(grad, axis=-1, keepdims=True) - hat * inner))
        return sums

    zero = jnp.zeros((8, D), F32)
    one, two = lax.fori_loop(0, ROWS // CHUNK, body, (zero, zero))
    gv[row : row + 1, :] = jnp.sum(one, axis=0, keepdims=True)
    gv[row + 1 : row + 2, :] = jnp.sum(two, axis=0, keepdims=True)


def attend_back(j, same_of, qkv, lse, ga, gm):
    query, key, value, grad = qkv[j], qkv[6 + j], qkv[12 + j], ga[j]
    first = lax.broadcasted_iota(jnp.int32, (ROWS, LANES), 1) < HEAD_DIM
    turned = key.T
    parts, grad_key, grad_value = [], None, None
    for h in range(2):
        mine = first if h == 0 else ~first
        own = jnp.where(mine, query, jnp.zeros_like(query))
        own_grad = jnp.where(mine, grad, jnp.zeros_like(grad))
        soft = jnp.where(same_of(), jnp.exp(dot_nt(key, own) * 0.125 - lse[2 * j + h]), 0.0)
        grad_soft = dot_nt(value, own_grad)
        inner = jnp.sum(soft * grad_soft, axis=0, keepdims=True)
        raw = (0.125 * soft * (grad_soft - inner)).astype(BF16)
        one = dot(soft.astype(BF16), own_grad)
        two = dot(raw, own)
        grad_value = one if h == 0 else grad_value + one
        grad_key = two if h == 0 else grad_key + two
        parts.append(dot(turned[HEAD_DIM * h : HEAD_DIM * (h + 1), :], raw))
    gm[j] = jnp.concatenate(parts, axis=0).T.astype(BF16)
    gm[6 + j] = grad_key.astype(BF16)
    gm[12 + j] = grad_value.astype(BF16)


FLAT = 7240
HALF = PIECE // 2


def step_kernel(own_hbm, tok_hbm, keep_ref, clip_ref, table_hbm, cot_hbm, *refs):
    out_ref, gtok_ref, flat_ref, norm_ref = refs[:4]
    emb, n1, qkv, att, lse, resid, n2, act, slope = refs[4:13]
    (
        tok_ref, table_ref, cot_ref, keep_col, clip_col, clip_row, in_sem,
        cot, work, low_rows, gn, ga, gm, gv, g, v_ref, tail, vbuf,
        sib, xa, ya, yb, xb, zu, zd, shard, vsum, vpart, norms,
        own_sem, edge_sem, gv_send, gv_recv, gz_send, gz_recv, gp_send, gp_recv, gc_send, gc_recv, tok_sem,
        sib_send, sib_recv, h_send, h_recv, t_send, t_recv, z_send, z_recv, g_send, g_recv, v_send, v_recv, e_sem, n_send, n_recv,
    ) = refs[13:]
    me = Place()
    s, z, c, x, y = me.s, me.z, me.c, me.x, me.y
    q = me.dp
    qx, qy, qd = q + 1 - 2 * x, q + 2 - 4 * y, 3 - q
    rows = own_hbm.shape[0]
    real = cot_ref.shape[0]

    own_copy = pltpu.make_async_copy(own_hbm, flat_ref.at[pl.ds(TAIL, rows)], own_sem)
    own_copy.start()
    loads = [
        pltpu.make_async_copy(src, dst, in_sem.at[n])
        for n, (src, dst) in enumerate(((tok_hbm, tok_ref), (table_hbm, table_ref), (cot_hbm, cot_ref)))
    ]
    for load in loads:
        load.start()
    gv[...] = jnp.zeros_like(gv)
    me.barrier()
    own_copy.wait()
    tail[...] = flat_ref[rows : rows + TAIL, :]
    edge = remote(tail, flat_ref.at[pl.ds(0, TAIL)], edge_sem.at[0], edge_sem.at[1], me.at(me.dp, (s + 1) % 8))

    @pl.when(s < 7)
    def _():
        edge.start()

    @pl.when(s == 7)
    def _():
        for n in range(7):
            remote(tail, vbuf, gv_send.at[n], gv_recv, me.at(me.dp, n)).start()
        vbuf[...] = tail[...]

    place_tokens(keep_ref, clip_ref, keep_col, clip_col, clip_row)
    loads[0].wait()
    loads[1].wait()
    embed(tok_ref, keep_col, table_ref, emb)

    @pl.when(s > 0)
    def _():
        edge.wait_recv()

    def to_sib(p, i):
        piece = piece_of(2 * p + c, i)
        return remote(g.at[piece], g.at[piece], gc_send.at[p, i], gc_recv.at[p, i], me.sib)

    def line_copy(p, k, way):
        piece = piece_of(2 * p + c, q + 4 * k)
        return remote(g.at[piece], g.at[piece], gz_send.at[way, p, k], gz_recv.at[p, k], (me.up, me.down)[way])

    def plane_copy(kind, p, quarter, k):
        piece = piece_of(2 * p + c, quarter + 4 * k)
        ref = g.at[piece]
        if kind >= 2:
            ref = g.at[piece, pl.ds(HALF * (kind - 2), HALF)]
        return remote(ref, ref, gp_send.at[kind, p, k], gp_recv.at[kind, p, k], (me.xn, me.yn)[kind % 2])

    def place_piece(i, stride, first):
        piece = piece_of(s, i)
        for j in range(6):
            g[piece, :, LANES * j : LANES * (j + 1)] = flat_ref[pl.ds(TAIL - 9 * s + first + j, PIECE, stride=stride), :].astype(BF16)

    weave(s, place_piece)
    flat_ref[6912:, :] = jnp.zeros((FLAT - 6912, LANES), F32)

    def own_up(k):
        line_copy(z, k, 0).start()

    @pl.when(z < 3)
    def _():
        own_up(0)

    @pl.when(z > 0)
    def _():
        loop(0, 3, lambda k: line_copy(z, k, 1).start())

    @pl.when(z == 0)
    def _():
        loop(1, 3, own_up)

    loop(0, 12, lambda i: to_sib(z, i).start())

    @pl.when(s < 7)
    def _():
        remote(tail, vbuf, gv_send.at[0], gv_recv, me.sib).wait_recv()

    for j in range(6):
        v_ref[0:12, LANES * j : LANES * (j + 1)] = vbuf[pl.ds(j, 12, stride=6), :].astype(BF16).astype(F32)

    def line_step(n):
        p, k = arrival(z, n)

        @pl.when(p < z)
        def _():
            line_copy(p, k, 0).wait_recv()

            @pl.when(z < 3)
            def _():
                line_copy(p, k, 0).start()

        @pl.when(p > z)
        def _():
            line_copy(p, k, 1).wait_recv()

            @pl.when(z > 0)
            def _():
                line_copy(p, k, 1).start()

        plane_copy(0, p, q, k).start()
        plane_copy(1, p, q, k).start()
        to_sib(p, q + 4 * k).start()
        if n in (2, 6):

            @pl.when(z == (1 if n == 2 else 2))
            def _():
                loop(1, 3, own_up)

    def plane_step(n):
        p, k = arrival(z, n)
        plane_copy(0, p, qx, k).wait_recv()
        plane_copy(3, p, qx, k).start()
        to_sib(p, qx + 4 * k).start()
        plane_copy(1, p, qy, k).wait_recv()
        plane_copy(2, p, qy, k).start()
        to_sib(p, qy + 4 * k).start()

    def far_step(n):
        p, k = arrival(z, n)
        plane_copy(2, p, qd, k).wait_recv()
        plane_copy(3, p, qd, k).wait_recv()
        to_sib(p, qd + 4 * k).start()

    def have(p, k):
        for quarter in range(4):
            to_sib(p, quarter + 4 * k).wait_recv()

    same_of = lambda: clip_col[...] == clip_row[...]
    norm_one(emb, v_ref, n1)
    line_step(0)
    line_step(1)
    plane_step(0)
    line_step(2)
    plane_step(1)
    line_step(3)
    far_step(0)
    line_step(4)
    plane_step(2)
    far_step(1)
    line_step(5)
    plane_step(3)
    line_step(6)
    far_step(2)

    def qkv_step(b):
        @pl.when(b == 1)
        def _():
            line_step(7)
            plane_step(4)
            far_step(3)

        @pl.when(b == 2)
        def _():
            line_step(8)
            plane_step(5)
            far_step(4)

        have(0, b)
        project(b, n1, g, v_ref, qkv)

    loop(0, 3, qkv_step)

    def attend_step(j):
        @pl.when(j == 3)
        def _():
            plane_step(6)
            far_step(5)

        attend(j, same_of, qkv, att, lse)

    loop(0, 6, attend_step)
    plane_step(7)
    far_step(6)
    have(1, 0)
    have(1, 1)
    out_project(att, g, v_ref, emb, resid, n2)
    have(1, 2)

    def expand_step(j):
        @pl.when(j == 1)
        def _():
            plane_step(8)
            far_step(7)

        @pl.when(j == 2)
        def _():
            far_step(8)

        @pl.when(j < 3)
        def _():
            have(2, j)

        expand(j, n2, g, v_ref, work, act, slope)

    loop(0, 4, expand_step)
    for k in range(3):
        have(3, k)
    loop(0, 4, lambda j: contract(j, act, g, work))
    out_ref[...] = (resid[0:real, :] + work[0:real, :] + v_ref[7:8, :]).astype(BF16)

    @pl.when(s < 7)
    def _():
        edge.wait_send()

    @pl.when(s == 7)
    def _():
        for n in range(7):
            remote(tail, vbuf, gv_send.at[n], gv_recv, me.sib).wait_send()

    def line_sent(p, k):
        @pl.when((p <= z) & (z < 3))
        def _():
            line_copy(p, k, 0).wait_send()

        @pl.when((p >= z) & (z > 0))
        def _():
            line_copy(p, k, 1).wait_send()

        @pl.when(p != z)
        def _():
            plane_copy(0, p, q, k).wait_send()
            plane_copy(1, p, q, k).wait_send()
            plane_copy(2, p, qy, k).wait_send()
            plane_copy(3, p, qx, k).wait_send()

    loop(0, 12, lambda n: line_sent(n // 3, n % 3))
    loop(0, 48, lambda n: to_sib(n // 12, n % 12).wait_send())

    def add_into(piece, rows, got):
        g[piece, rows, :] = (g[piece, rows, :].astype(F32) + got.astype(F32)).astype(BF16)

    low, high, whole = pl.ds(0, HALF), pl.ds(HALF, HALF), pl.ds(0, PIECE)

    def sib_copy(p, i):
        piece = grad_piece(2 * p + 1 - c, i)
        return remote(g.at[piece], sib.at[p, i], sib_send.at[p, i], sib_recv.at[p, i], me.sib)

    def send_span(parity, p, first, count):
        @pl.when(c == 1 - parity)
        def _():
            loop(0, count, lambda r: sib_copy(p, first + r).start())

    partners = (me.sib, me.xn, me.yn, me.at(me.dp, (s + 2 - 4 * (z % 2)) % 8), me.at(me.dp, (s + 4) % 8))

    def v_step(n):
        copy = remote(vsum.at[n], vpart.at[n], v_send.at[n], v_recv.at[n], partners[n])
        return copy

    def xa_copy(p, yy, k):
        piece = grad_piece(2 * p + c, 3 * (2 * yy + 1 - x) + k)
        return remote(g.at[piece, low], xa.at[p, yy, k], h_send.at[0, p, yy, k], h_recv.at[0, p, yy, k], me.xn)

    def yb_copy(p, xx, k):
        piece = grad_piece(2 * p + c, 3 * (2 * (1 - y) + xx) + k)
        return remote(g.at[piece, high], yb.at[p, xx, k], h_send.at[1, p, xx, k], h_recv.at[1, p, xx, k], me.yn)

    def ya_copy(p, k):
        piece = grad_piece(2 * p + c, 3 * (2 * (1 - y) + x) + k)
        return remote(g.at[piece, low], ya.at[p, k], t_send.at[0, p, k], t_recv.at[0, p, k], me.yn)

    def xb_copy(p, k):
        piece = grad_piece(2 * p + c, 3 * (2 * y + 1 - x) + k)
        return remote(g.at[piece, high], xb.at[p, k], t_send.at[1, p, k], t_recv.at[1, p, k], me.xn)

    def sib_third(p, k):
        def body(n):
            i = 3 * n + k
            sib_copy(p, i).wait_recv()
            add_into(grad_piece(2 * p + c, i), whole, sib[p, i])

        loop(0, 4, body)
        for n in range(2):
            xa_copy(p, n, k).start()
            yb_copy(p, n, k).start()

    def first_third(p, k):
        xa_copy(p, 1 - y, k).wait_recv()
        add_into(grad_piece(2 * p + c, 3 * (2 * (1 - y) + x) + k), low, xa[p, 1 - y, k])
        ya_copy(p, k).start()
        yb_copy(p, 1 - x, k).wait_recv()
        add_into(grad_piece(2 * p + c, 3 * (2 * y + 1 - x) + k), high, yb[p, 1 - x, k])
        xb_copy(p, k).start()
        own = grad_piece(2 * p + c, 3 * q + k)
        xa_copy(p, y, k).wait_recv()
        add_into(own, low, xa[p, y, k])
        yb_copy(p, x, k).wait_recv()
        add_into(own, high, yb[p, x, k])

    from_sib = lambda p: loop(0, 3, lambda k: sib_third(p, k))
    first_half = lambda p: loop(0, 3, lambda k: first_third(p, k))

    def z_copy(p, k, h, way):
        piece = grad_piece(2 * p + c, 3 * q + k)
        rows = (low, high)[h]
        return remote(g.at[piece, rows], (zu, zd)[way].at[p, k, rows], z_send.at[way, p, k, h], z_recv.at[way, p, k, h], (me.up, me.down)[way])

    def second_third(p, k):
        own = grad_piece(2 * p + c, 3 * q + k)
        for h in range(2):
            (ya_copy, xb_copy)[h](p, k).wait_recv()
            add_into(own, (low, high)[h], (ya, xb)[h][p, k])

            @pl.when((z == 0) & (p > 0))
            def _():
                z_copy(p, k, h, 0).start()

            @pl.when((z == 3) & (p < 3))
            def _():
                z_copy(p, k, h, 1).start()

    def line_third(p, k):
        own = grad_piece(2 * p + c, 3 * q + k)
        for h in range(2):
            rows = (low, high)[h]

            @pl.when((z > 0) & (z < p))
            def _():
                z_copy(p, k, h, 0).wait_recv()
                add_into(own, rows, zu[p, k, rows])
                z_copy(p, k, h, 0).start()

            @pl.when((z < 3) & (z > p))
            def _():
                z_copy(p, k, h, 1).wait_recv()
                add_into(own, rows, zd[p, k, rows])
                z_copy(p, k, h, 1).start()

    second_half = lambda p: loop(0, 3, lambda k: second_third(p, k))
    along_z = lambda p: loop(0, 3, lambda k: line_third(p, k))

    def share(kind, quarter, k):
        at = 3 * quarter + k
        ref = shard.at[at] if kind < 2 else shard.at[at, (low, high)[kind - 2]]
        to = (me.xn, me.yn, me.xn, me.yn)[kind]
        return remote(ref, ref, g_send.at[kind, k], g_recv.at[kind, k], to)

    def finish(k):
        own = grad_piece(2 * z + c, 3 * q + k)

        for h in range(2):
            rows = (low, high)[h]

            @pl.when(z > 0)
            def _():
                z_copy(z, k, h, 0).wait_recv()
                add_into(own, rows, zu[z, k, rows])

            @pl.when(z < 3)
            def _():
                z_copy(z, k, h, 1).wait_recv()
                add_into(own, rows, zd[z, k, rows])

        shard[3 * q + k] = g[own]
        share(0, q, k).start()
        share(1, q, k).start()


    loads[2].wait()
    cot[...] = jnp.concatenate([cot_ref[...].astype(F32), jnp.zeros((ROWS - real, D), F32)], axis=0).astype(BF16)

    def down_step(j):
        put_block(g, 8 + j, dot_tn(act[j], cot[...]))

        def send(r):
            at = 8 * (j - 1) + r

            @pl.when(at // 12 == 1 - c)
            def _():
                sib_copy(3, at % 12).start()

        loop(0, 8, send)

    loop(1, 4, down_step)
    col_sums(gv, 7, cot[...].astype(F32))

    def act_step(j):
        @pl.when(j == 1)
        def _():
            put_block(g, 8, dot_tn(act[0], cot[...]))
            send_span(1, 2, 4, 8)
            from_sib(3)

        act_grad(j, cot, g, slope, gv, work, low_rows, gn)
        put_block(g, 4 + j, dot_tn(n2[...], low_rows[...]))
        send_span(0, 1, 8 + j, 1)
        send_span(0, 2, 3 * j, 3)
        send_span(1, 1, 3 * j, 3)
        send_span(1, 2, j, 1)

    loop(0, 4, act_step)
    first_half(3)

    def keep_resid(at, value):
        work[at, :] = value
        low_rows[at, :] = value.astype(BF16)

    norm_back(resid, gn, v_ref[5:6, :], lambda at: cot[at, :].astype(F32), keep_resid, gv, 5)
    from_sib(2)
    second_half(3)
    col_sums(gv, 4, low_rows[...].astype(F32))
    grad = dot_nt(low_rows[...], block(g, 3))
    for j in range(6):
        ga[j] = grad[:, LANES * j : LANES * (j + 1)].astype(BF16)
    put_block(g, 3, dot_tn(slabs(att, 0), low_rows[...]))
    send_span(0, 1, 0, 8)

    def attend_back_step(j):
        @pl.when(j == 2)
        def _():
            from_sib(1)
            along_z(3)

        @pl.when(j == 4)
        def _():
            first_half(2)

        attend_back(j, same_of, qkv, lse, ga, gm)

    loop(0, 6, attend_back_step)

    def qkv_back_step(b):
        mixed = slabs(gm, 6 * b)

        @pl.when(b != 1)
        def _():
            gv[pl.ds(2 + b // 2, 1), :] = jnp.sum(mixed.astype(F32), axis=0, keepdims=True)

        add_part(b, gn, dot_nt(mixed, block(g, b)))
        put_block(g, b, dot_tn(n1[...], mixed))
        send_span(0, 0, 4 * b, 4)
        send_span(1, 0, 4 * b, 4)

        @pl.when(b == 0)
        def _():
            second_half(2)
            along_z(2)

        @pl.when(b == 1)
        def _():
            first_half(1)

    loop(0, 3, qkv_back_step)

    def keep_tokens(at, value):
        work[at, :] = value

    norm_back(emb, gn, v_ref[0:1, :], lambda at: work[at, :], keep_tokens, gv, 0)
    tok_copy = pltpu.make_async_copy(work.at[pl.ds(0, real)], gtok_ref, tok_sem)
    tok_copy.start()
    vsum[0] = gv[...]

    def v_turn(n):
        v_step(n).wait_recv()
        vsum[n + 1] = vsum[n] + vpart[n]
        if n < 4:
            v_step(n + 1).start()

    v_step(0).start()
    sib_third(0, 0)
    sib_third(0, 1)
    second_half(1)
    v_turn(0)
    first_third(0, 0)
    sib_third(0, 2)
    line_third(1, 0)
    v_turn(1)
    first_third(0, 1)
    line_third(1, 1)
    second_third(0, 0)
    v_turn(2)
    first_third(0, 2)
    line_third(1, 2)
    second_third(0, 1)
    line_third(0, 0)
    second_third(0, 2)
    line_third(0, 1)
    line_third(0, 2)
    v_turn(3)
    loop(0, 3, finish)

    def pass_on(k):
        share(0, qx, k).wait_recv()
        share(3, qx, k).start()
        share(1, qy, k).wait_recv()
        share(2, qy, k).start()

    loop(0, 3, pass_on)
    v_turn(4)

    def last(k):
        share(2, qd, k).wait_recv()
        share(3, qd, k).wait_recv()

    loop(0, 3, last)

    norms[0] = jnp.zeros((8, LANES), F32)

    def lay(i, stride, first):
        total = norms[0]
        for j in range(6):
            part = shard[i, :, LANES * j : LANES * (j + 1)].astype(F32)
            flat_ref[pl.ds(first + j, PIECE, stride=stride), :] = part
            total = total + jnp.sum((part * part).reshape(PIECE // 8, 8, LANES), axis=0)
        norms[0] = total

    weave(s, lay)

    @pl.when(s == 7)
    def _():
        total = norms[0]
        for j in range(6):
            part = vsum[5, 0:12, LANES * j : LANES * (j + 1)]
            flat_ref[pl.ds(6912 + j, 12, stride=6), :] = part
            total = total + jnp.concatenate([part[0:8] * part[0:8], jnp.zeros((8, LANES), F32)], axis=0)[0:8]
            total = total + jnp.concatenate([part[8:12] * part[8:12], jnp.zeros((4, LANES), F32)], axis=0)
        norms[0] = total

    edge = remote(flat_ref.at[pl.ds(0, TAIL)], flat_ref.at[pl.ds(6912, TAIL)], e_sem.at[0], e_sem.at[1], me.at(me.dp, (s + 7) % 8))

    @pl.when(s > 0)
    def _():
        edge.start()

    def norm_copy(n):
        return remote(norms.at[0], norms.at[n], n_send.at[n], n_recv.at[n], me.at(me.dp, (s + n) % 8))

    for n in range(1, 8):
        norm_copy(n).start()

    def sent_sib(n):
        sib_copy(n // 12, n % 12).wait_send()

    loop(0, 48, sent_sib)

    def sent_plane(n):
        p, k = n // 3, n % 3
        for m in range(2):
            xa_copy(p, m, k).wait_send()
            yb_copy(p, m, k).wait_send()
        ya_copy(p, k).wait_send()
        xb_copy(p, k).wait_send()

        for h in range(2):

            @pl.when(z < p)
            def _():
                z_copy(p, k, h, 0).wait_send()

            @pl.when(z > p)
            def _():
                z_copy(p, k, h, 1).wait_send()

    loop(0, 12, sent_plane)

    def sent_share(k):
        share(0, q, k).wait_send()
        share(1, q, k).wait_send()
        share(2, qy, k).wait_send()
        share(3, qx, k).wait_send()

    loop(0, 3, sent_share)
    for n in range(5):
        v_step(n).wait_send()

    tok_copy.wait()
    total = norms[0]
    for n in range(1, 8):
        norm_copy(n).wait()
        total = total + norms[n]
    norm_ref[...] = total

    @pl.when(s > 0)
    def _():
        edge.wait_send()

    @pl.when(s < 7)
    def _():
        edge.wait_recv()


def step(own, tokens, keep, clip, cotangent):
    dma = pltpu.SemaphoreType.DMA
    anywhere = pl.BlockSpec(memory_space=pl.ANY)
    table = jnp.asarray(position_table())
    return pl.pallas_call(
        step_kernel,
        name="step",
        out_shape=[
            jax.ShapeDtypeStruct(tokens.shape, BF16),
            jax.ShapeDtypeStruct(cotangent.shape, F32),
            jax.ShapeDtypeStruct((FLAT, LANES), F32),
            jax.ShapeDtypeStruct((8, LANES), F32),
        ],
        in_specs=[anywhere, anywhere, VM, VM, anywhere, anywhere],
        out_specs=[VM, anywhere, VM, VM],
        scratch_shapes=[pltpu.VMEM(*k) for k in kept_shapes()]
        + [
            pltpu.VMEM(tokens.shape, BF16),
            pltpu.VMEM(table.shape, BF16),
            pltpu.VMEM(cotangent.shape, BF16),
            pltpu.VMEM((ROWS, 1), jnp.int32),
            pltpu.VMEM((ROWS, 1), jnp.int32),
            pltpu.VMEM((1, ROWS), jnp.int32),
            dma((3,)),
            pltpu.VMEM((ROWS, D), BF16),
            pltpu.VMEM((ROWS, D), F32),
            pltpu.VMEM((ROWS, D), BF16),
            pltpu.VMEM((ROWS, D), F32),
            pltpu.VMEM((6, ROWS, LANES), BF16),
            pltpu.VMEM((18, ROWS, LANES), BF16),
            pltpu.VMEM((16, D), F32),
            pltpu.VMEM((120, PIECE, D), BF16),
            pltpu.VMEM((16, D), F32),
            pltpu.VMEM((TAIL, LANES), F32),
            pltpu.VMEM((TAIL, LANES), F32),
            pltpu.VMEM((4, 12, PIECE, D), BF16),
            pltpu.VMEM((4, 2, 3, HALF, D), BF16),
            pltpu.VMEM((4, 3, HALF, D), BF16),
            pltpu.VMEM((4, 2, 3, HALF, D), BF16),
            pltpu.VMEM((4, 3, HALF, D), BF16),
            pltpu.VMEM((4, 3, PIECE, D), BF16),
            pltpu.VMEM((4, 3, PIECE, D), BF16),
            pltpu.VMEM((12, PIECE, D), BF16),
            pltpu.VMEM((6, 16, D), F32),
            pltpu.VMEM((5, 16, D), F32),
            pltpu.VMEM((8, 8, LANES), F32),
            dma,
            dma((2,)),
            dma((7,)),
            dma,
            dma((2, 4, 3)),
            dma((4, 3)),
            dma((4, 4, 3)),
            dma((4, 4, 3)),
            dma((4, 12)),
            dma((4, 12)),
            dma,
            dma((4, 12)),
            dma((4, 12)),
            dma((2, 4, 2, 3)),
            dma((2, 4, 2, 3)),
            dma((2, 4, 3)),
            dma((2, 4, 3)),
            dma((2, 4, 3, 2)),
            dma((2, 4, 3, 2)),
            dma((4, 3)),
            dma((4, 3)),
            dma((5,)),
            dma((5,)),
            dma((2,)),
            dma((8,)),
            dma((8,)),
        ],
        compiler_params=pltpu.CompilerParams(collective_id=0, has_side_effects=True, vmem_limit_bytes=LIMIT),
    )(own, tokens, keep, clip, table, cotangent)


STEP_ROWS = 1392


def update_kernel(
    flat_ref, norm_ref, param_ref, first_ref, second_ref, layer_ref, tok_ref,
    grad_out, change_out, first_out, second_out, layer_out, tok_out,
):
    layer_out[...] = layer_ref[...]
    tok_out[...] = tok_ref[...]
    s = lax.axis_index("fsdp")
    n = pl.program_id(0)
    rows = param_ref.shape[0]
    grad = flat_ref[pl.ds(n * rows + 9 * s, rows), :]
    squares = jnp.sum(jnp.sum(norm_ref[...], axis=0, keepdims=True), axis=1, keepdims=True)
    factor = jnp.minimum(1.0, 1.0 / (jnp.sqrt(squares) + 1e-06))
    clipped = grad * factor
    new_first = 0.9 * first_ref[...] + 0.1 * clipped
    new_second = 0.999 * second_ref[...] + 0.001 * clipped * clipped
    first_hat = new_first * (1.0 / first_correct)
    second_hat = new_second * (1.0 / second_correct)
    row = s * 6921 + n * rows + lax.broadcasted_iota(jnp.int32, (rows, LANES), 0)
    decay = jnp.where(row < MATS // LANES, 0.05, 0.0)
    step_rate = 0.001 * 0.75**6
    grad_out[...] = grad
    first_out[...] = new_first
    second_out[...] = new_second
    change_out[...] = step_rate * (first_hat / (jnp.sqrt(second_hat) + 1e-08) + decay * param_ref[...])


def update(flat, norm, params, first, second, layer, grad_tokens):
    rows = params.shape[0]
    steps = pl.cdiv(rows, STEP_ROWS)
    spec = pl.BlockSpec((STEP_ROWS, LANES), lambda n: (n, 0))
    token_rows = 8 * pl.cdiv(layer.shape[0], 8 * steps)
    token_spec = pl.BlockSpec((token_rows, D), lambda n: (n, 0))
    return pl.pallas_call(
        update_kernel,
        name="update",
        grid=(steps,),
        out_shape=[jax.ShapeDtypeStruct((rows, LANES), F32)] * 4
        + [jax.ShapeDtypeStruct(layer.shape, BF16), jax.ShapeDtypeStruct(grad_tokens.shape, F32)],
        in_specs=[VM, VM, spec, spec, spec, token_spec, token_spec],
        out_specs=[spec] * 4 + [token_spec] * 2,
        compiler_params=pltpu.CompilerParams(vmem_limit_bytes=LIMIT),
    )(flat, norm, params, first, second, layer, grad_tokens)


def shards(tokens, cotangent, keep_index, clip_ids, flat_params, first_moment, second_moment):
    flat = flat_params.reshape(-1, LANES)
    layer_out, grad_tokens, summed, norm = step(flat, tokens, keep_index, clip_ids, cotangent)
    outs = update(summed, norm, flat, first_moment.reshape(-1, LANES), second_moment.reshape(-1, LANES), layer_out, grad_tokens)
    grad, change, first, second = (o.reshape(-1) for o in outs[:4])
    layer_out, grad_tokens = outs[4:]
    return (layer_out, grad_tokens, grad, change, first, second)


def layer_norm(values, gain_vec, shift_vec):
    row_mean = jnp.mean(values, axis=-1, keepdims=True)
    centered = values - row_mean
    variance = jnp.mean(centered * centered, axis=-1, keepdims=True)
    return centered * lax.rsqrt(variance + 1e-06) * gain_vec + shift_vec


def gelu_exact(values):
    return jax.nn.gelu(values, approximate=False)


def positions(keep_flat):
    quarter = D // 4
    frequency = 1.0 / 10000.0 ** (jnp.arange(quarter).astype(jnp.float32) / quarter)
    row_angle = (keep_flat // GRID).astype(jnp.float32)[:, None] * frequency
    col_angle = (keep_flat % GRID).astype(jnp.float32)[:, None] * frequency
    return jnp.concatenate(
        [jnp.sin(row_angle), jnp.cos(row_angle), jnp.sin(col_angle), jnp.cos(col_angle)], axis=1
    )


def unpack_flat(flat):
    mats = 4 * D * D + 2 * D * FF
    w_qkv = flat[: 3 * D * D].reshape(D, 3 * D)
    w_out = flat[3 * D * D : 4 * D * D].reshape(D, D)
    w_up = flat[4 * D * D : 4 * D * D + D * FF].reshape(D, FF)
    w_down = flat[4 * D * D + D * FF : mats].reshape(FF, D)
    vectors = flat[mats : mats + 8 * D].reshape(8, D)
    bias_up = flat[mats + 8 * D :]
    return (w_qkv, w_out, w_up, w_down, vectors, bias_up)


def split_heads(values):
    return values.reshape(values.shape[0], HEADS, HEAD_DIM).transpose(1, 0, 2)


def join_heads(values):
    return values.transpose(1, 0, 2).reshape(values.shape[1], D)


def product(left, right):
    return jnp.dot(left, right, preferred_element_type=jnp.float32)


def plain_shards(tokens, cotangent, keep_index, clip_ids, flat_params, first_moment, second_moment):
    shard_len = flat_params.shape[0]
    mats = 4 * D * D + 2 * D * FF
    score_scale = HEAD_DIM ** (-0.5)
    sent = flat_params.astype(jnp.bfloat16)
    gathered = lax.all_gather(sent, "fsdp", axis=0, tiled=True)
    w_qkv, w_out, w_up, w_down, vectors_low, bias_up_low = unpack_flat(gathered)
    vectors = vectors_low.astype(jnp.float32)
    bias_up = bias_up_low.astype(jnp.float32)
    embedded = tokens.astype(jnp.float32) + positions(keep_index.reshape(-1))
    normed, norm_back = jax.vjp(layer_norm, embedded, vectors[0], vectors[1])
    normed_low = normed.astype(jnp.bfloat16)
    mixed_qkv = product(normed_low, w_qkv)
    query_low = (mixed_qkv[:, :D] + vectors[2]).astype(jnp.bfloat16)
    key_low = mixed_qkv[:, D : 2 * D].astype(jnp.bfloat16)
    value_low = (mixed_qkv[:, 2 * D :] + vectors[3]).astype(jnp.bfloat16)
    query_heads = split_heads(query_low)
    key_heads = split_heads(key_low)
    value_heads = split_heads(value_low)
    clip_tok = jnp.repeat(clip_ids.reshape(-1), KEEP)
    same_clip = clip_tok[:, None] == clip_tok[None, :]

    def attend(head_item):
        q_head, k_head, v_head = head_item
        scores = jnp.where(same_clip, product(q_head, k_head.T) * score_scale, -1e30)
        row_top = jnp.max(scores, axis=1, keepdims=True)
        weight_exp = jnp.exp(scores - row_top)
        row_total = jnp.sum(weight_exp, axis=1, keepdims=True)
        soft_low = (weight_exp / row_total).astype(jnp.bfloat16)
        return (product(soft_low, v_head), row_top + jnp.log(row_total))

    attended_heads, log_total = lax.map(attend, (query_heads, key_heads, value_heads))
    attended_low = join_heads(attended_heads).astype(jnp.bfloat16)
    resid = embedded + product(attended_low, w_out) + vectors[4]
    normed_two, norm_two_back = jax.vjp(layer_norm, resid, vectors[5], vectors[6])
    normed_two_low = normed_two.astype(jnp.bfloat16)
    pre_act = product(normed_two_low, w_up) + bias_up
    activated, gelu_back = jax.vjp(gelu_exact, pre_act)
    activated_low = activated.astype(jnp.bfloat16)
    layer_out = (resid + product(activated_low, w_down) + vectors[7]).astype(jnp.bfloat16)
    w_qkv, w_out, w_up, w_down, vectors_low, bias_up_low = unpack_flat(
        lax.all_gather(sent, "fsdp", axis=0, tiled=True)
    )
    grad_out = cotangent.astype(jnp.float32)
    grad_w_down = product(activated_low.T, cotangent)
    grad_bias_down = jnp.sum(grad_out, axis=0)
    grad_act = product(cotangent, w_down.T)
    grad_pre_low = gelu_back(grad_act)[0].astype(jnp.bfloat16)
    grad_w_up = product(normed_two_low.T, grad_pre_low)
    grad_bias_up = jnp.sum(grad_pre_low.astype(jnp.float32), axis=0)
    grad_normed_two = product(grad_pre_low, w_up.T)
    grad_resid_norm, grad_gain_two, grad_shift_two = norm_two_back(grad_normed_two)
    grad_resid = grad_out + grad_resid_norm
    grad_branch_low = grad_resid.astype(jnp.bfloat16)
    grad_w_out = product(attended_low.T, grad_branch_low)
    grad_bias_out = jnp.sum(grad_branch_low.astype(jnp.float32), axis=0)
    grad_attended_low = product(grad_branch_low, w_out.T).astype(jnp.bfloat16)

    def attend_back(head_item):
        q_head, k_head, v_head, g_head, lse_head = head_item
        soft = jnp.where(
            same_clip, jnp.exp(product(q_head, k_head.T) * score_scale - lse_head), 0.0
        )
        grad_soft = product(g_head, v_head.T)
        grad_value = product(soft.astype(jnp.bfloat16).T, g_head)
        inner = jnp.sum(soft * grad_soft, axis=1, keepdims=True)
        grad_raw = (score_scale * soft * (grad_soft - inner)).astype(jnp.bfloat16)
        return (product(grad_raw, k_head), product(grad_raw.T, q_head), grad_value)

    grad_query, grad_key, grad_value = lax.map(
        attend_back,
        (query_heads, key_heads, value_heads, split_heads(grad_attended_low), log_total),
    )
    grad_mixed = jnp.concatenate(
        [join_heads(grad_query), join_heads(grad_key), join_heads(grad_value)], axis=1
    ).astype(jnp.bfloat16)
    grad_w_qkv = product(normed_low.T, grad_mixed)
    mixed_sums = jnp.sum(grad_mixed.astype(jnp.float32), axis=0)
    grad_normed = product(grad_mixed, w_qkv.T)
    grad_embedded, grad_gain_one, grad_shift_one = norm_back(grad_normed)
    grad_tokens = grad_resid + grad_embedded
    full_grad = jnp.concatenate(
        [
            grad_w_qkv.reshape(-1),
            grad_w_out.reshape(-1),
            grad_w_up.reshape(-1),
            grad_w_down.reshape(-1),
            grad_gain_one,
            grad_shift_one,
            mixed_sums[:D],
            mixed_sums[2 * D :],
            grad_bias_out,
            grad_gain_two,
            grad_shift_two,
            grad_bias_down,
            grad_bias_up,
        ]
    )
    replicas = lax.axis_size("dp")
    owners = lax.axis_size("fsdp")
    reordered = full_grad.reshape(owners, replicas, -1).transpose(1, 0, 2).reshape(-1)
    own_piece = lax.psum_scatter(reordered, ("dp", "fsdp"), scatter_dimension=0, tiled=True)
    own_grad = lax.all_gather(own_piece.astype(jnp.bfloat16), "dp", axis=0, tiled=True).astype(
        own_piece.dtype
    )
    squares = lax.psum(jnp.sum(own_grad * own_grad), "fsdp")
    clip_factor = jnp.minimum(1.0, 1.0 / (jnp.sqrt(squares) + 1e-06))
    clipped = own_grad * clip_factor
    new_first = 0.9 * first_moment + 0.1 * clipped
    new_second = 0.999 * second_moment + 0.001 * clipped * clipped
    first_hat = new_first / first_correct
    second_hat = new_second / second_correct
    position = lax.axis_index("fsdp") * shard_len + jnp.arange(shard_len, dtype=jnp.int32)
    decay_mask = (position < mats).astype(jnp.float32)
    step_rate = 0.001 * 0.75**6
    param_change = step_rate * (
        first_hat / (jnp.sqrt(second_hat) + 1e-08) + 0.05 * decay_mask * flat_params
    )
    return (layer_out, grad_tokens, own_grad, param_change, new_first, new_second)


def solution(mesh):
    placed = (
        P(("dp", "fsdp"), None),
        P(("dp", "fsdp"), None),
        P(("dp", "fsdp"), None),
        P(("dp", "fsdp"), None),
        P("fsdp"),
        P("fsdp"),
        P("fsdp"),
    )
    staged = mesh.shape["dp"] == 4 and mesh.shape["fsdp"] == 8
    return jax.shard_map(
        shards if staged else plain_shards,
        mesh=mesh,
        in_specs=placed,
        out_specs=(
            P(("dp", "fsdp"), None),
            P(("dp", "fsdp"), None),
            P("fsdp"),
            P("fsdp"),
            P("fsdp"),
            P("fsdp"),
        ),
        check_vma=False,
    )
```

```python
import functools

import jax
import jax.numpy as jnp
import numpy as np
from jax import lax
from jax.experimental import pallas as pl
from jax.experimental.pallas import tpu as pltpu
from jax.sharding import PartitionSpec as P

D = 768
FF = 3072
HEADS = 12
HEAD_DIM = 64
GRID = 14
KEEP = 49
MATS = 4 * D * D + 2 * D * FF

first_correct = 0.9999734386011124
second_correct = 0.09520785288629106

F32 = jnp.float32
BF16 = jnp.bfloat16
MESH = pl.DeviceIdType.MESH
LIMIT = 66_000_000

ROWS = 400
CHUNK = 80
PIECE = 96
PIECES = 12
LANES = 128
TAIL = 72


def div(a, b):
    return a // b if isinstance(a, int) else lax.div(a, np.int32(b))


def ge(s, k):
    return div(s + 8 - k, 8)


def piece_of(s, i):
    g5, by3, by4, by8 = div(i + 4, 8), div(i, 3), div(i, 4), div(i, 8)
    forms = (
        4 * by4 + i,
        4 * by4 + 4 + i,
        24 + i + by8 * (7 * i - 56),
        33 + 5 * by3 + i,
        36 + 5 * by3 + i,
        (1 - g5) * (39 + 8 * i) + g5 * (60 + i),
        72 + i,
        84 + i,
    )
    out = forms[0]
    for k in range(1, 8):
        out = out + ge(s, k) * (forms[k] - forms[k - 1])
    return out


def grad_piece(s, i):
    return piece_of(s, i) + 24 * ge(s, 6)


def grad_block(b):
    return 8 * b + 24 * div(b + 7, 16)


ARRIVALS = (
    ((1, 0), (1, 1), (1, 2), (2, 0), (2, 1), (2, 2), (3, 0), (3, 1), (3, 2)),
    ((0, 0), (0, 1), (0, 2), (2, 0), (2, 1), (2, 2), (3, 0), (3, 1), (3, 2)),
    ((3, 0), (1, 0), (0, 0), (0, 1), (0, 2), (1, 1), (1, 2), (3, 1), (3, 2)),
    ((2, 0), (1, 0), (0, 0), (0, 1), (0, 2), (1, 1), (1, 2), (2, 1), (2, 2)),
)


def arrival(z, n):
    out = []
    for m in range(2):
        row = [ARRIVALS[plane][n][m] for plane in range(4)]
        value = row[0]
        for plane in range(1, 4):
            value = value + (row[plane] - row[plane - 1]) * div(z + 4 - plane, 4)
        out.append(value)
    return out


def dot(a, b):
    return lax.dot_general(a, b, (((1,), (0,)), ((), ())), preferred_element_type=F32)


def dot_nt(a, b):
    return lax.dot_general(a, b, (((1,), (1,)), ((), ())), preferred_element_type=F32)


def dot_tn(a, b):
    return lax.dot_general(a, b, (((0,), (0,)), ((), ())), preferred_element_type=F32)


def loop(start, stop, body):
    def step(i, carry):
        body(i)
        return carry

    lax.fori_loop(start, stop, step, 0)


def chunks(body):
    loop(0, ROWS // CHUNK, lambda n: body(pl.ds(pl.multiple_of(n * CHUNK, CHUNK), CHUNK)))


class Place:
    def __init__(self):
        self.dp = lax.axis_index("dp")
        self.s = lax.axis_index("fsdp")
        self.x, self.y = self.dp % 2, self.dp // 2
        self.z, self.c = self.s // 2, self.s % 2
        self.sib = self.at(self.dp, self.s + 1 - 2 * self.c)
        self.xn = self.at(self.dp + 1 - 2 * self.x, self.s)
        self.yn = self.at(self.dp + 2 - 4 * self.y, self.s)
        self.up = self.at(self.dp, self.s + 2)
        self.down = self.at(self.dp, self.s - 2)

    def at(self, dp, s):
        return (dp, s)

    def barrier(self):
        sem = pltpu.get_barrier_semaphore()
        for n in range(1, 8):
            pl.semaphore_signal(sem, inc=1, device_id=self.at(self.dp, (self.s + n) % 8), device_id_type=MESH)
        for peer in (self.xn, self.yn):
            pl.semaphore_signal(sem, inc=1, device_id=peer, device_id_type=MESH)
        pl.semaphore_wait(sem, 9)


def remote(src, dst, send, recv, to):
    return pltpu.make_async_remote_copy(
        src_ref=src, dst_ref=dst, send_sem=send, recv_sem=recv, device_id=to, device_id_type=MESH
    )


def weave(s, body):
    @pl.when(s <= 1)
    def _():
        loop(0, 12, lambda i: body(i, 18, (i % 4) * (96 * 18) + (i // 4) * 6))

    @pl.when(s == 2)
    def _():
        loop(0, 8, lambda i: body(i, 6, i * (96 * 6)))
        loop(8, 12, lambda i: body(i, 24, 4608 + (i - 8) * 6))

    @pl.when((s == 3) | (s == 4))
    def _():
        loop(0, 12, lambda i: body(i, 24, (i % 3) * (96 * 24) + (i // 3) * 6))

    @pl.when(s == 5)
    def _():
        loop(0, 4, lambda i: body(i, 24, i * 6))
        loop(4, 12, lambda i: body(i, 6, 2304 + (i - 4) * (96 * 6)))

    @pl.when(s >= 6)
    def _():
        loop(0, 12, lambda i: body(i, 6, i * (96 * 6)))


def position_table():
    quarter = D // 4
    exponent = np.arange(quarter, dtype=np.float32) / np.float32(quarter)
    frequency = np.float32(1.0) / np.power(np.float32(10000.0), exponent).astype(np.float32)
    angle = (np.arange(GRID, dtype=np.float32)[:, None] * frequency).astype(np.float64)
    waves = np.concatenate([np.sin(angle), np.cos(angle)], axis=1).astype(np.float32)
    table = np.zeros((32, D), np.float32)
    table[:GRID, : D // 2] = waves
    table[16 : 16 + GRID, D // 2 :] = waves
    parts = []
    for _ in range(3):
        part = table.astype(jnp.bfloat16)
        parts.append(part)
        table = table - part.astype(np.float32)
    return np.stack(parts)


def norm_stats(v):
    mean = jnp.mean(v, axis=-1, keepdims=True)
    centered = v - mean
    rstd = lax.rsqrt(jnp.mean(centered * centered, axis=-1, keepdims=True) + 1e-06)
    return centered * rstd, rstd


def block(g_ref, b):
    return g_ref[pl.ds(8 * b, 8)].reshape(D, D)


def slabs(ref, first):
    return jnp.concatenate([ref[first + j] for j in range(6)], axis=1)


def place_tokens(keep_ref, clip_ref, keep_col, clip_col, clip_row):
    token = lax.broadcasted_iota(jnp.int32, (ROWS, KEEP), 0)
    lane = lax.broadcasted_iota(jnp.int32, (ROWS, KEEP), 1)
    down = lax.broadcasted_iota(jnp.int32, (ROWS, 1), 0)
    across = lax.broadcasted_iota(jnp.int32, (1, ROWS), 1)
    patches = jnp.zeros((ROWS, KEEP), F32)
    col = jnp.full((ROWS, 1), -1, jnp.int32)
    row = jnp.full((1, ROWS), -1, jnp.int32)
    for i in range(keep_ref.shape[0]):
        first, last = KEEP * i, KEEP * i + KEEP
        patches = jnp.where(token == lane + first, keep_ref[i : i + 1, :].astype(F32), patches)
        clip = clip_ref[0:1, i : i + 1]
        col = jnp.where((down >= first) & (down < last), clip, col)
        row = jnp.where((across >= first) & (across < last), clip, row)
    keep_col[...] = jnp.sum(patches, axis=1, keepdims=True).astype(jnp.int32)
    clip_col[...] = col
    clip_row[...] = row


def embed(tok_ref, keep_ref, table_ref, emb):
    real = tok_ref.shape[0]
    emb[0:real, :] = tok_ref[...].astype(F32)
    emb[real:, :] = jnp.zeros((ROWS - real, D), F32)

    def body(at):
        keep = keep_ref[at, :]
        row = (keep * 4682) >> 16
        col = keep - GRID * row + 16
        lane = lax.broadcasted_iota(jnp.int32, (CHUNK, 32), 1)
        hot = jnp.where((lane == row) | (lane == col), 1.0, 0.0).astype(BF16)
        spot = dot(hot, table_ref[0]) + (dot(hot, table_ref[1]) + dot(hot, table_ref[2]))
        emb[at, :] = emb[at, :] + spot

    chunks(body)


def norm_one(emb, v_ref, n1):
    gain, shift = v_ref[0:1, :], v_ref[1:2, :]

    def body(at):
        n1[at, :] = (norm_stats(emb[at, :])[0] * gain + shift).astype(BF16)

    chunks(body)


def project(b, n1, g_ref, v_ref, qkv):
    mixed = dot(n1[...], block(g_ref, b)) + v_ref[pl.ds(2 + b // 2, 1), :] * jnp.where(b == 1, 0.0, 1.0)
    for j in range(6):
        qkv[6 * b + j] = mixed[:, LANES * j : LANES * (j + 1)].astype(BF16)


def attend(j, same_of, qkv, att, lse):
    query, key, value = qkv[j], qkv[6 + j], qkv[12 + j]
    first = lax.broadcasted_iota(jnp.int32, (ROWS, LANES), 1) < HEAD_DIM
    turned = value.T
    parts = []
    for h in range(2):
        own = jnp.where(first if h == 0 else ~first, query, jnp.zeros_like(query))
        scores = jnp.where(same_of(), dot_nt(key, own) * 0.125, -1e30)
        top = jnp.max(scores, axis=0, keepdims=True)
        weight = jnp.exp(scores - top)
        total = jnp.sum(weight, axis=0, keepdims=True)
        soft = (weight * (1.0 / total)).astype(BF16)
        lse[2 * j + h] = top + jnp.log(total)
        parts.append(dot(turned[HEAD_DIM * h : HEAD_DIM * (h + 1), :], soft))
    att[j] = jnp.concatenate(parts, axis=0).T.astype(BF16)


def out_project(att, g_ref, v_ref, emb, resid, n2):
    resid[...] = dot(slabs(att, 0), block(g_ref, 3))
    bias, gain, shift = v_ref[4:5, :], v_ref[5:6, :], v_ref[6:7, :]

    def body(at):
        value = emb[at, :] + resid[at, :] + bias
        resid[at, :] = value
        n2[at, :] = (norm_stats(value)[0] * gain + shift).astype(BF16)

    chunks(body)


def expand(j, n2, g_ref, v_ref, work, act, slope):
    work[...] = dot(n2[...], block(g_ref, 4 + j))

    def body(at):
        pre = work[at, :] + v_ref[pl.ds(8 + j, 1), :]
        phi = 0.5 * (1.0 + lax.erf(pre * 0.7071067811865476))
        act[j, at, :] = (pre * phi).astype(BF16)
        slope[j, at, :] = (phi + pre * (0.3989422804014327 * jnp.exp(-0.5 * pre * pre))).astype(BF16)

    chunks(body)


def contract(j, act, g_ref, work):
    add_part(j, work, dot(act[j], block(g_ref, 8 + j)))


def kept_shapes():
    return [
        ((ROWS, D), F32),
        ((ROWS, D), BF16),
        ((18, ROWS, LANES), BF16),
        ((6, ROWS, LANES), BF16),
        ((HEADS, 1, ROWS), F32),
        ((ROWS, D), F32),
        ((ROWS, D), BF16),
        ((4, ROWS, D), BF16),
        ((4, ROWS, D), BF16),
    ]


VM = pl.BlockSpec(memory_space=pltpu.VMEM)


def col_sums(dest, row, source):
    dest[row : row + 1, :] = jnp.sum(source, axis=0, keepdims=True)


def put_block(gw, b, value):
    gw[pl.ds(grad_block(b), 8)] = value.astype(BF16).reshape(8, PIECE, D)


def act_grad(j, cot, g_ref, slope, gv, work, pre_low, gn):
    work[...] = dot_nt(cot[...], block(g_ref, 8 + j))
    total = jnp.zeros((8, D), F32)

    def body(n, total):
        at = pl.ds(pl.multiple_of(n * CHUNK, CHUNK), CHUNK)
        low = (slope[j, at, :].astype(F32) * work[at, :]).astype(BF16)
        pre_low[at, :] = low
        return total + jnp.sum(low.astype(F32).reshape(CHUNK // 8, 8, D), axis=0)

    total = lax.fori_loop(0, ROWS // CHUNK, body, total)
    gv[pl.ds(8 + j, 1), :] = jnp.sum(total, axis=0, keepdims=True)
    add_part(j, gn, dot_nt(pre_low[...], block(g_ref, 4 + j)))


def add_part(j, total, part):
    @pl.when(j == 0)
    def _():
        total[...] = part

    @pl.when(j > 0)
    def _():
        total[...] += part


def norm_back(value_ref, gn, gain, extra, store, gv, row):
    def body(n, sums):
        at = pl.ds(pl.multiple_of(n * CHUNK, CHUNK), CHUNK)
        hat, rstd = norm_stats(value_ref[at, :])
        grad = gn[at, :]
        fold = lambda v: jnp.sum(v.reshape(CHUNK // 8, 8, D), axis=0)
        sums = (sums[0] + fold(grad * hat), sums[1] + fold(grad))
        grad = grad * gain
        inner = jnp.mean(grad * hat, axis=-1, keepdims=True)
        store(at, extra(at) + rstd * (grad - jnp.mean(grad, axis=-1, keepdims=True) - hat * inner))
        return sums

    zero = jnp.zeros((8, D), F32)
    one, two = lax.fori_loop(0, ROWS // CHUNK, body, (zero, zero))
    gv[row : row + 1, :] = jnp.sum(one, axis=0, keepdims=True)
    gv[row + 1 : row + 2, :] = jnp.sum(two, axis=0, keepdims=True)


def attend_back(j, same_of, qkv, lse, ga, gm):
    query, key, value, grad = qkv[j], qkv[6 + j], qkv[12 + j], ga[j]
    first = lax.broadcasted_iota(jnp.int32, (ROWS, LANES), 1) < HEAD_DIM
    turned = key.T
    parts, grad_key, grad_value = [], None, None
    for h in range(2):
        mine = first if h == 0 else ~first
        own = jnp.where(mine, query, jnp.zeros_like(query))
        own_grad = jnp.where(mine, grad, jnp.zeros_like(grad))
        soft = jnp.where(same_of(), jnp.exp(dot_nt(key, own) * 0.125 - lse[2 * j + h]), 0.0)
        grad_soft = dot_nt(value, own_grad)
        inner = jnp.sum(soft * grad_soft, axis=0, keepdims=True)
        raw = (0.125 * soft * (grad_soft - inner)).astype(BF16)
        one = dot(soft.astype(BF16), own_grad)
        two = dot(raw, own)
        grad_value = one if h == 0 else grad_value + one
        grad_key = two if h == 0 else grad_key + two
        parts.append(dot(turned[HEAD_DIM * h : HEAD_DIM * (h + 1), :], raw))
    gm[j] = jnp.concatenate(parts, axis=0).T.astype(BF16)
    gm[6 + j] = grad_key.astype(BF16)
    gm[12 + j] = grad_value.astype(BF16)


FLAT = 7240
HALF = PIECE // 2


def step_kernel(own_hbm, tok_hbm, keep_ref, clip_ref, table_hbm, cot_hbm, *refs):
    out_ref, gtok_ref, flat_ref, norm_ref = refs[:4]
    emb, n1, qkv, att, lse, resid, n2, act, slope = refs[4:13]
    (
        tok_ref, table_ref, cot_ref, keep_col, clip_col, clip_row, in_sem,
        cot, work, low_rows, gn, ga, gm, gv, g, v_ref, tail, vbuf,
        sib, xa, ya, yb, xb, zu, zd, shard, vsum, vpart, norms,
        own_sem, edge_sem, gv_send, gv_recv, gz_send, gz_recv, gp_send, gp_recv, gc_send, gc_recv, tok_sem,
        sib_send, sib_recv, h_send, h_recv, t_send, t_recv, z_send, z_recv, g_send, g_recv, v_send, v_recv, e_sem, n_send, n_recv,
    ) = refs[13:]
    me = Place()
    s, z, c, x, y = me.s, me.z, me.c, me.x, me.y
    q = me.dp
    qx, qy, qd = q + 1 - 2 * x, q + 2 - 4 * y, 3 - q
    rows = own_hbm.shape[0]
    real = cot_ref.shape[0]

    own_copy = pltpu.make_async_copy(own_hbm, flat_ref.at[pl.ds(TAIL, rows)], own_sem)
    own_copy.start()
    loads = [
        pltpu.make_async_copy(src, dst, in_sem.at[n])
        for n, (src, dst) in enumerate(((tok_hbm, tok_ref), (table_hbm, table_ref), (cot_hbm, cot_ref)))
    ]
    for load in loads:
        load.start()
    gv[...] = jnp.zeros_like(gv)
    me.barrier()
    own_copy.wait()
    tail[...] = flat_ref[rows : rows + TAIL, :]
    edge = remote(tail, flat_ref.at[pl.ds(0, TAIL)], edge_sem.at[0], edge_sem.at[1], me.at(me.dp, (s + 1) % 8))

    @pl.when(s < 7)
    def _():
        edge.start()

    @pl.when(s == 7)
    def _():
        for n in range(7):
            remote(tail, vbuf, gv_send.at[n], gv_recv, me.at(me.dp, n)).start()
        vbuf[...] = tail[...]

    place_tokens(keep_ref, clip_ref, keep_col, clip_col, clip_row)
    loads[0].wait()
    loads[1].wait()
    embed(tok_ref, keep_col, table_ref, emb)

    @pl.when(s > 0)
    def _():
        edge.wait_recv()

    def to_sib(p, i):
        piece = piece_of(2 * p + c, i)
        return remote(g.at[piece], g.at[piece], gc_send.at[p, i], gc_recv.at[p, i], me.sib)

    def line_copy(p, k, way):
        piece = piece_of(2 * p + c, q + 4 * k)
        return remote(g.at[piece], g.at[piece], gz_send.at[way, p, k], gz_recv.at[p, k], (me.up, me.down)[way])

    def plane_copy(kind, p, quarter, k):
        piece = piece_of(2 * p + c, quarter + 4 * k)
        ref = g.at[piece]
        if kind >= 2:
            ref = g.at[piece, pl.ds(HALF * (kind - 2), HALF)]
        return remote(ref, ref, gp_send.at[kind, p, k], gp_recv.at[kind, p, k], (me.xn, me.yn)[kind % 2])

    def place_piece(i, stride, first):
        piece = piece_of(s, i)
        for j in range(6):
            g[piece, :, LANES * j : LANES * (j + 1)] = flat_ref[pl.ds(TAIL - 9 * s + first + j, PIECE, stride=stride), :].astype(BF16)

    weave(s, place_piece)
    flat_ref[6912:, :] = jnp.zeros((FLAT - 6912, LANES), F32)

    def own_up(k):
        line_copy(z, k, 0).start()

    @pl.when(z < 3)
    def _():
        own_up(0)

    @pl.when(z > 0)
    def _():
        loop(0, 3, lambda k: line_copy(z, k, 1).start())

    @pl.when(z == 0)
    def _():
        loop(1, 3, own_up)

    loop(0, 12, lambda i: to_sib(z, i).start())

    @pl.when(s < 7)
    def _():
        remote(tail, vbuf, gv_send.at[0], gv_recv, me.sib).wait_recv()

    for j in range(6):
        v_ref[0:12, LANES * j : LANES * (j + 1)] = vbuf[pl.ds(j, 12, stride=6), :].astype(BF16).astype(F32)

    def line_step(n):
        p, k = arrival(z, n)

        @pl.when(p < z)
        def _():
            line_copy(p, k, 0).wait_recv()

            @pl.when(z < 3)
            def _():
                line_copy(p, k, 0).start()

        @pl.when(p > z)
        def _():
            line_copy(p, k, 1).wait_recv()

            @pl.when(z > 0)
            def _():
                line_copy(p, k, 1).start()

        plane_copy(0, p, q, k).start()
        plane_copy(1, p, q, k).start()
        to_sib(p, q + 4 * k).start()
        if n in (2, 6):

            @pl.when(z == (1 if n == 2 else 2))
            def _():
                loop(1, 3, own_up)

    def plane_step(n):
        p, k = arrival(z, n)
        plane_copy(0, p, qx, k).wait_recv()
        plane_copy(3, p, qx, k).start()
        to_sib(p, qx + 4 * k).start()
        plane_copy(1, p, qy, k).wait_recv()
        plane_copy(2, p, qy, k).start()
        to_sib(p, qy + 4 * k).start()

    def far_step(n):
        p, k = arrival(z, n)
        plane_copy(2, p, qd, k).wait_recv()
        plane_copy(3, p, qd, k).wait_recv()
        to_sib(p, qd + 4 * k).start()

    def have(p, k):
        for quarter in range(4):
            to_sib(p, quarter + 4 * k).wait_recv()

    same_of = lambda: clip_col[...] == clip_row[...]
    norm_one(emb, v_ref, n1)
    line_step(0)
    line_step(1)
    plane_step(0)
    line_step(2)
    plane_step(1)
    line_step(3)
    far_step(0)
    line_step(4)
    plane_step(2)
    far_step(1)
    line_step(5)
    plane_step(3)
    line_step(6)
    far_step(2)

    def qkv_step(b):
        @pl.when(b == 1)
        def _():
            line_step(7)
            plane_step(4)
            far_step(3)

        @pl.when(b == 2)
        def _():
            line_step(8)
            plane_step(5)
            far_step(4)

        have(0, b)
        project(b, n1, g, v_ref, qkv)

    loop(0, 3, qkv_step)

    def attend_step(j):
        @pl.when(j == 3)
        def _():
            plane_step(6)
            far_step(5)

        attend(j, same_of, qkv, att, lse)

    loop(0, 6, attend_step)
    plane_step(7)
    far_step(6)
    have(1, 0)
    have(1, 1)
    out_project(att, g, v_ref, emb, resid, n2)
    have(1, 2)

    def expand_step(j):
        @pl.when(j == 1)
        def _():
            plane_step(8)
            far_step(7)

        @pl.when(j == 2)
        def _():
            far_step(8)

        @pl.when(j < 3)
        def _():
            have(2, j)

        expand(j, n2, g, v_ref, work, act, slope)

    loop(0, 4, expand_step)
    for k in range(3):
        have(3, k)
    loop(0, 4, lambda j: contract(j, act, g, work))
    out_ref[...] = (resid[0:real, :] + work[0:real, :] + v_ref[7:8, :]).astype(BF16)

    @pl.when(s < 7)
    def _():
        edge.wait_send()

    @pl.when(s == 7)
    def _():
        for n in range(7):
            remote(tail, vbuf, gv_send.at[n], gv_recv, me.sib).wait_send()

    def line_sent(p, k):
        @pl.when((p <= z) & (z < 3))
        def _():
            line_copy(p, k, 0).wait_send()

        @pl.when((p >= z) & (z > 0))
        def _():
            line_copy(p, k, 1).wait_send()

        @pl.when(p != z)
        def _():
            plane_copy(0, p, q, k).wait_send()
            plane_copy(1, p, q, k).wait_send()
            plane_copy(2, p, qy, k).wait_send()
            plane_copy(3, p, qx, k).wait_send()

    loop(0, 12, lambda n: line_sent(n // 3, n % 3))
    loop(0, 48, lambda n: to_sib(n // 12, n % 12).wait_send())

    def add_into(piece, rows, got):
        g[piece, rows, :] = (g[piece, rows, :].astype(F32) + got.astype(F32)).astype(BF16)

    low, high, whole = pl.ds(0, HALF), pl.ds(HALF, HALF), pl.ds(0, PIECE)

    def sib_copy(p, i):
        piece = grad_piece(2 * p + 1 - c, i)
        return remote(g.at[piece], sib.at[p, i], sib_send.at[p, i], sib_recv.at[p, i], me.sib)

    def send_span(parity, p, first, count):
        @pl.when(c == 1 - parity)
        def _():
            loop(0, count, lambda r: sib_copy(p, first + r).start())

    partners = (me.sib, me.xn, me.yn, me.at(me.dp, (s + 2 - 4 * (z % 2)) % 8), me.at(me.dp, (s + 4) % 8))

    def v_step(n):
        copy = remote(vsum.at[n], vpart.at[n], v_send.at[n], v_recv.at[n], partners[n])
        return copy

    def xa_copy(p, yy, k):
        piece = grad_piece(2 * p + c, 3 * (2 * yy + 1 - x) + k)
        return remote(g.at[piece, low], xa.at[p, yy, k], h_send.at[0, p, yy, k], h_recv.at[0, p, yy, k], me.xn)

    def yb_copy(p, xx, k):
        piece = grad_piece(2 * p + c, 3 * (2 * (1 - y) + xx) + k)
        return remote(g.at[piece, high], yb.at[p, xx, k], h_send.at[1, p, xx, k], h_recv.at[1, p, xx, k], me.yn)

    def ya_copy(p, k):
        piece = grad_piece(2 * p + c, 3 * (2 * (1 - y) + x) + k)
        return remote(g.at[piece, low], ya.at[p, k], t_send.at[0, p, k], t_recv.at[0, p, k], me.yn)

    def xb_copy(p, k):
        piece = grad_piece(2 * p + c, 3 * (2 * y + 1 - x) + k)
        return remote(g.at[piece, high], xb.at[p, k], t_send.at[1, p, k], t_recv.at[1, p, k], me.xn)

    def sib_third(p, k):
        def body(n):
            i = 3 * n + k
            sib_copy(p, i).wait_recv()
            add_into(grad_piece(2 * p + c, i), whole, sib[p, i])

        loop(0, 4, body)
        for n in range(2):
            xa_copy(p, n, k).start()
            yb_copy(p, n, k).start()

    def first_third(p, k):
        xa_copy(p, 1 - y, k).wait_recv()
        add_into(grad_piece(2 * p + c, 3 * (2 * (1 - y) + x) + k), low, xa[p, 1 - y, k])
        ya_copy(p, k).start()
        yb_copy(p, 1 - x, k).wait_recv()
        add_into(grad_piece(2 * p + c, 3 * (2 * y + 1 - x) + k), high, yb[p, 1 - x, k])
        xb_copy(p, k).start()
        own = grad_piece(2 * p + c, 3 * q + k)
        xa_copy(p, y, k).wait_recv()
        add_into(own, low, xa[p, y, k])
        yb_copy(p, x, k).wait_recv()
        add_into(own, high, yb[p, x, k])

    from_sib = lambda p: loop(0, 3, lambda k: sib_third(p, k))
    first_half = lambda p: loop(0, 3, lambda k: first_third(p, k))

    def z_copy(p, k, h, way):
        piece = grad_piece(2 * p + c, 3 * q + k)
        rows = (low, high)[h]
        return remote(g.at[piece, rows], (zu, zd)[way].at[p, k, rows], z_send.at[way, p, k, h], z_recv.at[way, p, k, h], (me.up, me.down)[way])

    def second_third(p, k):
        own = grad_piece(2 * p + c, 3 * q + k)
        for h in range(2):
            (ya_copy, xb_copy)[h](p, k).wait_recv()
            add_into(own, (low, high)[h], (ya, xb)[h][p, k])

            @pl.when((z == 0) & (p > 0))
            def _():
                z_copy(p, k, h, 0).start()

            @pl.when((z == 3) & (p < 3))
            def _():
                z_copy(p, k, h, 1).start()

    def line_third(p, k):
        own = grad_piece(2 * p + c, 3 * q + k)
        for h in range(2):
            rows = (low, high)[h]

            @pl.when((z > 0) & (z < p))
            def _():
                z_copy(p, k, h, 0).wait_recv()
                add_into(own, rows, zu[p, k, rows])
                z_copy(p, k, h, 0).start()

            @pl.when((z < 3) & (z > p))
            def _():
                z_copy(p, k, h, 1).wait_recv()
                add_into(own, rows, zd[p, k, rows])
                z_copy(p, k, h, 1).start()

    second_half = lambda p: loop(0, 3, lambda k: second_third(p, k))
    along_z = lambda p: loop(0, 3, lambda k: line_third(p, k))

    def share(kind, quarter, k):
        at = 3 * quarter + k
        ref = shard.at[at] if kind < 2 else shard.at[at, (low, high)[kind - 2]]
        to = (me.xn, me.yn, me.xn, me.yn)[kind]
        return remote(ref, ref, g_send.at[kind, k], g_recv.at[kind, k], to)

    def finish(k):
        own = grad_piece(2 * z + c, 3 * q + k)

        for h in range(2):
            rows = (low, high)[h]

            @pl.when(z > 0)
            def _():
                z_copy(z, k, h, 0).wait_recv()
                add_into(own, rows, zu[z, k, rows])

            @pl.when(z < 3)
            def _():
                z_copy(z, k, h, 1).wait_recv()
                add_into(own, rows, zd[z, k, rows])

        shard[3 * q + k] = g[own]
        share(0, q, k).start()
        share(1, q, k).start()


    loads[2].wait()
    cot[...] = jnp.concatenate([cot_ref[...].astype(F32), jnp.zeros((ROWS - real, D), F32)], axis=0).astype(BF16)

    def down_step(j):
        put_block(g, 8 + j, dot_tn(act[j], cot[...]))

        def send(r):
            at = 8 * (j - 1) + r

            @pl.when(at // 12 == 1 - c)
            def _():
                sib_copy(3, at % 12).start()

        loop(0, 8, send)

    loop(1, 4, down_step)
    col_sums(gv, 7, cot[...].astype(F32))

    def act_step(j):
        @pl.when(j == 1)
        def _():
            put_block(g, 8, dot_tn(act[0], cot[...]))
            send_span(1, 2, 4, 8)
            from_sib(3)

        act_grad(j, cot, g, slope, gv, work, low_rows, gn)
        put_block(g, 4 + j, dot_tn(n2[...], low_rows[...]))
        send_span(0, 1, 8 + j, 1)
        send_span(0, 2, 3 * j, 3)
        send_span(1, 1, 3 * j, 3)
        send_span(1, 2, j, 1)

    loop(0, 4, act_step)
    first_half(3)

    def keep_resid(at, value):
        work[at, :] = value
        low_rows[at, :] = value.astype(BF16)

    norm_back(resid, gn, v_ref[5:6, :], lambda at: cot[at, :].astype(F32), keep_resid, gv, 5)
    from_sib(2)
    second_half(3)
    col_sums(gv, 4, low_rows[...].astype(F32))
    grad = dot_nt(low_rows[...], block(g, 3))
    for j in range(6):
        ga[j] = grad[:, LANES * j : LANES * (j + 1)].astype(BF16)
    put_block(g, 3, dot_tn(slabs(att, 0), low_rows[...]))
    send_span(0, 1, 0, 8)

    def attend_back_step(j):
        @pl.when(j == 2)
        def _():
            from_sib(1)
            along_z(3)

        @pl.when(j == 4)
        def _():
            first_half(2)

        attend_back(j, same_of, qkv, lse, ga, gm)

    loop(0, 6, attend_back_step)

    def qkv_back_step(b):
        mixed = slabs(gm, 6 * b)

        @pl.when(b != 1)
        def _():
            gv[pl.ds(2 + b // 2, 1), :] = jnp.sum(mixed.astype(F32), axis=0, keepdims=True)

        add_part(b, gn, dot_nt(mixed, block(g, b)))
        put_block(g, b, dot_tn(n1[...], mixed))
        send_span(0, 0, 4 * b, 4)
        send_span(1, 0, 4 * b, 4)

        @pl.when(b == 0)
        def _():
            second_half(2)
            along_z(2)

        @pl.when(b == 1)
        def _():
            first_half(1)

    loop(0, 3, qkv_back_step)

    def keep_tokens(at, value):
        work[at, :] = value

    norm_back(emb, gn, v_ref[0:1, :], lambda at: work[at, :], keep_tokens, gv, 0)
    tok_copy = pltpu.make_async_copy(work.at[pl.ds(0, real)], gtok_ref, tok_sem)
    tok_copy.start()
    vsum[0] = gv[...]

    def v_turn(n):
        v_step(n).wait_recv()
        vsum[n + 1] = vsum[n] + vpart[n]
        if n < 4:
            v_step(n + 1).start()

    v_step(0).start()
    sib_third(0, 0)
    sib_third(0, 1)
    second_half(1)
    v_turn(0)
    first_third(0, 0)
    sib_third(0, 2)
    line_third(1, 0)
    v_turn(1)
    first_third(0, 1)
    line_third(1, 1)
    second_third(0, 0)
    v_turn(2)
    first_third(0, 2)
    line_third(1, 2)
    second_third(0, 1)
    line_third(0, 0)
    second_third(0, 2)
    line_third(0, 1)
    line_third(0, 2)
    v_turn(3)
    loop(0, 3, finish)

    def pass_on(k):
        share(0, qx, k).wait_recv()
        share(3, qx, k).start()
        share(1, qy, k).wait_recv()
        share(2, qy, k).start()

    loop(0, 3, pass_on)
    v_turn(4)

    def last(k):
        share(2, qd, k).wait_recv()
        share(3, qd, k).wait_recv()

    loop(0, 3, last)

    norms[0] = jnp.zeros((8, LANES), F32)

    def lay(i, stride, first):
        total = norms[0]
        for j in range(6):
            part = shard[i, :, LANES * j : LANES * (j + 1)].astype(F32)
            flat_ref[pl.ds(first + j, PIECE, stride=stride), :] = part
            total = total + jnp.sum((part * part).reshape(PIECE // 8, 8, LANES), axis=0)
        norms[0] = total

    weave(s, lay)

    @pl.when(s == 7)
    def _():
        total = norms[0]
        for j in range(6):
            part = vsum[5, 0:12, LANES * j : LANES * (j + 1)]
            flat_ref[pl.ds(6912 + j, 12, stride=6), :] = part
            total = total + jnp.concatenate([part[0:8] * part[0:8], jnp.zeros((8, LANES), F32)], axis=0)[0:8]
            total = total + jnp.concatenate([part[8:12] * part[8:12], jnp.zeros((4, LANES), F32)], axis=0)
        norms[0] = total

    edge = remote(flat_ref.at[pl.ds(0, TAIL)], flat_ref.at[pl.ds(6912, TAIL)], e_sem.at[0], e_sem.at[1], me.at(me.dp, (s + 7) % 8))

    @pl.when(s > 0)
    def _():
        edge.start()

    def norm_copy(n):
        return remote(norms.at[0], norms.at[n], n_send.at[n], n_recv.at[n], me.at(me.dp, (s + n) % 8))

    for n in range(1, 8):
        norm_copy(n).start()

    def sent_sib(n):
        sib_copy(n // 12, n % 12).wait_send()

    loop(0, 48, sent_sib)

    def sent_plane(n):
        p, k = n // 3, n % 3
        for m in range(2):
            xa_copy(p, m, k).wait_send()
            yb_copy(p, m, k).wait_send()
        ya_copy(p, k).wait_send()
        xb_copy(p, k).wait_send()

        for h in range(2):

            @pl.when(z < p)
            def _():
                z_copy(p, k, h, 0).wait_send()

            @pl.when(z > p)
            def _():
                z_copy(p, k, h, 1).wait_send()

    loop(0, 12, sent_plane)

    def sent_share(k):
        share(0, q, k).wait_send()
        share(1, q, k).wait_send()
        share(2, qy, k).wait_send()
        share(3, qx, k).wait_send()

    loop(0, 3, sent_share)
    for n in range(5):
        v_step(n).wait_send()

    tok_copy.wait()
    total = norms[0]
    for n in range(1, 8):
        norm_copy(n).wait()
        total = total + norms[n]
    norm_ref[...] = total

    @pl.when(s > 0)
    def _():
        edge.wait_send()

    @pl.when(s < 7)
    def _():
        edge.wait_recv()


def step(own, tokens, keep, clip, cotangent):
    dma = pltpu.SemaphoreType.DMA
    anywhere = pl.BlockSpec(memory_space=pl.ANY)
    table = jnp.asarray(position_table())
    return pl.pallas_call(
        step_kernel,
        name="step",
        out_shape=[
            jax.ShapeDtypeStruct(tokens.shape, BF16),
            jax.ShapeDtypeStruct(cotangent.shape, F32),
            jax.ShapeDtypeStruct((FLAT, LANES), F32),
            jax.ShapeDtypeStruct((8, LANES), F32),
        ],
        in_specs=[anywhere, anywhere, VM, VM, anywhere, anywhere],
        out_specs=[VM, anywhere, VM, VM],
        scratch_shapes=[pltpu.VMEM(*k) for k in kept_shapes()]
        + [
            pltpu.VMEM(tokens.shape, BF16),
            pltpu.VMEM(table.shape, BF16),
            pltpu.VMEM(cotangent.shape, BF16),
            pltpu.VMEM((ROWS, 1), jnp.int32),
            pltpu.VMEM((ROWS, 1), jnp.int32),
            pltpu.VMEM((1, ROWS), jnp.int32),
            dma((3,)),
            pltpu.VMEM((ROWS, D), BF16),
            pltpu.VMEM((ROWS, D), F32),
            pltpu.VMEM((ROWS, D), BF16),
            pltpu.VMEM((ROWS, D), F32),
            pltpu.VMEM((6, ROWS, LANES), BF16),
            pltpu.VMEM((18, ROWS, LANES), BF16),
            pltpu.VMEM((16, D), F32),
            pltpu.VMEM((120, PIECE, D), BF16),
            pltpu.VMEM((16, D), F32),
            pltpu.VMEM((TAIL, LANES), F32),
            pltpu.VMEM((TAIL, LANES), F32),
            pltpu.VMEM((4, 12, PIECE, D), BF16),
            pltpu.VMEM((4, 2, 3, HALF, D), BF16),
            pltpu.VMEM((4, 3, HALF, D), BF16),
            pltpu.VMEM((4, 2, 3, HALF, D), BF16),
            pltpu.VMEM((4, 3, HALF, D), BF16),
            pltpu.VMEM((4, 3, PIECE, D), BF16),
            pltpu.VMEM((4, 3, PIECE, D), BF16),
            pltpu.VMEM((12, PIECE, D), BF16),
            pltpu.VMEM((6, 16, D), F32),
            pltpu.VMEM((5, 16, D), F32),
            pltpu.VMEM((8, 8, LANES), F32),
            dma,
            dma((2,)),
            dma((7,)),
            dma,
            dma((2, 4, 3)),
            dma((4, 3)),
            dma((4, 4, 3)),
            dma((4, 4, 3)),
            dma((4, 12)),
            dma((4, 12)),
            dma,
            dma((4, 12)),
            dma((4, 12)),
            dma((2, 4, 2, 3)),
            dma((2, 4, 2, 3)),
            dma((2, 4, 3)),
            dma((2, 4, 3)),
            dma((2, 4, 3, 2)),
            dma((2, 4, 3, 2)),
            dma((4, 3)),
            dma((4, 3)),
            dma((5,)),
            dma((5,)),
            dma((2,)),
            dma((8,)),
            dma((8,)),
        ],
        compiler_params=pltpu.CompilerParams(collective_id=0, has_side_effects=True, vmem_limit_bytes=LIMIT),
    )(own, tokens, keep, clip, table, cotangent)


STEP_ROWS = 1736


def update_kernel(
    flat_ref, norm_ref, param_ref, first_ref, second_ref, layer_ref, tok_ref,
    grad_out, change_out, first_out, second_out, layer_out, tok_out,
):
    layer_out[...] = layer_ref[...]
    tok_out[...] = tok_ref[...]
    s = lax.axis_index("fsdp")
    n = pl.program_id(0)
    rows = param_ref.shape[0]
    grad = flat_ref[pl.ds(n * rows + 9 * s, rows), :]
    squares = jnp.sum(jnp.sum(norm_ref[...], axis=0, keepdims=True), axis=1, keepdims=True)
    factor = jnp.minimum(1.0, 1.0 / (jnp.sqrt(squares) + 1e-06))
    clipped = grad * factor
    new_first = 0.9 * first_ref[...] + 0.1 * clipped
    new_second = 0.999 * second_ref[...] + 0.001 * clipped * clipped
    first_hat = new_first * (1.0 / first_correct)
    second_hat = new_second * (1.0 / second_correct)
    row = s * 6921 + n * rows + lax.broadcasted_iota(jnp.int32, (rows, LANES), 0)
    decay = jnp.where(row < MATS // LANES, 0.05, 0.0)
    step_rate = 0.001 * 0.75**6
    grad_out[...] = grad
    first_out[...] = new_first
    second_out[...] = new_second
    change_out[...] = step_rate * (first_hat / (jnp.sqrt(second_hat) + 1e-08) + decay * param_ref[...])


def update(flat, norm, params, first, second, layer, grad_tokens):
    rows = params.shape[0]
    steps = pl.cdiv(rows, STEP_ROWS)
    spec = pl.BlockSpec((STEP_ROWS, LANES), lambda n: (n, 0))
    token_rows = 8 * pl.cdiv(layer.shape[0], 8 * steps)
    token_spec = pl.BlockSpec((token_rows, D), lambda n: (n, 0))
    return pl.pallas_call(
        update_kernel,
        name="update",
        grid=(steps,),
        out_shape=[jax.ShapeDtypeStruct((rows, LANES), F32)] * 4
        + [jax.ShapeDtypeStruct(layer.shape, BF16), jax.ShapeDtypeStruct(grad_tokens.shape, F32)],
        in_specs=[VM, VM, spec, spec, spec, token_spec, token_spec],
        out_specs=[spec] * 4 + [token_spec] * 2,
        compiler_params=pltpu.CompilerParams(vmem_limit_bytes=LIMIT),
    )(flat, norm, params, first, second, layer, grad_tokens)


def shards(tokens, cotangent, keep_index, clip_ids, flat_params, first_moment, second_moment):
    flat = flat_params.reshape(-1, LANES)
    layer_out, grad_tokens, summed, norm = step(flat, tokens, keep_index, clip_ids, cotangent)
    outs = update(summed, norm, flat, first_moment.reshape(-1, LANES), second_moment.reshape(-1, LANES), layer_out, grad_tokens)
    grad, change, first, second = (o.reshape(-1) for o in outs[:4])
    layer_out, grad_tokens = outs[4:]
    return (layer_out, grad_tokens, grad, change, first, second)


def layer_norm(values, gain_vec, shift_vec):
    row_mean = jnp.mean(values, axis=-1, keepdims=True)
    centered = values - row_mean
    variance = jnp.mean(centered * centered, axis=-1, keepdims=True)
    return centered * lax.rsqrt(variance + 1e-06) * gain_vec + shift_vec


def gelu_exact(values):
    return jax.nn.gelu(values, approximate=False)


def positions(keep_flat):
    quarter = D // 4
    frequency = 1.0 / 10000.0 ** (jnp.arange(quarter).astype(jnp.float32) / quarter)
    row_angle = (keep_flat // GRID).astype(jnp.float32)[:, None] * frequency
    col_angle = (keep_flat % GRID).astype(jnp.float32)[:, None] * frequency
    return jnp.concatenate(
        [jnp.sin(row_angle), jnp.cos(row_angle), jnp.sin(col_angle), jnp.cos(col_angle)], axis=1
    )


def unpack_flat(flat):
    mats = 4 * D * D + 2 * D * FF
    w_qkv = flat[: 3 * D * D].reshape(D, 3 * D)
    w_out = flat[3 * D * D : 4 * D * D].reshape(D, D)
    w_up = flat[4 * D * D : 4 * D * D + D * FF].reshape(D, FF)
    w_down = flat[4 * D * D + D * FF : mats].reshape(FF, D)
    vectors = flat[mats : mats + 8 * D].reshape(8, D)
    bias_up = flat[mats + 8 * D :]
    return (w_qkv, w_out, w_up, w_down, vectors, bias_up)


def split_heads(values):
    return values.reshape(values.shape[0], HEADS, HEAD_DIM).transpose(1, 0, 2)


def join_heads(values):
    return values.transpose(1, 0, 2).reshape(values.shape[1], D)


def product(left, right):
    return jnp.dot(left, right, preferred_element_type=jnp.float32)


def plain_shards(tokens, cotangent, keep_index, clip_ids, flat_params, first_moment, second_moment):
    shard_len = flat_params.shape[0]
    mats = 4 * D * D + 2 * D * FF
    score_scale = HEAD_DIM ** (-0.5)
    sent = flat_params.astype(jnp.bfloat16)
    gathered = lax.all_gather(sent, "fsdp", axis=0, tiled=True)
    w_qkv, w_out, w_up, w_down, vectors_low, bias_up_low = unpack_flat(gathered)
    vectors = vectors_low.astype(jnp.float32)
    bias_up = bias_up_low.astype(jnp.float32)
    embedded = tokens.astype(jnp.float32) + positions(keep_index.reshape(-1))
    normed, norm_back = jax.vjp(layer_norm, embedded, vectors[0], vectors[1])
    normed_low = normed.astype(jnp.bfloat16)
    mixed_qkv = product(normed_low, w_qkv)
    query_low = (mixed_qkv[:, :D] + vectors[2]).astype(jnp.bfloat16)
    key_low = mixed_qkv[:, D : 2 * D].astype(jnp.bfloat16)
    value_low = (mixed_qkv[:, 2 * D :] + vectors[3]).astype(jnp.bfloat16)
    query_heads = split_heads(query_low)
    key_heads = split_heads(key_low)
    value_heads = split_heads(value_low)
    clip_tok = jnp.repeat(clip_ids.reshape(-1), KEEP)
    same_clip = clip_tok[:, None] == clip_tok[None, :]

    def attend(head_item):
        q_head, k_head, v_head = head_item
        scores = jnp.where(same_clip, product(q_head, k_head.T) * score_scale, -1e30)
        row_top = jnp.max(scores, axis=1, keepdims=True)
        weight_exp = jnp.exp(scores - row_top)
        row_total = jnp.sum(weight_exp, axis=1, keepdims=True)
        soft_low = (weight_exp / row_total).astype(jnp.bfloat16)
        return (product(soft_low, v_head), row_top + jnp.log(row_total))

    attended_heads, log_total = lax.map(attend, (query_heads, key_heads, value_heads))
    attended_low = join_heads(attended_heads).astype(jnp.bfloat16)
    resid = embedded + product(attended_low, w_out) + vectors[4]
    normed_two, norm_two_back = jax.vjp(layer_norm, resid, vectors[5], vectors[6])
    normed_two_low = normed_two.astype(jnp.bfloat16)
    pre_act = product(normed_two_low, w_up) + bias_up
    activated, gelu_back = jax.vjp(gelu_exact, pre_act)
    activated_low = activated.astype(jnp.bfloat16)
    layer_out = (resid + product(activated_low, w_down) + vectors[7]).astype(jnp.bfloat16)
    w_qkv, w_out, w_up, w_down, vectors_low, bias_up_low = unpack_flat(
        lax.all_gather(sent, "fsdp", axis=0, tiled=True)
    )
    grad_out = cotangent.astype(jnp.float32)
    grad_w_down = product(activated_low.T, cotangent)
    grad_bias_down = jnp.sum(grad_out, axis=0)
    grad_act = product(cotangent, w_down.T)
    grad_pre_low = gelu_back(grad_act)[0].astype(jnp.bfloat16)
    grad_w_up = product(normed_two_low.T, grad_pre_low)
    grad_bias_up = jnp.sum(grad_pre_low.astype(jnp.float32), axis=0)
    grad_normed_two = product(grad_pre_low, w_up.T)
    grad_resid_norm, grad_gain_two, grad_shift_two = norm_two_back(grad_normed_two)
    grad_resid = grad_out + grad_resid_norm
    grad_branch_low = grad_resid.astype(jnp.bfloat16)
    grad_w_out = product(attended_low.T, grad_branch_low)
    grad_bias_out = jnp.sum(grad_branch_low.astype(jnp.float32), axis=0)
    grad_attended_low = product(grad_branch_low, w_out.T).astype(jnp.bfloat16)

    def attend_back(head_item):
        q_head, k_head, v_head, g_head, lse_head = head_item
        soft = jnp.where(
            same_clip, jnp.exp(product(q_head, k_head.T) * score_scale - lse_head), 0.0
        )
        grad_soft = product(g_head, v_head.T)
        grad_value = product(soft.astype(jnp.bfloat16).T, g_head)
        inner = jnp.sum(soft * grad_soft, axis=1, keepdims=True)
        grad_raw = (score_scale * soft * (grad_soft - inner)).astype(jnp.bfloat16)
        return (product(grad_raw, k_head), product(grad_raw.T, q_head), grad_value)

    grad_query, grad_key, grad_value = lax.map(
        attend_back,
        (query_heads, key_heads, value_heads, split_heads(grad_attended_low), log_total),
    )
    grad_mixed = jnp.concatenate(
        [join_heads(grad_query), join_heads(grad_key), join_heads(grad_value)], axis=1
    ).astype(jnp.bfloat16)
    grad_w_qkv = product(normed_low.T, grad_mixed)
    mixed_sums = jnp.sum(grad_mixed.astype(jnp.float32), axis=0)
    grad_normed = product(grad_mixed, w_qkv.T)
    grad_embedded, grad_gain_one, grad_shift_one = norm_back(grad_normed)
    grad_tokens = grad_resid + grad_embedded
    full_grad = jnp.concatenate(
        [
            grad_w_qkv.reshape(-1),
            grad_w_out.reshape(-1),
            grad_w_up.reshape(-1),
            grad_w_down.reshape(-1),
            grad_gain_one,
            grad_shift_one,
            mixed_sums[:D],
            mixed_sums[2 * D :],
            grad_bias_out,
            grad_gain_two,
            grad_shift_two,
            grad_bias_down,
            grad_bias_up,
        ]
    )
    replicas = lax.axis_size("dp")
    owners = lax.axis_size("fsdp")
    reordered = full_grad.reshape(owners, replicas, -1).transpose(1, 0, 2).reshape(-1)
    own_piece = lax.psum_scatter(reordered, ("dp", "fsdp"), scatter_dimension=0, tiled=True)
    own_grad = lax.all_gather(own_piece.astype(jnp.bfloat16), "dp", axis=0, tiled=True).astype(
        own_piece.dtype
    )
    squares = lax.psum(jnp.sum(own_grad * own_grad), "fsdp")
    clip_factor = jnp.minimum(1.0, 1.0 / (jnp.sqrt(squares) + 1e-06))
    clipped = own_grad * clip_factor
    new_first = 0.9 * first_moment + 0.1 * clipped
    new_second = 0.999 * second_moment + 0.001 * clipped * clipped
    first_hat = new_first / first_correct
    second_hat = new_second / second_correct
    position = lax.axis_index("fsdp") * shard_len + jnp.arange(shard_len, dtype=jnp.int32)
    decay_mask = (position < mats).astype(jnp.float32)
    step_rate = 0.001 * 0.75**6
    param_change = step_rate * (
        first_hat / (jnp.sqrt(second_hat) + 1e-08) + 0.05 * decay_mask * flat_params
    )
    return (layer_out, grad_tokens, own_grad, param_change, new_first, new_second)


def solution(mesh):
    placed = (
        P(("dp", "fsdp"), None),
        P(("dp", "fsdp"), None),
        P(("dp", "fsdp"), None),
        P(("dp", "fsdp"), None),
        P("fsdp"),
        P("fsdp"),
        P("fsdp"),
    )
    staged = mesh.shape["dp"] == 4 and mesh.shape["fsdp"] == 8
    return jax.shard_map(
        shards if staged else plain_shards,
        mesh=mesh,
        in_specs=placed,
        out_specs=(
            P(("dp", "fsdp"), None),
            P(("dp", "fsdp"), None),
            P("fsdp"),
            P("fsdp"),
            P("fsdp"),
            P("fsdp"),
        ),
        check_vma=False,
    )
```
